32 devices in a mesh: grp: 2 (over y), pix: 4 (over z), ori: 2 (over x), pat: 2 (over core).
Axes of the slice: x: 2, y: 2, z: 4, core: 2. Of those that a mesh axis runs over, the one named last changes fastest.
Arguments:
- patterns: bfloat16 [2048, 65536], P(('grp', 'pat'), 'pix'), parts along dimension 0, may hold values from -40 to 40
- model: bfloat16 [131072, 2048], P(('grp', 'pix'), 'ori'), parts along dimension 0, may hold values from -6 to 6
- scale_table: float32 [32], P('grp'), parts along dimension 0, may hold values from 0.5 to 2
- scale_index: int32 [2048], P(('grp', 'pat')), parts along dimension 0, may hold values from 0 to 15
- weight_table: float32 [16], P('grp'), parts along dimension 0, may hold values from -1 to 1
- weight_class: int32 [4096], P(('grp', 'ori')), parts along dimension 0, may hold values from 0 to 7
Outputs:
- new_model: bfloat16 [131072, 2048], P(('grp', 'pix', 'pat'), 'ori'), parts along dimension 0
The draws below stay inside these ranges and needn't reach their ends.
There are 2 independent parts, one for each index of `grp`. The reference program is written for one: setup_inputs(seed, part) draws one part's arguments, and reference() takes and returns one part's arrays. A program takes and returns all parts, laid end to end along the dimension named above; each array names one. Nothing has to cross between parts.
All inputs are finite; a program needn't handle non-finite values.
Results may differ from the reference program's by a relative error of at most 0.0034.
Values may be sent and summed in bfloat16 or wider, within the bound.
No kernel may reach another device: no remote copies, remote signals or barrier semaphores. Data moves between devices by JAX's collectives and lax.ppermute only.
A program may use at most 256 MiB of HBM per device.

```python
import math
import jax
import jax.numpy as jnp
from jax import lax

P_SIZE = 65536
R = 2048
S = 16
Q = 8
N = 1024


def slice_base(key):
    return jnp.clip(jax.random.normal(jax.random.fold_in(key, 17), (P_SIZE, R), jnp.float32), -6.0, 6.0)


def draw_model(key, part):
    return slice_base(key).astype(jnp.bfloat16)


def draw_patterns(key, part):
    noise = jax.random.normal(jax.random.fold_in(key, 23), (N, P_SIZE), jnp.float32)
    base = slice_base(key)
    first = jax.random.randint(jax.random.fold_in(key, 31), (N,), 0, R)
    second = jax.random.randint(jax.random.fold_in(key, 37), (N,), 0, R)
    strength = jnp.array([1.5, 2.0, 3.0], jnp.float32)[jnp.arange(N) % 3]
    aligned = strength[:, None] * (base[:, first].T + base[:, second].T) + noise
    special = jnp.arange(N) % 16 == 0
    values = jnp.where(special[:, None], aligned, noise)
    return jnp.clip(values, -40.0, 40.0).astype(jnp.bfloat16)


def set_ends(entries, own_key, low, top_value):
    shape = entries.shape
    place = [jax.random.randint(jax.random.fold_in(own_key, axis), (), 0, shape[axis]) for axis in range(len(shape))]
    entries = entries.at[tuple(place)].set(low)
    longest = shape.index(max(shape))
    place[longest] = (place[longest] + 1) % shape[longest]
    return entries.at[tuple(place)].set(top_value)


def setup_inputs(seed: int = 0, part: int = 0) -> dict:
    key_of = jax.random.split(jax.random.key(seed), 7)
    own_keys = jax.random.split(jax.random.fold_in(key_of[6], part), 7)
    return {
        "patterns": draw_patterns(jax.random.fold_in(jax.random.fold_in(key_of[6], part), 71), part),
        "model": draw_model(jax.random.fold_in(jax.random.fold_in(key_of[6], part), 71), part),
        "scale_table": jnp.clip(jnp.exp(jax.random.uniform(own_keys[2], (S,), jnp.float32, math.log(0.5), math.log(2.0))), 0.5, 2.0),
        "scale_index": set_ends(jax.random.randint(own_keys[3], (N,), 0, S), jax.random.fold_in(own_keys[3], 1), 0, S - 1).astype(jnp.int32),
        "weight_table": jnp.clip(jax.random.uniform(own_keys[4], (Q,), jnp.float32, -1.0, 1.0), -1.0, 1.0),
        "weight_class": set_ends(jax.random.randint(own_keys[5], (R,), 0, Q), jax.random.fold_in(own_keys[5], 1), 0, Q - 1).astype(jnp.int32),
    }


prior_weight = 0.5


def reference(patterns, model, scale_table, scale_index, weight_table, weight_class):
    levels = jnp.arange(scale_table.shape[0], dtype=jnp.int32)
    phi = jnp.sum(jnp.where(scale_index[:, None] == levels[None, :], scale_table[None, :], 0.0), axis=1)
    classes = jnp.arange(weight_table.shape[0], dtype=jnp.int32)
    logw = jnp.sum(jnp.where(weight_class[:, None] == classes[None, :], weight_table[None, :], 0.0), axis=1)
    cross = jnp.dot(patterns, model, preferred_element_type=jnp.float32)
    squares = jnp.sum(jnp.square(model.astype(jnp.float32)), axis=0)
    beta = P_SIZE ** -0.5
    scores = beta * (phi[:, None] * cross - 0.5 * (phi * phi)[:, None] * squares[None, :]) + logw[None, :]
    top = jnp.max(scores, axis=1)
    lse = top + jnp.log(jnp.sum(jnp.exp(scores - top[:, None]), axis=1))
    prob = jnp.exp(scores - lse[:, None])
    weights = (prob * phi[:, None]).astype(jnp.bfloat16)
    den = prior_weight + jnp.sum(prob * (phi * phi)[:, None], axis=0)
    numer = lax.dot_general(patterns, weights, (((0,), (0,)), ((), ())), preferred_element_type=jnp.float32)
    numer = numer + prior_weight * model.astype(jnp.float32)
    return (numer / den[None, :]).astype(jnp.bfloat16)
```

```python
import functools

import jax
import jax.numpy as jnp
from jax import lax
from jax.experimental import pallas as pl
from jax.experimental.pallas import tpu as pltpu
from jax.sharding import PartitionSpec as P

prior_weight = 0.5
MIB = 1 << 20
SLOTS = 6


def table_lookup(table, index):
    levels = jnp.arange(table.shape[0], dtype=jnp.int32)
    return jnp.sum(jnp.where(index[:, None] == levels[None, :], table[None, :], 0.0), axis=1)


def params(limit):
    return pltpu.CompilerParams(vmem_limit_bytes=limit)


def cost(flops, moved):
    return pl.CostEstimate(flops=flops, bytes_accessed=moved, transcendentals=0)


def bit_reverse(value, bits):
    return sum(((value >> i) & 1) << (bits - 1 - i) for i in range(bits))


def cross_kernel(where, phi, patterns, model, send, keep, pbuf, mbuf, acc, squares, psem, msem, *, column, tk, steps, beta):
    tn = acc.shape[1]

    def copies(i):
        slot = lax.rem(i, SLOTS)
        at = pl.multiple_of(i * tk, tk)
        return (
            pltpu.make_async_copy(patterns.at[:, pl.ds(at, tk)], pbuf.at[slot], psem.at[slot]),
            pltpu.make_async_copy(model.at[pl.ds(at, tk), pl.ds(column, tn)], mbuf.at[slot], msem.at[slot]),
        )

    for i in range(min(SLOTS - 1, steps)):
        for copy in copies(i):
            copy.start()
    acc[...] = jnp.zeros_like(acc)
    squares[...] = jnp.zeros_like(squares)

    def body(i, carry):
        for copy in copies(i):
            copy.wait()

        @pl.when(i + SLOTS - 1 < steps)
        def _():
            for copy in copies(i + SLOTS - 1):
                copy.start()

        slot = lax.rem(i, SLOTS)
        tile = mbuf[slot]
        acc[...] += jnp.dot(pbuf[slot], tile, preferred_element_type=jnp.float32)
        wide = tile.astype(jnp.float32)
        squares[...] += jnp.sum((wide * wide).reshape(tk // 8, 8, tn), axis=0)
        return carry

    lax.fori_loop(0, steps, body, 0)
    sq = jnp.sum(squares[...], axis=0, keepdims=True)
    scale = phi[...]
    acc[...] = beta * (scale * acc[...] - 0.5 * (scale * scale) * sq)
    half = send.shape[0]
    send[...] = acc[pl.ds(pl.multiple_of((1 - where[0]) * half, half), half), :]
    keep[...] = acc[pl.ds(pl.multiple_of(where[0] * half, half), half), :]


def cross_chunk(where, phi, patterns, model, column, tn, beta):
    rows, depth = patterns.shape
    tk = min(1024, depth)
    half = rows // 2
    out = jax.ShapeDtypeStruct((half, tn), jnp.float32)
    anywhere = pl.BlockSpec(memory_space=pl.ANY)
    return pl.pallas_call(
        functools.partial(cross_kernel, column=column, tk=tk, steps=depth // tk, beta=beta),
        out_shape=(out, out),
        grid_spec=pltpu.PrefetchScalarGridSpec(
            num_scalar_prefetch=1,
            grid=(1,),
            in_specs=[pl.BlockSpec((rows, 1), lambda i, s: (0, 0)), anywhere, anywhere],
            out_specs=(pl.BlockSpec((half, tn), lambda i, s: (0, 0)),) * 2,
            scratch_shapes=[
                pltpu.VMEM((SLOTS, rows, tk), jnp.bfloat16),
                pltpu.VMEM((SLOTS, tk, tn), jnp.bfloat16),
                pltpu.VMEM((rows, tn), jnp.float32),
                pltpu.VMEM((8, tn), jnp.float32),
                pltpu.SemaphoreType.DMA((SLOTS,)),
                pltpu.SemaphoreType.DMA((SLOTS,)),
            ],
        ),
        compiler_params=params(24 * MIB),
        cost_estimate=cost(2 * rows * depth * tn, 2 * depth * (rows + tn)),
        name="cross",
    )(where, phi, patterns, model)


def softmax_kernel(where, table, classes, *refs, chunks, terms):
    parts, (exps, stats) = refs[:-2], refs[-2:]
    count = exps.shape[0]
    tn = exps.shape[1] // chunks
    logw = jnp.zeros(classes.shape, jnp.float32)
    for q in range(table.shape[0]):
        logw = logw + jnp.where(classes[...] == q, table[q], 0.0)
    for c in range(chunks):
        total = None
        for t in range(terms):
            rows = pl.ds(pl.multiple_of(where[t], count), count)
            part = parts[c * terms + t][rows, :]
            total = part if total is None else total + part
        exps[:, c * tn : (c + 1) * tn] = total + logw[:, c * tn : (c + 1) * tn]
    top = jnp.max(exps[...], axis=1, keepdims=True)
    exps[...] = jnp.exp(exps[...] - top)
    total = jnp.sum(exps[...], axis=1, keepdims=True)
    lanes = (count, 128)
    stats[:8, :] = jnp.transpose(jnp.broadcast_to(top, lanes))[:8, :]
    stats[8:, :] = jnp.transpose(jnp.broadcast_to(total, lanes))[:8, :]


def softmax_stage(where, table, classes, parts, count, chunks):
    terms = len(parts) // chunks
    columns = classes.shape[1]
    full = pl.BlockSpec(memory_space=pltpu.VMEM)
    scalar = pl.BlockSpec(memory_space=pltpu.SMEM)
    return pl.pallas_call(
        functools.partial(softmax_kernel, chunks=chunks, terms=terms),
        out_shape=(
            jax.ShapeDtypeStruct((count, columns), jnp.float32),
            jax.ShapeDtypeStruct((16, count), jnp.float32),
        ),
        in_specs=[scalar, scalar, full] + [full] * len(parts),
        out_specs=(full, full),
        compiler_params=params(16 * MIB),
        name="softmax",
    )(where, table, classes, *parts)


def combine(mine, other):
    top = jnp.maximum(mine[:8], other[:8])
    total = mine[8:] * jnp.exp(mine[:8] - top) + other[8:] * jnp.exp(other[:8] - top)
    return jnp.concatenate([top, total], axis=0)


def weight_kernel(where, phi, exps, own, mine, other, *outs):
    count = exps.shape[0]

    def column(row):
        return jnp.transpose(jnp.broadcast_to(row[:1, :], (128, count)))[:, :1]

    top = jnp.maximum(mine[:8, :], other[:8, :])
    total = mine[8:, :] * jnp.exp(mine[:8, :] - top) + other[8:, :] * jnp.exp(other[:8, :] - top)
    factor = column(jnp.exp(own[:8, :] - top) / total)
    factor = factor * phi[pl.ds(pl.multiple_of(where[0], count), count), :]
    tn = outs[0].shape[1]
    for c, out in enumerate(outs):
        out[...] = (exps[:, c * tn : (c + 1) * tn] * factor).astype(jnp.bfloat16)


def weight_stage(where, phi, exps, own, mine, other, chunks):
    count, columns = exps.shape
    full = pl.BlockSpec(memory_space=pltpu.VMEM)
    return pl.pallas_call(
        weight_kernel,
        out_shape=(jax.ShapeDtypeStruct((count, columns // chunks), jnp.bfloat16),) * chunks,
        in_specs=[pl.BlockSpec(memory_space=pltpu.SMEM)] + [full] * 5,
        out_specs=(full,) * chunks,
        compiler_params=params(8 * MIB),
        name="weights",
    )(where, phi, exps, own, mine, other)


def pack_kernel(where, *refs):
    parts, out = refs[:-1], refs[-1]
    count = parts[0].shape[0]
    for d, part in enumerate(parts):
        out[pl.ds(pl.multiple_of(where[d], count), count), :] = part[...]


def pack(where, parts):
    count, tn = parts[0].shape
    full = pl.BlockSpec(memory_space=pltpu.VMEM)
    return pl.pallas_call(
        pack_kernel,
        out_shape=jax.ShapeDtypeStruct((count * len(parts), tn), jnp.bfloat16),
        in_specs=[pl.BlockSpec(memory_space=pltpu.SMEM)] + [full] * len(parts),
        out_specs=full,
        compiler_params=params(8 * MIB),
        name="pack",
    )(where, *parts)


def numer_kernel(where, pown, psib, wown, wsib, fown, fsib, model, *refs, sub):
    out, scale = refs[-2:]

    @pl.when(pl.program_id(0) == 0)
    def _():
        den = jnp.sum(wown[...].astype(jnp.float32) * fown[...], axis=0, keepdims=True)
        den = den + jnp.sum(wsib[...].astype(jnp.float32) * fsib[...], axis=0, keepdims=True)
        scale[...] = 1.0 / (prior_weight + den)

    dims = (((0,), (0,)), ((), ()))
    for r in range(0, out.shape[0], sub):
        rows = slice(r, r + sub)
        acc = lax.dot_general(pown[:, rows], wown[...], dims, preferred_element_type=jnp.float32)
        acc = acc + lax.dot_general(psib[:, rows], wsib[...], dims, preferred_element_type=jnp.float32)
        acc = acc + prior_weight * model[rows, :].astype(jnp.float32)
        out[rows, :] = (acc * scale[...]).astype(jnp.bfloat16)


def numer_chunk(where, pown, psib, wown, wsib, fown, fsib, model, chunk, previous):
    depth, tn = wown.shape
    pixels, columns = model.shape[0] // 2, model.shape[1]
    tm = min(1024, pixels)
    blocks = pixels // tm
    in_specs = [
        pl.BlockSpec((depth, tm), lambda i, s: (0, s[0] * blocks + i)),
        pl.BlockSpec((depth, tm), lambda i, s: (0, s[0] * blocks + i)),
        pl.BlockSpec((depth, tn), lambda i, s: (0, 0)),
        pl.BlockSpec((depth, tn), lambda i, s: (0, 0)),
        pl.BlockSpec((depth, 1), lambda i, s: (0, 0)),
        pl.BlockSpec((depth, 1), lambda i, s: (0, 0)),
        pl.BlockSpec((tm, tn), lambda i, s: (s[0] * blocks + i, chunk)),
    ]
    args = [where, pown, psib, wown, wsib, fown, fsib, model]
    aliases = {}
    if previous is not None:
        in_specs.append(pl.BlockSpec(memory_space=pl.ANY))
        args.append(previous)
        aliases = {len(args) - 1: 0}
    return pl.pallas_call(
        functools.partial(numer_kernel, sub=min(256, tm)),
        out_shape=jax.ShapeDtypeStruct((pixels, columns), jnp.bfloat16),
        grid_spec=pltpu.PrefetchScalarGridSpec(
            num_scalar_prefetch=1,
            grid=(blocks,),
            in_specs=in_specs,
            out_specs=pl.BlockSpec((tm, tn), lambda i, s: (i, chunk)),
            scratch_shapes=[pltpu.VMEM((1, tn), jnp.float32)],
        ),
        input_output_aliases=aliases,
        compiler_params=params(24 * MIB),
        cost_estimate=cost(4 * depth * pixels * tn, 4 * pixels * (depth + tn)),
        name="numer",
    )(*args)


def exchange(value, axis, size, distance):
    return lax.ppermute(value, axis, [(i, i ^ distance) for i in range(size)])


def local(patterns, model, scale_table, scale_index, weight_table, weight_class, *, sizes):
    pix, ori = sizes["pix"], sizes["ori"]
    hops = pix.bit_length() - 1
    rows, columns = patterns.shape[0], model.shape[1]
    count = rows // pix
    tn = min(256, columns)
    chunks = columns // tn
    beta = (patterns.shape[1] * pix) ** -0.5
    place = lax.axis_index("pix")
    bits = [(place >> i) & 1 for i in range(hops)]

    phi = table_lookup(scale_table, scale_index)[:, None]
    phi_sib = exchange(phi, "pat", 2, 1)
    classes = weight_class[None, :]

    first = jnp.stack([bits[0]])
    held = []
    for c in range(chunks):
        send, keep = cross_chunk(first, phi, patterns, model, c * tn, tn, beta)
        terms = [keep, exchange(send, "pix", pix, 1)]
        offsets = [0, 0]
        size = rows // 2
        for hop in range(1, hops):
            size //= 2
            away = None
            for k, term in enumerate(terms):
                part = lax.dynamic_slice_in_dim(term, offsets[k] + (1 - bits[hop]) * size, size, 0)
                away = part if away is None else away + part
            offsets = [o + bits[hop] * size for o in offsets] + [0]
            terms.append(exchange(away, "pix", pix, 1 << hop))
        held.extend(terms)
    behind, _ = lax.optimization_barrier((patterns, held[-len(terms)]))
    psib = exchange(behind, "pat", 2, 1)

    where = jnp.stack([jnp.asarray(o, jnp.int32) for o in offsets])
    exps, own = softmax_stage(where, weight_table, classes, held, count, chunks)
    mine = own
    other = None
    for hop in range(ori.bit_length() - 1):
        if other is not None:
            mine = combine(mine, other)
        other = exchange(mine, "ori", ori, 1 << hop)
    share = bit_reverse(place, hops)
    weights = weight_stage(jnp.stack([share * count]), phi, exps, own, mine, other, chunks)

    order = jnp.stack([(share ^ bit_reverse(d, hops)) * count for d in range(pix)])
    side = jnp.stack([lax.axis_index("pat")])
    result = None
    for c in range(chunks):
        parts = [weights[c]] + [exchange(weights[c], "pix", pix, d) for d in range(1, pix)]
        wown = pack(order, parts)
        wsib = exchange(wown, "pat", 2, 1)
        result = numer_chunk(side, patterns, psib, wown, wsib, phi, phi_sib, model, c, result)
    return result


def solution(mesh):
    placed = (
        P(("grp", "pat"), "pix"),
        P(("grp", "pix"), "ori"),
        P("grp"),
        P(("grp", "pat")),
        P("grp"),
        P(("grp", "ori")),
    )
    return jax.shard_map(
        functools.partial(local, sizes=dict(mesh.shape)),
        mesh=mesh,
        in_specs=placed,
        out_specs=P(("grp", "pix", "pat"), "ori"),
        check_vma=False,
    )
```

```python
import functools

import jax
import jax.numpy as jnp
from jax import lax
from jax.experimental import pallas as pl
from jax.experimental.pallas import tpu as pltpu
from jax.sharding import PartitionSpec as P

prior_weight = 0.5
MIB = 1 << 20
SLOTS = 6
VMEM = pl.BlockSpec(memory_space=pltpu.VMEM)
SMEM = pl.BlockSpec(memory_space=pltpu.SMEM)
HBM = pl.BlockSpec(memory_space=pltpu.HBM)
ANY = pl.BlockSpec(memory_space=pl.ANY)


def table_lookup(table, index):
    levels = jnp.arange(table.shape[0], dtype=jnp.int32)
    return jnp.sum(jnp.where(index[:, None] == levels[None, :], table[None, :], 0.0), axis=1)


def params(limit):
    return pltpu.CompilerParams(vmem_limit_bytes=limit)


def cost(flops, moved):
    return pl.CostEstimate(flops=flops, bytes_accessed=moved, transcendentals=0)


def bit_reverse(value, bits):
    return sum(((value >> i) & 1) << (bits - 1 - i) for i in range(bits))


def cross_kernel(where, phi, patterns, model, after, send, keep, *refs, column, tk, steps, beta, first, turns):
    turned, refs = refs[: len(turns)], refs[len(turns) :]
    if first:
        held, mbuf, acc, squares, msem, psem = refs
    else:
        held, (mbuf, acc, squares, msem) = patterns, refs
    tn = acc.shape[1]

    def copies(i):
        slot = lax.rem(i, SLOTS)
        at = pl.multiple_of(i * tk, tk)
        both = [pltpu.make_async_copy(model.at[pl.ds(at, tk), pl.ds(column, tn)], mbuf.at[slot], msem.at[slot])]
        if first:
            both.append(pltpu.make_async_copy(patterns.at[:, pl.ds(at, tk)], held.at[:, pl.ds(at, tk)], psem.at[slot]))
        return both

    for i in range(min(SLOTS - 1, steps)):
        for copy in copies(i):
            copy.start()
    acc[...] = jnp.zeros_like(acc)
    squares[...] = jnp.zeros_like(squares)

    def body(i, carry):
        for copy in copies(i):
            copy.wait()

        @pl.when(i + SLOTS - 1 < steps)
        def _():
            for copy in copies(i + SLOTS - 1):
                copy.start()

        tile = mbuf[lax.rem(i, SLOTS)]
        part = held[:, pl.ds(pl.multiple_of(i * tk, tk), tk)]
        acc[...] += jnp.dot(part, tile, preferred_element_type=jnp.float32)
        wide = tile.astype(jnp.float32)
        squares[...] += jnp.sum((wide * wide).reshape(tk // 8, 8, tn), axis=0)
        for own, out in zip(turns, turned):
            pixels = out.shape[0]
            width = pixels // steps
            side = where[1] if own else 1 - where[1]
            piece = held[:, pl.ds(pl.multiple_of(side * pixels + i * width, width), width)]
            out[pl.ds(pl.multiple_of(i * width, width), width), :] = piece.T
        return carry

    lax.fori_loop(0, steps, body, 0)
    sq = jnp.sum(squares[...], axis=0, keepdims=True)
    scale = phi[...]
    acc[...] = beta * (scale * acc[...] - 0.5 * (scale * scale) * sq)
    half = send.shape[0]
    send[...] = acc[pl.ds(pl.multiple_of((1 - where[0]) * half, half), half), :]
    keep[...] = acc[pl.ds(pl.multiple_of(where[0] * half, half), half), :]


def cross_chunk(where, phi, patterns, model, after, column, tn, beta, first, turns):
    rows, depth = patterns.shape
    tk = min(1024, depth)
    half = rows // 2
    shapes = [jax.ShapeDtypeStruct((half, tn), jnp.float32)] * 2
    shapes += [(pltpu.VMEM if own else pltpu.HBM)((depth // 2, rows), patterns.dtype) for own in turns]
    scratch = [
        pltpu.VMEM((SLOTS, tk, tn), jnp.bfloat16),
        pltpu.VMEM((rows, tn), jnp.float32),
        pltpu.VMEM((8, tn), jnp.float32),
        pltpu.SemaphoreType.DMA((SLOTS,)),
    ]
    if first:
        shapes.append(pltpu.VMEM(patterns.shape, patterns.dtype))
        scratch.append(pltpu.SemaphoreType.DMA((SLOTS,)))
    patterns = pltpu.with_memory_space_constraint(patterns, pltpu.HBM if first else pltpu.VMEM)
    model = pltpu.with_memory_space_constraint(model, pltpu.HBM)
    return pl.pallas_call(
        functools.partial(
            cross_kernel, column=column, tk=tk, steps=depth // tk, beta=beta, first=first, turns=turns
        ),
        out_shape=shapes,
        in_specs=[SMEM, VMEM, HBM if first else VMEM, HBM, ANY],
        out_specs=[VMEM] * len(shapes),
        scratch_shapes=scratch,
        compiler_params=params(20 * MIB),
        cost_estimate=cost(2 * rows * depth * tn, 2 * depth * (rows + tn)),
        name="cross",
    )(where, phi, patterns, model, after)


def forward_kernel(where, *refs, base):
    parts, out = refs[:-1], refs[-1]
    size = out.shape[0]
    total = None
    for t, part in enumerate(parts):
        piece = part[pl.ds(pl.multiple_of(where[base + t], size), size), :]
        total = piece if total is None else total + piece
    out[...] = total


def forward(where, base, parts, size):
    return pl.pallas_call(
        functools.partial(forward_kernel, base=base),
        out_shape=jax.ShapeDtypeStruct((size, parts[0].shape[1]), jnp.float32),
        in_specs=[SMEM] + [VMEM] * len(parts),
        out_specs=VMEM,
        compiler_params=params(8 * MIB),
        name="forward",
    )(where, *parts)


def softmax_kernel(where, table, classes, after, *refs, chunks, terms, base):
    parts, (exps, stats) = refs[:-2], refs[-2:]
    count = exps.shape[0]
    tn = exps.shape[1] // chunks
    logw = jnp.zeros(classes.shape, jnp.float32)
    for q in range(table.shape[0]):
        logw = logw + jnp.where(classes[...] == q, table[q], 0.0)
    for c in range(chunks):
        total = None
        for t in range(terms):
            rows = pl.ds(pl.multiple_of(where[base + t], count), count)
            part = parts[c * terms + t][rows, :]
            total = part if total is None else total + part
        exps[:, c * tn : (c + 1) * tn] = total + logw[:, c * tn : (c + 1) * tn]
    top = jnp.max(exps[...], axis=1, keepdims=True)
    exps[...] = jnp.exp(exps[...] - top)
    total = jnp.sum(exps[...], axis=1, keepdims=True)
    lanes = (count, 128)
    stats[:8, :] = jnp.transpose(jnp.broadcast_to(top, lanes))[:8, :]
    stats[8:, :] = jnp.transpose(jnp.broadcast_to(total, lanes))[:8, :]


def softmax_stage(where, base, table, classes, after, parts, count, chunks):
    terms = len(parts) // chunks
    columns = classes.shape[1]
    return pl.pallas_call(
        functools.partial(softmax_kernel, chunks=chunks, terms=terms, base=base),
        out_shape=(
            jax.ShapeDtypeStruct((count, columns), jnp.float32),
            jax.ShapeDtypeStruct((16, count), jnp.float32),
        ),
        in_specs=[SMEM, SMEM, VMEM, ANY] + [VMEM] * len(parts),
        out_specs=(VMEM, VMEM),
        compiler_params=params(16 * MIB),
        name="softmax",
    )(where, table, classes, after, *parts)


def combine(mine, other):
    top = jnp.maximum(mine[:8], other[:8])
    total = mine[8:] * jnp.exp(mine[:8] - top) + other[8:] * jnp.exp(other[:8] - top)
    return jnp.concatenate([top, total], axis=0)


def weight_kernel(where, phi, exps, own, mine, other, *outs, base):
    count = exps.shape[0]

    def column(row):
        return jnp.transpose(jnp.broadcast_to(row[:1, :], (128, count)))[:, :1]

    top = jnp.maximum(mine[:8, :], other[:8, :])
    total = mine[8:, :] * jnp.exp(mine[:8, :] - top) + other[8:, :] * jnp.exp(other[:8, :] - top)
    factor = column(jnp.exp(own[:8, :] - top) / total)
    factor = factor * phi[pl.ds(pl.multiple_of(where[base], count), count), :]
    at = 0
    for out in outs:
        tn = out.shape[1]
        out[...] = (exps[:, at : at + tn] * factor).astype(jnp.bfloat16)
        at += tn


def weight_stage(where, base, phi, exps, own, mine, other, widths):
    count = exps.shape[0]
    return pl.pallas_call(
        functools.partial(weight_kernel, base=base),
        out_shape=[jax.ShapeDtypeStruct((count, tn), jnp.bfloat16) for tn in widths],
        in_specs=[SMEM] + [VMEM] * 5,
        out_specs=[VMEM] * len(widths),
        compiler_params=params(8 * MIB),
        name="weights",
    )(where, phi, exps, own, mine, other)


def pack_kernel(where, *refs, base):
    parts, out = refs[:-2], refs[-1]
    count = parts[0].shape[0]
    for d, part in enumerate(parts):
        out[pl.ds(pl.multiple_of(where[base + d], count), count), :] = part[...]


def pack(where, base, parts, after):
    count, tn = parts[0].shape
    after = pltpu.with_memory_space_constraint(after, pltpu.HBM)
    return pl.pallas_call(
        functools.partial(pack_kernel, base=base),
        out_shape=jax.ShapeDtypeStruct((count * len(parts), tn), jnp.bfloat16),
        in_specs=[SMEM] + [VMEM] * len(parts) + [HBM],
        out_specs=VMEM,
        compiler_params=params(8 * MIB),
        name="pack",
    )(where, *parts, after)


def numer_kernel(where, pown, psib, wown, wsib, fown, fsib, model, *refs, column, tm, sub):
    out, mbuf, obuf, msem, osem = refs[-5:]
    pixels, tn = pown.shape[0], wown.shape[1]
    steps = pixels // tm

    def fetch(i):
        slot = lax.rem(i, 3)
        at = pl.multiple_of(where[1] * pixels + i * tm, tm)
        return pltpu.make_async_copy(model.at[pl.ds(at, tm), pl.ds(column, tn)], mbuf.at[slot], msem.at[slot])

    def store(i):
        slot = lax.rem(i, 2)
        at = pl.multiple_of(i * tm, tm)
        return pltpu.make_async_copy(obuf.at[slot], out.at[pl.ds(at, tm), pl.ds(column, tn)], osem.at[slot])

    for i in range(min(2, steps)):
        fetch(i).start()
    den = jnp.sum(wown[...].astype(jnp.float32) * fown[...], axis=0, keepdims=True)
    den = den + jnp.sum(wsib[...].astype(jnp.float32) * fsib[...], axis=0, keepdims=True)
    scale = 1.0 / (prior_weight + den)

    def body(i, carry):
        fetch(i).wait()

        @pl.when(i + 2 < steps)
        def _():
            fetch(i + 2).start()

        @pl.when(i >= 2)
        def _():
            store(i - 2).wait()

        for r in range(0, tm, sub):
            rows = pl.ds(pl.multiple_of(i * tm + r, sub), sub)
            acc = jnp.dot(pown[rows, :], wown[...], preferred_element_type=jnp.float32)
            acc = acc + jnp.dot(psib[rows, :], wsib[...], preferred_element_type=jnp.float32)
            acc = acc + prior_weight * mbuf[lax.rem(i, 3), r : r + sub, :].astype(jnp.float32)
            obuf[lax.rem(i, 2), r : r + sub, :] = (acc * scale).astype(jnp.bfloat16)
        store(i).start()
        return carry

    lax.fori_loop(0, steps, body, 0)
    for i in range(max(0, steps - 2), steps):
        store(i).wait()


def numer_chunk(where, pown, psib, wown, wsib, fown, fsib, model, column, previous):
    depth, tn = wown.shape
    pixels, columns = pown.shape[0], model.shape[1]
    tm = min(1024, pixels)
    pown = pltpu.with_memory_space_constraint(pown, pltpu.VMEM)
    psib = pltpu.with_memory_space_constraint(psib, pltpu.VMEM)
    model = pltpu.with_memory_space_constraint(model, pltpu.HBM)
    args = [where, pown, psib, wown, wsib, fown, fsib, model]
    in_specs = [SMEM] + [VMEM] * 6 + [HBM]
    aliases = {}
    if previous is not None:
        in_specs.append(HBM)
        args.append(pltpu.with_memory_space_constraint(previous, pltpu.HBM))
        aliases = {len(args) - 1: 0}
    return pl.pallas_call(
        functools.partial(numer_kernel, column=column, tm=tm, sub=min(512, tm)),
        out_shape=jax.ShapeDtypeStruct((pixels, columns), jnp.bfloat16),
        in_specs=in_specs,
        out_specs=HBM,
        scratch_shapes=[
            pltpu.VMEM((3, tm, tn), jnp.bfloat16),
            pltpu.VMEM((2, tm, tn), jnp.bfloat16),
            pltpu.SemaphoreType.DMA((3,)),
            pltpu.SemaphoreType.DMA((2,)),
        ],
        input_output_aliases=aliases,
        compiler_params=params(24 * MIB),
        cost_estimate=cost(4 * depth * pixels * tn, 4 * pixels * (depth + tn)),
        name="numer",
    )(*args)


def exchange(value, axis, size, distance):
    return lax.ppermute(value, axis, [(i, i ^ distance) for i in range(size)])


def local(patterns, model, scale_table, scale_index, weight_table, weight_class, *, sizes):
    pix, ori = sizes["pix"], sizes["ori"]
    hops = pix.bit_length() - 1
    rows, columns = patterns.shape[0], model.shape[1]
    count = rows // pix
    tn = min(256, columns)
    chunks = columns // tn
    beta = (patterns.shape[1] * pix) ** -0.5
    place = lax.axis_index("pix")
    bits = [(place >> i) & 1 for i in range(hops)]

    phi = table_lookup(scale_table, scale_index)[:, None]
    classes = weight_class[None, :]
    side = lax.axis_index("pat")

    share = bit_reverse(place, hops) * count
    entries = [bits[0], side]
    starts, offsets, size = {}, [0, 0], rows // 2
    for hop in range(1, hops):
        size //= 2
        starts[hop] = len(entries)
        entries += [o + (1 - bits[hop]) * size for o in offsets]
        offsets = [o + bits[hop] * size for o in offsets] + [0]
    starts["terms"] = len(entries)
    entries += offsets
    starts["share"] = len(entries)
    entries.append(share)
    starts["order"] = len(entries)
    entries += [share ^ (bit_reverse(d, hops) * count) for d in range(pix)]
    where = jnp.stack([jnp.asarray(e, jnp.int32) for e in entries])

    later = min(2, chunks - 1)
    turned, terms = {}, {}
    source, after = patterns, phi

    def reduce_further(c):
        size = rows // 2
        for hop in range(1, hops):
            size //= 2
            away = forward(where, starts[hop], terms[c], size)
            terms[c].append(exchange(away, "pix", pix, 1 << hop))
        return away

    for c in range(chunks):
        turns = ((False,) if c == 1 else ()) + ((True,) if c == later else ())
        send, keep, *rest = cross_chunk(where, phi, source, model, after, c * tn, tn, beta, c == 0, turns)
        if c == 0:
            source = rest[-1]
        for own, value in zip(turns, rest):
            turned[own] = value
        terms[c] = [keep, exchange(send, "pix", pix, 1)]
        if c >= 1:
            after = reduce_further(c - 1)
        if c == 1:
            psib = exchange(turned[False], "pat", 2, 1)
    reduce_further(chunks - 1)
    held = [term for c in range(chunks) for term in terms[c]]
    phi_sib = exchange(phi, "pat", 2, 1)

    exps, own = softmax_stage(where, starts["terms"], weight_table, classes, psib, held, count, chunks)
    mine = own
    other = None
    for hop in range(ori.bit_length() - 1):
        if other is not None:
            mine = combine(mine, other)
        other = exchange(mine, "ori", ori, 1 << hop)
    widths = [tn] * min(2, chunks)
    if chunks > 2:
        widths.append(tn * (chunks - 2))
    weights = weight_stage(where, starts["share"], phi, exps, own, mine, other, widths)

    gathered = [[w] + [exchange(w, "pix", pix, d) for d in range(1, pix)] for w in weights]
    at, result, after = 0, None, model
    for width, parts in zip(widths, gathered):
        wown = pack(where, starts["order"], parts, after)
        wsib = exchange(wown, "pat", 2, 1)
        result = numer_chunk(where, turned[True], psib, wown, wsib, phi, phi_sib, model, at, result)
        after = result
        at += width
    return result


def solution(mesh):
    placed = (
        P(("grp", "pat"), "pix"),
        P(("grp", "pix"), "ori"),
        P("grp"),
        P(("grp", "pat")),
        P("grp"),
        P(("grp", "ori")),
    )
    return jax.shard_map(
        functools.partial(local, sizes=dict(mesh.shape)),
        mesh=mesh,
        in_specs=placed,
        out_specs=P(("grp", "pix", "pat"), "ori"),
        check_vma=False,
    )
```

```python
import functools

import jax
import jax.numpy as jnp
from jax import lax
from jax.experimental import pallas as pl
from jax.experimental.pallas import tpu as pltpu
from jax.sharding import PartitionSpec as P

prior_weight = 0.5
MIB = 1 << 20
SLOTS = 6
VMEM = pl.BlockSpec(memory_space=pltpu.VMEM)
SMEM = pl.BlockSpec(memory_space=pltpu.SMEM)
HBM = pl.BlockSpec(memory_space=pltpu.HBM)
ANY = pl.BlockSpec(memory_space=pl.ANY)


def table_lookup(table, index):
    levels = jnp.arange(table.shape[0], dtype=jnp.int32)
    return jnp.sum(jnp.where(index[:, None] == levels[None, :], table[None, :], 0.0), axis=1)


def params(limit):
    return pltpu.CompilerParams(vmem_limit_bytes=limit)


def cost(flops, moved):
    return pl.CostEstimate(flops=flops, bytes_accessed=moved, transcendentals=0)


def bit_reverse(value, bits):
    return sum(((value >> i) & 1) << (bits - 1 - i) for i in range(bits))


def cross_kernel(where, phi, patterns, model, after, send, keep, *refs, column, tk, steps, beta, first, turns):
    turned, refs = refs[: len(turns)], refs[len(turns) :]
    if first:
        held, mbuf, acc, squares, msem, psem = refs
    else:
        held, (mbuf, acc, squares, msem) = patterns, refs
    tn = acc.shape[1]

    def copies(i):
        slot = lax.rem(i, SLOTS)
        at = pl.multiple_of(i * tk, tk)
        both = [pltpu.make_async_copy(model.at[pl.ds(at, tk), pl.ds(column, tn)], mbuf.at[slot], msem.at[slot])]
        if first:
            both.append(pltpu.make_async_copy(patterns.at[:, pl.ds(at, tk)], held.at[:, pl.ds(at, tk)], psem.at[slot]))
        return both

    for i in range(min(SLOTS - 1, steps)):
        for copy in copies(i):
            copy.start()
    acc[...] = jnp.zeros_like(acc)
    squares[...] = jnp.zeros_like(squares)

    def body(i, carry):
        for copy in copies(i):
            copy.wait()

        @pl.when(i + SLOTS - 1 < steps)
        def _():
            for copy in copies(i + SLOTS - 1):
                copy.start()

        tile = mbuf[lax.rem(i, SLOTS)]
        part = held[:, pl.ds(pl.multiple_of(i * tk, tk), tk)]
        acc[...] += jnp.dot(part, tile, preferred_element_type=jnp.float32)
        wide = tile.astype(jnp.float32)
        squares[...] += jnp.sum((wide * wide).reshape(tk // 8, 8, tn), axis=0)
        for own, out in zip(turns, turned):
            pixels = out.shape[0]
            width = pixels // steps
            side = where[1] if own else 1 - where[1]
            piece = held[:, pl.ds(pl.multiple_of(side * pixels + i * width, width), width)]
            out[pl.ds(pl.multiple_of(i * width, width), width), :] = piece.T
        return carry

    lax.fori_loop(0, steps, body, 0)
    sq = jnp.sum(squares[...], axis=0, keepdims=True)
    scale = phi[...]
    acc[...] = beta * (scale * acc[...] - 0.5 * (scale * scale) * sq)
    half = send.shape[0]
    send[...] = acc[pl.ds(pl.multiple_of((1 - where[0]) * half, half), half), :]
    keep[...] = acc[pl.ds(pl.multiple_of(where[0] * half, half), half), :]


def cross_chunk(where, phi, patterns, model, after, column, tn, beta, first, turns):
    rows, depth = patterns.shape
    tk = min(1024, depth)
    half = rows // 2
    shapes = [jax.ShapeDtypeStruct((half, tn), jnp.float32)] * 2
    shapes += [(pltpu.VMEM if own else pltpu.HBM)((depth // 2, rows), patterns.dtype) for own in turns]
    scratch = [
        pltpu.VMEM((SLOTS, tk, tn), jnp.bfloat16),
        pltpu.VMEM((rows, tn), jnp.float32),
        pltpu.VMEM((8, tn), jnp.float32),
        pltpu.SemaphoreType.DMA((SLOTS,)),
    ]
    if first:
        shapes.append(pltpu.VMEM(patterns.shape, patterns.dtype))
        scratch.append(pltpu.SemaphoreType.DMA((SLOTS,)))
    patterns = pltpu.with_memory_space_constraint(patterns, pltpu.HBM if first else pltpu.VMEM)
    model = pltpu.with_memory_space_constraint(model, pltpu.HBM)
    return pl.pallas_call(
        functools.partial(
            cross_kernel, column=column, tk=tk, steps=depth // tk, beta=beta, first=first, turns=turns
        ),
        out_shape=shapes,
        in_specs=[SMEM, VMEM, HBM if first else VMEM, HBM, ANY],
        out_specs=[VMEM] * len(shapes),
        scratch_shapes=scratch,
        compiler_params=params(20 * MIB),
        cost_estimate=cost(2 * rows * depth * tn, 2 * depth * (rows + tn)),
        name="cross",
    )(where, phi, patterns, model, after)


def forward_kernel(where, *refs, base):
    parts, out = refs[:-1], refs[-1]
    size = out.shape[0]
    total = None
    for t, part in enumerate(parts):
        piece = part[pl.ds(pl.multiple_of(where[base + t], size), size), :]
        total = piece if total is None else total + piece
    out[...] = total


def forward(where, base, parts, size):
    return pl.pallas_call(
        functools.partial(forward_kernel, base=base),
        out_shape=jax.ShapeDtypeStruct((size, parts[0].shape[1]), jnp.float32),
        in_specs=[SMEM] + [VMEM] * len(parts),
        out_specs=VMEM,
        compiler_params=params(8 * MIB),
        name="forward",
    )(where, *parts)


def softmax_kernel(where, table, classes, after, *refs, chunks, terms, base):
    parts, (exps, stats) = refs[:-2], refs[-2:]
    count = exps.shape[0]
    tn = exps.shape[1] // chunks
    logw = jnp.zeros(classes.shape, jnp.float32)
    for q in range(table.shape[0]):
        logw = logw + jnp.where(classes[...] == q, table[q], 0.0)
    for c in range(chunks):
        total = None
        for t in range(terms):
            rows = pl.ds(pl.multiple_of(where[base + t], count), count)
            part = parts[c * terms + t][rows, :]
            total = part if total is None else total + part
        exps[:, c * tn : (c + 1) * tn] = total + logw[:, c * tn : (c + 1) * tn]
    top = jnp.max(exps[...], axis=1, keepdims=True)
    exps[...] = jnp.exp(exps[...] - top)
    total = jnp.sum(exps[...], axis=1, keepdims=True)
    lanes = (count, 128)
    stats[:8, :] = jnp.transpose(jnp.broadcast_to(top, lanes))[:8, :]
    stats[8:, :] = jnp.transpose(jnp.broadcast_to(total, lanes))[:8, :]


def softmax_stage(where, base, table, classes, after, parts, count, chunks):
    terms = len(parts) // chunks
    columns = classes.shape[1]
    return pl.pallas_call(
        functools.partial(softmax_kernel, chunks=chunks, terms=terms, base=base),
        out_shape=(
            jax.ShapeDtypeStruct((count, columns), jnp.float32),
            jax.ShapeDtypeStruct((16, count), jnp.float32),
        ),
        in_specs=[SMEM, SMEM, VMEM, ANY] + [VMEM] * len(parts),
        out_specs=(VMEM, VMEM),
        compiler_params=params(16 * MIB),
        name="softmax",
    )(where, table, classes, after, *parts)


def combine(mine, other):
    top = jnp.maximum(mine[:8], other[:8])
    total = mine[8:] * jnp.exp(mine[:8] - top) + other[8:] * jnp.exp(other[:8] - top)
    return jnp.concatenate([top, total], axis=0)


def weight_kernel(where, phi, exps, own, mine, other, *outs, base):
    count = exps.shape[0]

    def column(row):
        return jnp.transpose(jnp.broadcast_to(row[:1, :], (128, count)))[:, :1]

    top = jnp.maximum(mine[:8, :], other[:8, :])
    total = mine[8:, :] * jnp.exp(mine[:8, :] - top) + other[8:, :] * jnp.exp(other[:8, :] - top)
    factor = column(jnp.exp(own[:8, :] - top) / total)
    factor = factor * phi[pl.ds(pl.multiple_of(where[base], count), count), :]
    at = 0
    for out in outs:
        tn = out.shape[1]
        out[...] = (exps[:, at : at + tn] * factor).astype(jnp.bfloat16)
        at += tn


def weight_stage(where, base, phi, exps, own, mine, other, widths):
    count = exps.shape[0]
    return pl.pallas_call(
        functools.partial(weight_kernel, base=base),
        out_shape=[jax.ShapeDtypeStruct((count, tn), jnp.bfloat16) for tn in widths],
        in_specs=[SMEM] + [VMEM] * 5,
        out_specs=[VMEM] * len(widths),
        compiler_params=params(8 * MIB),
        name="weights",
    )(where, phi, exps, own, mine, other)


def pack_kernel(where, *refs, base):
    parts, out = refs[:-2], refs[-1]
    count = parts[0].shape[0]
    for d, part in enumerate(parts):
        out[pl.ds(pl.multiple_of(where[base + d], count), count), :] = part[...]


def pack(where, base, parts, after):
    count, tn = parts[0].shape
    after = pltpu.with_memory_space_constraint(after, pltpu.HBM)
    return pl.pallas_call(
        functools.partial(pack_kernel, base=base),
        out_shape=jax.ShapeDtypeStruct((count * len(parts), tn), jnp.bfloat16),
        in_specs=[SMEM] + [VMEM] * len(parts) + [HBM],
        out_specs=VMEM,
        compiler_params=params(8 * MIB),
        name="pack",
    )(where, *parts, after)


def load_kernel(source, after, out, sems):
    n = sems.shape[0]
    rows = out.shape[0] // n
    pieces = [pl.ds(i * rows, rows) for i in range(n)]
    copies = [pltpu.make_async_copy(source.at[p], out.at[p], sems.at[i]) for i, p in enumerate(pieces)]
    for copy in copies:
        copy.start()
    for copy in copies:
        copy.wait()


def load(source, after):
    return pl.pallas_call(
        load_kernel,
        out_shape=pltpu.VMEM(source.shape, source.dtype),
        in_specs=[HBM, ANY],
        out_specs=VMEM,
        scratch_shapes=[pltpu.SemaphoreType.DMA((4,))],
        compiler_params=params(8 * MIB),
        name="load",
    )(pltpu.with_memory_space_constraint(source, pltpu.HBM), after)


def numer_kernel(where, pown, psib, wown, wsib, fown, fsib, model, *refs, column, tm, sub):
    out, mbuf, obuf, msem, osem = refs[-5:]
    pixels, tn = pown.shape[0], wown.shape[1]
    steps = pixels // tm

    def fetch(i):
        slot = lax.rem(i, 3)
        at = pl.multiple_of(where[1] * pixels + i * tm, tm)
        return pltpu.make_async_copy(model.at[pl.ds(at, tm), pl.ds(column, tn)], mbuf.at[slot], msem.at[slot])

    def store(i):
        slot = lax.rem(i, 2)
        at = pl.multiple_of(i * tm, tm)
        return pltpu.make_async_copy(obuf.at[slot], out.at[pl.ds(at, tm), pl.ds(column, tn)], osem.at[slot])

    for i in range(min(2, steps)):
        fetch(i).start()
    den = jnp.sum(wown[...].astype(jnp.float32) * fown[...], axis=0, keepdims=True)
    den = den + jnp.sum(wsib[...].astype(jnp.float32) * fsib[...], axis=0, keepdims=True)
    scale = 1.0 / (prior_weight + den)

    def body(i, carry):
        fetch(i).wait()

        @pl.when(i + 2 < steps)
        def _():
            fetch(i + 2).start()

        @pl.when(i >= 2)
        def _():
            store(i - 2).wait()

        for r in range(0, tm, sub):
            rows = pl.ds(pl.multiple_of(i * tm + r, sub), sub)
            acc = jnp.dot(pown[rows, :], wown[...], preferred_element_type=jnp.float32)
            acc = acc + jnp.dot(psib[rows, :], wsib[...], preferred_element_type=jnp.float32)
            acc = acc + prior_weight * mbuf[lax.rem(i, 3), r : r + sub, :].astype(jnp.float32)
            obuf[lax.rem(i, 2), r : r + sub, :] = (acc * scale).astype(jnp.bfloat16)
        store(i).start()
        return carry

    lax.fori_loop(0, steps, body, 0)
    for i in range(max(0, steps - 2), steps):
        store(i).wait()


def numer_chunk(where, pown, psib, wown, wsib, fown, fsib, model, column, previous):
    depth, tn = wown.shape
    pixels, columns = pown.shape[0], model.shape[1]
    tm = min(1024, pixels)
    pown = pltpu.with_memory_space_constraint(pown, pltpu.VMEM)
    psib = pltpu.with_memory_space_constraint(psib, pltpu.VMEM)
    model = pltpu.with_memory_space_constraint(model, pltpu.HBM)
    args = [where, pown, psib, wown, wsib, fown, fsib, model]
    in_specs = [SMEM] + [VMEM] * 6 + [HBM]
    aliases = {}
    if previous is not None:
        in_specs.append(HBM)
        args.append(pltpu.with_memory_space_constraint(previous, pltpu.HBM))
        aliases = {len(args) - 1: 0}
    return pl.pallas_call(
        functools.partial(numer_kernel, column=column, tm=tm, sub=min(256, tm)),
        out_shape=jax.ShapeDtypeStruct((pixels, columns), jnp.bfloat16),
        in_specs=in_specs,
        out_specs=HBM,
        scratch_shapes=[
            pltpu.VMEM((3, tm, tn), jnp.bfloat16),
            pltpu.VMEM((2, tm, tn), jnp.bfloat16),
            pltpu.SemaphoreType.DMA((3,)),
            pltpu.SemaphoreType.DMA((2,)),
        ],
        input_output_aliases=aliases,
        compiler_params=params(24 * MIB),
        cost_estimate=cost(4 * depth * pixels * tn, 4 * pixels * (depth + tn)),
        name="numer",
    )(*args)


def exchange(value, axis, size, distance):
    return lax.ppermute(value, axis, [(i, i ^ distance) for i in range(size)])


def iteration(patterns, model, scale_table, scale_index, weight_table, weight_class, *, sizes):
    pix, ori = sizes["pix"], sizes["ori"]
    hops = pix.bit_length() - 1
    rows, columns = patterns.shape[0], model.shape[1]
    count = rows // pix
    tn = min(256, columns)
    chunks = columns // tn
    beta = (patterns.shape[1] * pix) ** -0.5
    place = lax.axis_index("pix")
    bits = [(place >> i) & 1 for i in range(hops)]

    phi = table_lookup(scale_table, scale_index)[:, None]
    classes = weight_class[None, :]
    side = lax.axis_index("pat")

    share = bit_reverse(place, hops) * count
    entries = [bits[0], side]
    starts, offsets, size = {}, [0, 0], rows // 2
    for hop in range(1, hops):
        size //= 2
        starts[hop] = len(entries)
        entries += [o + (1 - bits[hop]) * size for o in offsets]
        offsets = [o + bits[hop] * size for o in offsets] + [0]
    starts["terms"] = len(entries)
    entries += offsets
    starts["share"] = len(entries)
    entries.append(share)
    starts["order"] = len(entries)
    entries += [share ^ (bit_reverse(d, hops) * count) for d in range(pix)]
    where = jnp.stack([jnp.asarray(e, jnp.int32) for e in entries])

    later = min(2, chunks - 1)
    turned, terms = {}, {}
    source, after = patterns, phi

    def reduce_further(c):
        size = rows // 2
        for hop in range(1, hops):
            size //= 2
            away = forward(where, starts[hop], terms[c], size)
            terms[c].append(exchange(away, "pix", pix, 1 << hop))
        return away

    for c in range(chunks):
        turns = ((False,) if c == 1 else ()) + ((True,) if c == later else ())
        send, keep, *rest = cross_chunk(where, phi, source, model, after, c * tn, tn, beta, c == 0, turns)
        if c == 0:
            source = rest[-1]
        for own, value in zip(turns, rest):
            turned[own] = value
        terms[c] = [keep, exchange(send, "pix", pix, 1)]
        if c >= 1:
            after = reduce_further(c - 1)
        if c == 1:
            psib = exchange(turned[False], "pat", 2, 1)
    last = reduce_further(chunks - 1)
    psib = load(psib, last)
    held = [term for c in range(chunks) for term in terms[c]]
    phi_sib = exchange(phi, "pat", 2, 1)

    exps, own = softmax_stage(where, starts["terms"], weight_table, classes, psib, held, count, chunks)
    mine = own
    other = None
    for hop in range(ori.bit_length() - 1):
        if other is not None:
            mine = combine(mine, other)
        other = exchange(mine, "ori", ori, 1 << hop)
    widths = [tn] * min(2, chunks)
    if chunks > 2:
        widths.append(tn * (chunks - 2))
    weights = weight_stage(where, starts["share"], phi, exps, own, mine, other, widths)

    gathered = [[w] + [exchange(w, "pix", pix, d) for d in range(1, pix)] for w in weights]
    at, result, after = 0, None, model
    for width, parts in zip(widths, gathered):
        wown = pack(where, starts["order"], parts, after)
        wsib = exchange(wown, "pat", 2, 1)
        result = numer_chunk(where, turned[True], psib, wown, wsib, phi, phi_sib, model, at, result)
        after = result
        at += width
    return result


def solution(mesh):
    placed = (
        P(("grp", "pat"), "pix"),
        P(("grp", "pix"), "ori"),
        P("grp"),
        P(("grp", "pat")),
        P("grp"),
        P(("grp", "ori")),
    )
    return jax.shard_map(
        functools.partial(iteration, sizes=dict(mesh.shape)),
        mesh=mesh,
        in_specs=placed,
        out_specs=P(("grp", "pix", "pat"), "ori"),
        check_vma=False,
    )
```

```python
import functools

import jax
import jax.numpy as jnp
from jax import lax
from jax.experimental import pallas as pl
from jax.experimental.pallas import tpu as pltpu
from jax.sharding import PartitionSpec as P

prior_weight = 0.5
MIB = 1 << 20
SLOTS = 4
VMEM = pl.BlockSpec(memory_space=pltpu.VMEM)
SMEM = pl.BlockSpec(memory_space=pltpu.SMEM)
HBM = pl.BlockSpec(memory_space=pltpu.HBM)
ANY = pl.BlockSpec(memory_space=pl.ANY)


def table_lookup(table, index):
    levels = jnp.arange(table.shape[0], dtype=jnp.int32)
    return jnp.sum(jnp.where(index[:, None] == levels[None, :], table[None, :], 0.0), axis=1)


def params(limit):
    return pltpu.CompilerParams(vmem_limit_bytes=limit)


def cost(flops, moved):
    return pl.CostEstimate(flops=flops, bytes_accessed=moved, transcendentals=0)


def bit_reverse(value, bits):
    return sum(((value >> i) & 1) << (bits - 1 - i) for i in range(bits))


def cross_kernel(where, phi, patterns, model, after, send, keep, *refs, column, tk, steps, beta, first, turns):
    turned, refs = refs[: len(turns)], refs[len(turns) :]
    if first:
        held, mbuf, acc, squares, msem, psem = refs
    else:
        held, (mbuf, acc, squares, msem) = patterns, refs
    tn = acc.shape[1]

    def copies(i):
        slot = lax.rem(i, SLOTS)
        at = pl.multiple_of(i * tk, tk)
        both = [pltpu.make_async_copy(model.at[pl.ds(at, tk), pl.ds(column, tn)], mbuf.at[slot], msem.at[slot])]
        if first:
            both.append(pltpu.make_async_copy(patterns.at[:, pl.ds(at, tk)], held.at[:, pl.ds(at, tk)], psem.at[slot]))
        return both

    for i in range(min(SLOTS - 1, steps)):
        for copy in copies(i):
            copy.start()
    acc[...] = jnp.zeros_like(acc)
    squares[...] = jnp.zeros_like(squares)

    def body(i, carry):
        for copy in copies(i):
            copy.wait()

        @pl.when(i + SLOTS - 1 < steps)
        def _():
            for copy in copies(i + SLOTS - 1):
                copy.start()

        tile = mbuf[lax.rem(i, SLOTS)]
        part = held[:, pl.ds(pl.multiple_of(i * tk, tk), tk)]
        acc[...] += jnp.dot(part, tile, preferred_element_type=jnp.float32)
        wide = tile.astype(jnp.float32)
        squares[...] += jnp.sum((wide * wide).reshape(tk // 8, 8, tn), axis=0)
        for own, out in zip(turns, turned):
            pixels = out.shape[0]
            width = pixels // steps
            side = where[1] if own else 1 - where[1]
            piece = held[:, pl.ds(pl.multiple_of(side * pixels + i * width, width), width)]
            out[pl.ds(pl.multiple_of(i * width, width), width), :] = piece.T
        return carry

    lax.fori_loop(0, steps, body, 0)
    sq = jnp.sum(squares[...], axis=0, keepdims=True)
    scale = phi[...]
    acc[...] = beta * (scale * acc[...] - 0.5 * (scale * scale) * sq)
    half = send.shape[0]
    send[...] = acc[pl.ds(pl.multiple_of((1 - where[0]) * half, half), half), :]
    keep[...] = acc[pl.ds(pl.multiple_of(where[0] * half, half), half), :]


def cross_chunk(where, phi, patterns, model, after, column, tn, beta, first, turns):
    rows, depth = patterns.shape
    tk = min(2048, depth)
    half = rows // 2
    shapes = [jax.ShapeDtypeStruct((half, tn), jnp.float32)] * 2
    shapes += [(pltpu.VMEM if own else pltpu.HBM)((depth // 2, rows), patterns.dtype) for own in turns]
    scratch = [
        pltpu.VMEM((SLOTS, tk, tn), jnp.bfloat16),
        pltpu.VMEM((rows, tn), jnp.float32),
        pltpu.VMEM((8, tn), jnp.float32),
        pltpu.SemaphoreType.DMA((SLOTS,)),
    ]
    if first:
        shapes.append(pltpu.VMEM(patterns.shape, patterns.dtype))
        scratch.append(pltpu.SemaphoreType.DMA((SLOTS,)))
    patterns = pltpu.with_memory_space_constraint(patterns, pltpu.HBM if first else pltpu.VMEM)
    model = pltpu.with_memory_space_constraint(model, pltpu.HBM)
    return pl.pallas_call(
        functools.partial(
            cross_kernel, column=column, tk=tk, steps=depth // tk, beta=beta, first=first, turns=turns
        ),
        out_shape=shapes,
        in_specs=[SMEM, VMEM, HBM if first else VMEM, HBM, ANY],
        out_specs=[VMEM] * len(shapes),
        scratch_shapes=scratch,
        compiler_params=params(20 * MIB),
        cost_estimate=cost(2 * rows * depth * tn, 2 * depth * (rows + tn)),
        name="cross",
    )(where, phi, patterns, model, after)


def forward_kernel(where, after, *refs, base):
    parts, out = refs[:-1], refs[-1]
    size = out.shape[0]
    total = None
    for t, part in enumerate(parts):
        piece = part[pl.ds(pl.multiple_of(where[base + t], size), size), :]
        total = piece if total is None else total + piece
    out[...] = total


def forward(where, base, parts, size, after):
    return pl.pallas_call(
        functools.partial(forward_kernel, base=base),
        out_shape=jax.ShapeDtypeStruct((size, parts[0].shape[1]), jnp.float32),
        in_specs=[SMEM, ANY] + [VMEM] * len(parts),
        out_specs=VMEM,
        compiler_params=params(8 * MIB),
        name="forward",
    )(where, after, *parts)


def softmax_kernel(where, table, classes, after, *refs, chunks, terms, base):
    parts, (exps, stats) = refs[:-2], refs[-2:]
    count = exps.shape[0]
    logw = jnp.zeros(classes.shape, jnp.float32)
    for q in range(table.shape[0]):
        logw = logw + jnp.where(classes[...] == q, table[q], 0.0)
    at = 0
    for c in range(chunks):
        tn = parts[c * terms].shape[1]
        total = None
        for t in range(terms):
            rows = pl.ds(pl.multiple_of(where[base + t], count), count)
            part = parts[c * terms + t][rows, :]
            total = part if total is None else total + part
        exps[:, at : at + tn] = total + logw[:, at : at + tn]
        at += tn
    top = jnp.max(exps[...], axis=1, keepdims=True)
    exps[...] = jnp.exp(exps[...] - top)
    total = jnp.sum(exps[...], axis=1, keepdims=True)
    lanes = (count, 128)
    stats[:8, :] = jnp.transpose(jnp.broadcast_to(top, lanes))[:8, :]
    stats[8:, :] = jnp.transpose(jnp.broadcast_to(total, lanes))[:8, :]


def softmax_stage(where, base, table, classes, after, parts, count, chunks):
    terms = len(parts) // chunks
    columns = classes.shape[1]
    return pl.pallas_call(
        functools.partial(softmax_kernel, chunks=chunks, terms=terms, base=base),
        out_shape=(
            jax.ShapeDtypeStruct((count, columns), jnp.float32),
            jax.ShapeDtypeStruct((16, count), jnp.float32),
        ),
        in_specs=[SMEM, SMEM, VMEM, ANY] + [VMEM] * len(parts),
        out_specs=(VMEM, VMEM),
        compiler_params=params(16 * MIB),
        name="softmax",
    )(where, table, classes, after, *parts)


def combine(mine, other):
    top = jnp.maximum(mine[:8], other[:8])
    total = mine[8:] * jnp.exp(mine[:8] - top) + other[8:] * jnp.exp(other[:8] - top)
    return jnp.concatenate([top, total], axis=0)


def weight_kernel(where, phi, exps, own, mine, other, *outs, base):
    count = exps.shape[0]

    def column(row):
        return jnp.transpose(jnp.broadcast_to(row[:1, :], (128, count)))[:, :1]

    top = jnp.maximum(mine[:8, :], other[:8, :])
    total = mine[8:, :] * jnp.exp(mine[:8, :] - top) + other[8:, :] * jnp.exp(other[:8, :] - top)
    factor = column(jnp.exp(own[:8, :] - top) / total)
    factor = factor * phi[pl.ds(pl.multiple_of(where[base], count), count), :]
    at = 0
    for out in outs:
        tn = out.shape[1]
        out[...] = (exps[:, at : at + tn] * factor).astype(jnp.bfloat16)
        at += tn


def weight_stage(where, base, phi, exps, own, mine, other, widths):
    count = exps.shape[0]
    return pl.pallas_call(
        functools.partial(weight_kernel, base=base),
        out_shape=[jax.ShapeDtypeStruct((count, tn), jnp.bfloat16) for tn in widths],
        in_specs=[SMEM] + [VMEM] * 5,
        out_specs=[VMEM] * len(widths),
        compiler_params=params(8 * MIB),
        name="weights",
    )(where, phi, exps, own, mine, other)


def pack_kernel(where, *refs, base):
    parts, out = refs[:-2], refs[-1]
    count = parts[0].shape[0]
    for d, part in enumerate(parts):
        out[pl.ds(pl.multiple_of(where[base + d], count), count), :] = part[...]


def pack(where, base, parts, after):
    count, tn = parts[0].shape
    after = pltpu.with_memory_space_constraint(after, pltpu.HBM)
    return pl.pallas_call(
        functools.partial(pack_kernel, base=base),
        out_shape=jax.ShapeDtypeStruct((count * len(parts), tn), jnp.bfloat16),
        in_specs=[SMEM] + [VMEM] * len(parts) + [HBM],
        out_specs=VMEM,
        compiler_params=params(8 * MIB),
        name="pack",
    )(where, *parts, after)


def load_kernel(source, after, out, sems):
    n = sems.shape[0]
    rows = out.shape[0] // n
    pieces = [pl.ds(i * rows, rows) for i in range(n)]
    copies = [pltpu.make_async_copy(source.at[p], out.at[p], sems.at[i]) for i, p in enumerate(pieces)]
    for copy in copies:
        copy.start()
    for copy in copies:
        copy.wait()


def load(source, after):
    return pl.pallas_call(
        load_kernel,
        out_shape=pltpu.VMEM(source.shape, source.dtype),
        in_specs=[HBM, ANY],
        out_specs=VMEM,
        scratch_shapes=[pltpu.SemaphoreType.DMA((4,))],
        compiler_params=params(8 * MIB),
        name="load",
    )(pltpu.with_memory_space_constraint(source, pltpu.HBM), after)


def numer_kernel(where, pown, psib, wown, wsib, fown, fsib, model, *refs, column, tm, sub):
    out, mbuf, obuf, msem, osem = refs[-5:]
    pixels, tn = pown.shape[0], wown.shape[1]
    steps = pixels // tm

    def fetch(i):
        slot = lax.rem(i, 3)
        at = pl.multiple_of(where[1] * pixels + i * tm, tm)
        return pltpu.make_async_copy(model.at[pl.ds(at, tm), pl.ds(column, tn)], mbuf.at[slot], msem.at[slot])

    def store(i):
        slot = lax.rem(i, 2)
        at = pl.multiple_of(i * tm, tm)
        return pltpu.make_async_copy(obuf.at[slot], out.at[pl.ds(at, tm), pl.ds(column, tn)], osem.at[slot])

    for i in range(min(2, steps)):
        fetch(i).start()
    den = jnp.sum(wown[...].astype(jnp.float32) * fown[...], axis=0, keepdims=True)
    den = den + jnp.sum(wsib[...].astype(jnp.float32) * fsib[...], axis=0, keepdims=True)
    scale = 1.0 / (prior_weight + den)

    def body(i, carry):
        @pl.when(i + 2 < steps)
        def _():
            fetch(i + 2).start()

        for r in range(0, tm, sub):
            rows = pl.ds(pl.multiple_of(i * tm + r, sub), sub)
            acc = jnp.dot(pown[rows, :], wown[...], preferred_element_type=jnp.float32)
            acc = acc + jnp.dot(psib[rows, :], wsib[...], preferred_element_type=jnp.float32)
            if r == 0:
                fetch(i).wait()

                @pl.when(i >= 2)
                def _():
                    store(i - 2).wait()

            acc = acc + prior_weight * mbuf[lax.rem(i, 3), r : r + sub, :].astype(jnp.float32)
            obuf[lax.rem(i, 2), r : r + sub, :] = (acc * scale).astype(jnp.bfloat16)
        store(i).start()
        return carry

    lax.fori_loop(0, steps, body, 0)
    for i in range(max(0, steps - 2), steps):
        store(i).wait()


def numer_chunk(where, pown, psib, wown, wsib, fown, fsib, model, column, previous):
    depth, tn = wown.shape
    pixels, columns = pown.shape[0], model.shape[1]
    tm = min(1024, pixels)
    pown = pltpu.with_memory_space_constraint(pown, pltpu.VMEM)
    psib = pltpu.with_memory_space_constraint(psib, pltpu.VMEM)
    model = pltpu.with_memory_space_constraint(model, pltpu.HBM)
    args = [where, pown, psib, wown, wsib, fown, fsib, model]
    in_specs = [SMEM] + [VMEM] * 6 + [HBM]
    aliases = {}
    if previous is not None:
        in_specs.append(HBM)
        args.append(pltpu.with_memory_space_constraint(previous, pltpu.HBM))
        aliases = {len(args) - 1: 0}
    return pl.pallas_call(
        functools.partial(numer_kernel, column=column, tm=tm, sub=min(256, tm)),
        out_shape=jax.ShapeDtypeStruct((pixels, columns), jnp.bfloat16),
        in_specs=in_specs,
        out_specs=HBM,
        scratch_shapes=[
            pltpu.VMEM((3, tm, tn), jnp.bfloat16),
            pltpu.VMEM((2, tm, tn), jnp.bfloat16),
            pltpu.SemaphoreType.DMA((3,)),
            pltpu.SemaphoreType.DMA((2,)),
        ],
        input_output_aliases=aliases,
        compiler_params=params(24 * MIB),
        cost_estimate=cost(4 * depth * pixels * tn, 4 * pixels * (depth + tn)),
        name="numer",
    )(*args)


def exchange(value, axis, size, distance):
    return lax.ppermute(value, axis, [(i, i ^ distance) for i in range(size)])


def iteration(patterns, model, scale_table, scale_index, weight_table, weight_class, *, sizes):
    pix, ori = sizes["pix"], sizes["ori"]
    hops = pix.bit_length() - 1
    rows, columns = patterns.shape[0], model.shape[1]
    count = rows // pix
    tn = min(256, columns)
    chunks = columns // tn
    widths = [2 * tn] + [tn] * (chunks - 2) if chunks >= 4 else [tn] * chunks
    starts = [sum(widths[:c]) for c in range(len(widths))]
    chunks = len(widths)
    beta = (patterns.shape[1] * pix) ** -0.5
    place = lax.axis_index("pix")
    bits = [(place >> i) & 1 for i in range(hops)]

    phi = table_lookup(scale_table, scale_index)[:, None]
    classes = weight_class[None, :]
    side = lax.axis_index("pat")

    share = bit_reverse(place, hops) * count
    entries = [bits[0], side]
    places, offsets, size = {}, [0, 0], rows // 2
    for hop in range(1, hops):
        size //= 2
        places[hop] = len(entries)
        entries += [o + (1 - bits[hop]) * size for o in offsets]
        offsets = [o + bits[hop] * size for o in offsets] + [0]
    places["terms"] = len(entries)
    entries += offsets
    places["share"] = len(entries)
    entries.append(share)
    places["order"] = len(entries)
    entries += [share ^ (bit_reverse(d, hops) * count) for d in range(pix)]
    where = jnp.stack([jnp.asarray(e, jnp.int32) for e in entries])

    later = min(2, chunks - 1)
    turned, terms = {}, {}
    source = patterns
    for c in range(chunks):
        turns = ((False,) if c == 1 else ()) + ((True,) if c == later else ())
        send, keep, *rest = cross_chunk(
            where, phi, source, model, phi if c == 0 else terms[c - 1][0], starts[c], widths[c], beta, c == 0, turns
        )
        if c == 0:
            source = rest[-1]
        for own, value in zip(turns, rest):
            turned[own] = value
        terms[c] = [keep, exchange(send, "pix", pix, 1)]
        if c == 1:
            psib = exchange(turned[False], "pat", 2, 1)
    after = keep
    for c in range(chunks):
        size = rows // 2
        for hop in range(1, hops):
            size //= 2
            after = forward(where, places[hop], terms[c], size, after)
            terms[c].append(exchange(after, "pix", pix, 1 << hop))
    psib = load(psib, after)
    held = [term for c in range(chunks) for term in terms[c]]
    phi_sib = exchange(phi, "pat", 2, 1)

    exps, own = softmax_stage(where, places["terms"], weight_table, classes, psib, held, count, chunks)
    mine = own
    other = None
    for hop in range(ori.bit_length() - 1):
        if other is not None:
            mine = combine(mine, other)
        other = exchange(mine, "ori", ori, 1 << hop)
    shares = [columns // 2] * 2 if columns >= 512 else [columns]
    weights = weight_stage(where, places["share"], phi, exps, own, mine, other, shares)

    gathered = [[w] + [exchange(w, "pix", pix, d) for d in range(1, pix)] for w in weights]
    at, result, after = 0, None, model
    for width, parts in zip(shares, gathered):
        wown = pack(where, places["order"], parts, after)
        wsib = exchange(wown, "pat", 2, 1)
        result = numer_chunk(where, turned[True], psib, wown, wsib, phi, phi_sib, model, at, result)
        after = result
        at += width
    return result


def solution(mesh):
    placed = (
        P(("grp", "pat"), "pix"),
        P(("grp", "pix"), "ori"),
        P("grp"),
        P(("grp", "pat")),
        P("grp"),
        P(("grp", "ori")),
    )
    return jax.shard_map(
        functools.partial(iteration, sizes=dict(mesh.shape)),
        mesh=mesh,
        in_specs=placed,
        out_specs=P(("grp", "pix", "pat"), "ori"),
        check_vma=False,
    )
```

```python
import functools

import jax
import jax.numpy as jnp
from jax import lax
from jax.experimental import pallas as pl
from jax.experimental.pallas import tpu as pltpu
from jax.sharding import PartitionSpec as P

prior_weight = 0.5
MIB = 1 << 20
SLOTS = 4
PARTS = 4
VMEM = pl.BlockSpec(memory_space=pltpu.VMEM)
SMEM = pl.BlockSpec(memory_space=pltpu.SMEM)
HBM = pl.BlockSpec(memory_space=pltpu.HBM)
ANY = pl.BlockSpec(memory_space=pl.ANY)


def table_lookup(table, index):
    levels = jnp.arange(table.shape[0], dtype=jnp.int32)
    return jnp.sum(jnp.where(index[:, None] == levels[None, :], table[None, :], 0.0), axis=1)


def params(limit):
    return pltpu.CompilerParams(vmem_limit_bytes=limit)


def cost(flops, moved):
    return pl.CostEstimate(flops=flops, bytes_accessed=moved, transcendentals=0)


def bit_reverse(value, bits):
    return sum(((value >> i) & 1) << (bits - 1 - i) for i in range(bits))


def cross_kernel(where, phi, patterns, model, after, send, keep, *refs, column, tk, steps, beta, first, turns):
    turned, refs = refs[: len(turns)], refs[len(turns) :]
    if first:
        held, mbuf, acc, squares, msem, psem = refs
    else:
        held, (mbuf, acc, squares, msem) = patterns, refs
    tn = acc.shape[1]

    def copies(i):
        slot = lax.rem(i, SLOTS)
        at = pl.multiple_of(i * tk, tk)
        both = [pltpu.make_async_copy(model.at[pl.ds(at, tk), pl.ds(column, tn)], mbuf.at[slot], msem.at[slot])]
        if first:
            both.append(pltpu.make_async_copy(patterns.at[:, pl.ds(at, tk)], held.at[:, pl.ds(at, tk)], psem.at[slot]))
        return both

    for i in range(min(SLOTS - 1, steps)):
        for copy in copies(i):
            copy.start()
    acc[...] = jnp.zeros_like(acc)
    squares[...] = jnp.zeros_like(squares)

    def body(i, carry):
        for copy in copies(i):
            copy.wait()

        @pl.when(i + SLOTS - 1 < steps)
        def _():
            for copy in copies(i + SLOTS - 1):
                copy.start()

        tile = mbuf[lax.rem(i, SLOTS)]
        part = held[:, pl.ds(pl.multiple_of(i * tk, tk), tk)]
        acc[...] += jnp.dot(part, tile, preferred_element_type=jnp.float32)
        wide = tile.astype(jnp.float32)
        squares[...] += jnp.sum((wide * wide).reshape(tk // 8, 8, tn), axis=0)
        for own, out in zip(turns, turned):
            pixels = out.shape[0]
            width = pixels // steps
            side = where[1] if own else 1 - where[1]
            piece = held[:, pl.ds(pl.multiple_of(side * pixels + i * width, width), width)]
            out[pl.ds(pl.multiple_of(i * width, width), width), :] = piece.T
        return carry

    lax.fori_loop(0, steps, body, 0)
    sq = jnp.sum(squares[...], axis=0, keepdims=True)
    scale = phi[...]
    acc[...] = beta * (scale * acc[...] - 0.5 * (scale * scale) * sq)
    half = send.shape[0]
    send[...] = acc[pl.ds(pl.multiple_of((1 - where[0]) * half, half), half), :]
    keep[...] = acc[pl.ds(pl.multiple_of(where[0] * half, half), half), :]


def cross_chunk(where, phi, patterns, model, after, column, tn, beta, first, turns):
    rows, depth = patterns.shape
    tk = min(2048, depth)
    half = rows // 2
    shapes = [jax.ShapeDtypeStruct((half, tn), jnp.float32)] * 2
    shapes += [pltpu.VMEM((depth // 2, rows), patterns.dtype)] * len(turns)
    scratch = [
        pltpu.VMEM((SLOTS, tk, tn), jnp.bfloat16),
        pltpu.VMEM((rows, tn), jnp.float32),
        pltpu.VMEM((8, tn), jnp.float32),
        pltpu.SemaphoreType.DMA((SLOTS,)),
    ]
    if first:
        shapes.append(pltpu.VMEM(patterns.shape, patterns.dtype))
        scratch.append(pltpu.SemaphoreType.DMA((SLOTS,)))
    patterns = pltpu.with_memory_space_constraint(patterns, pltpu.HBM if first else pltpu.VMEM)
    model = pltpu.with_memory_space_constraint(model, pltpu.HBM)
    return pl.pallas_call(
        functools.partial(
            cross_kernel, column=column, tk=tk, steps=depth // tk, beta=beta, first=first, turns=turns
        ),
        out_shape=shapes,
        in_specs=[SMEM, VMEM, HBM if first else VMEM, HBM, ANY],
        out_specs=[VMEM] * len(shapes),
        scratch_shapes=scratch,
        compiler_params=params(20 * MIB),
        cost_estimate=cost(2 * rows * depth * tn, 2 * depth * (rows + tn)),
        name="cross",
    )(where, phi, patterns, model, after)


def forward_kernel(where, after, *refs, base):
    parts, out = refs[:-1], refs[-1]
    size = out.shape[0]
    total = None
    for t, part in enumerate(parts):
        piece = part[pl.ds(pl.multiple_of(where[base + t], size), size), :]
        total = piece if total is None else total + piece
    out[...] = total


def forward(where, base, parts, size, after):
    return pl.pallas_call(
        functools.partial(forward_kernel, base=base),
        out_shape=jax.ShapeDtypeStruct((size, parts[0].shape[1]), jnp.float32),
        in_specs=[SMEM, ANY] + [VMEM] * len(parts),
        out_specs=VMEM,
        compiler_params=params(4 * MIB),
        name="forward",
    )(where, after, *parts)


def softmax_kernel(where, table, classes, after, *refs, chunks, terms, base):
    parts, (exps, stats) = refs[:-2], refs[-2:]
    count = exps.shape[0]
    logw = jnp.zeros(classes.shape, jnp.float32)
    for q in range(table.shape[0]):
        logw = logw + jnp.where(classes[...] == q, table[q], 0.0)
    at = 0
    for c in range(chunks):
        tn = parts[c * terms].shape[1]
        total = None
        for t in range(terms):
            rows = pl.ds(pl.multiple_of(where[base + t], count), count)
            part = parts[c * terms + t][rows, :]
            total = part if total is None else total + part
        exps[:, at : at + tn] = total + logw[:, at : at + tn]
        at += tn
    top = jnp.max(exps[...], axis=1, keepdims=True)
    exps[...] = jnp.exp(exps[...] - top)
    total = jnp.sum(exps[...], axis=1, keepdims=True)
    lanes = (count, 128)
    stats[:8, :] = jnp.transpose(jnp.broadcast_to(top, lanes))[:8, :]
    stats[8:, :] = jnp.transpose(jnp.broadcast_to(total, lanes))[:8, :]


def softmax_stage(where, base, table, classes, after, parts, count, chunks):
    terms = len(parts) // chunks
    columns = classes.shape[1]
    return pl.pallas_call(
        functools.partial(softmax_kernel, chunks=chunks, terms=terms, base=base),
        out_shape=(
            jax.ShapeDtypeStruct((count, columns), jnp.float32),
            jax.ShapeDtypeStruct((16, count), jnp.float32),
        ),
        in_specs=[SMEM, SMEM, VMEM, ANY] + [VMEM] * len(parts),
        out_specs=(VMEM, VMEM),
        compiler_params=params(6 * MIB),
        name="softmax",
    )(where, table, classes, after, *parts)


def combine(mine, other):
    top = jnp.maximum(mine[:8], other[:8])
    total = mine[8:] * jnp.exp(mine[:8] - top) + other[8:] * jnp.exp(other[:8] - top)
    return jnp.concatenate([top, total], axis=0)


def weight_kernel(where, phi, exps, own, mine, other, *outs, base):
    count = exps.shape[0]

    def column(row):
        return jnp.transpose(jnp.broadcast_to(row[:1, :], (128, count)))[:, :1]

    top = jnp.maximum(mine[:8, :], other[:8, :])
    total = mine[8:, :] * jnp.exp(mine[:8, :] - top) + other[8:, :] * jnp.exp(other[:8, :] - top)
    factor = column(jnp.exp(own[:8, :] - top) / total)
    factor = factor * phi[pl.ds(pl.multiple_of(where[base], count), count), :]
    at = 0
    for out in outs:
        tn = out.shape[1]
        out[...] = (exps[:, at : at + tn] * factor).astype(jnp.bfloat16)
        at += tn


def weight_stage(where, base, phi, exps, own, mine, other, widths):
    count = exps.shape[0]
    return pl.pallas_call(
        functools.partial(weight_kernel, base=base),
        out_shape=[jax.ShapeDtypeStruct((count, tn), jnp.bfloat16) for tn in widths],
        in_specs=[SMEM] + [VMEM] * 5,
        out_specs=[VMEM] * len(widths),
        compiler_params=params(4 * MIB),
        name="weights",
    )(where, phi, exps, own, mine, other)


def pack_kernel(where, *refs, base):
    parts, out = refs[:-2], refs[-1]
    count = parts[0].shape[0]
    for d, part in enumerate(parts):
        out[pl.ds(pl.multiple_of(where[base + d], count), count), :] = part[...]


def pack(where, base, parts, after):
    count, tn = parts[0].shape
    after = pltpu.with_memory_space_constraint(after, pltpu.HBM)
    return pl.pallas_call(
        functools.partial(pack_kernel, base=base),
        out_shape=jax.ShapeDtypeStruct((count * len(parts), tn), jnp.bfloat16),
        in_specs=[SMEM] + [VMEM] * len(parts) + [HBM],
        out_specs=VMEM,
        compiler_params=params(8 * MIB),
        name="pack",
    )(where, *parts, after)


def load_kernel(source, after, out, sems):
    n = sems.shape[0]
    rows = out.shape[0] // n
    pieces = [pl.ds(i * rows, rows) for i in range(n)]
    copies = [pltpu.make_async_copy(source.at[p], out.at[p], sems.at[i]) for i, p in enumerate(pieces)]
    for copy in copies:
        copy.start()
    for copy in copies:
        copy.wait()


def load(source, after):
    return pl.pallas_call(
        load_kernel,
        out_shape=pltpu.VMEM(source.shape, source.dtype),
        in_specs=[HBM, ANY],
        out_specs=VMEM,
        scratch_shapes=[pltpu.SemaphoreType.DMA((4,))],
        compiler_params=params(8 * MIB),
        name="load",
    )(pltpu.with_memory_space_constraint(source, pltpu.HBM), after)


def pass_kernel(where, pown, psib, *refs, blocks, first, last, base, side, tm):
    count = pown.shape[1] // blocks[1]
    mine = 2 * len(blocks[0])
    pairs, refs = refs[:mine], refs[mine:]
    pixels = pown.shape[0]
    steps = pixels // tm
    *refs, tiles, tsem = refs
    factors, refs = refs[:2], refs[2:]
    if first:
        model, *sums, den, wide, buf, sem = refs
        seen = prior_weight
    elif last:
        seen, *totals, out, wide, buf, sem = refs
        seen = seen[...]
    else:
        seen, *totals = refs[: PARTS + 1]
        *sums, den, wide = refs[PARTS + 1 :]
        seen = seen[...]
    for k in range(mine):
        wide[k * count : (k + 1) * count, :] = pairs[k][...]

    def pieces(i):
        slot = lax.rem(i, 3)
        rows = pl.ds(pl.multiple_of(i * tm, tm), tm)
        for k in range(mine):
            columns = pl.ds(pl.multiple_of(where[base + blocks[0][k // 2]], count), count)
            part = (pown, psib)[k % 2].at[rows, columns]
            yield pltpu.make_async_copy(part, tiles.at[slot, :, pl.ds(k * count, count)], tsem.at[slot, k])

    def fetch(i):
        slot = lax.rem(i, 3)
        at = pl.multiple_of(where[side] * pixels + i * tm, tm)
        return pltpu.make_async_copy(model.at[pl.ds(at, tm)], buf.at[slot], sem.at[slot])

    def store(i):
        slot = lax.rem(i, 2)
        return pltpu.make_async_copy(buf.at[slot], out.at[pl.ds(pl.multiple_of(i * tm, tm), tm)], sem.at[slot])

    for i in range(min(2, steps)):
        for copy in pieces(i):
            copy.start()
        if first:
            fetch(i).start()
    for k, part in enumerate(pairs):
        rows = pl.ds(pl.multiple_of(where[base + blocks[0][k // 2]], count), count)
        seen = seen + jnp.sum(part[...].astype(jnp.float32) * factors[k % 2][rows, :], axis=0, keepdims=True)
    if last:
        scale = 1.0 / seen
    else:
        den[...] = seen

    def body(part, i, carry):
        local = pl.ds(pl.multiple_of(i * tm - part * (pixels // PARTS), tm), tm)
        for copy in pieces(i):
            copy.wait()
        if first:
            fetch(i).wait()

        @pl.when(i + 2 < steps)
        def _():
            for copy in pieces(i + 2):
                copy.start()
            if first:
                fetch(i + 2).start()

        if last:

            @pl.when(i >= 2)
            def _():
                store(i - 2).wait()

        acc = jnp.dot(tiles[lax.rem(i, 3)], wide[...], preferred_element_type=jnp.float32)
        if first:
            sums[part][local, :] = acc + prior_weight * buf[lax.rem(i, 3)].astype(jnp.float32)
        elif last:
            buf[lax.rem(i, 2)] = ((acc + totals[part][local, :]) * scale).astype(jnp.bfloat16)
            store(i).start()
        else:
            sums[part][local, :] = acc + totals[part][local, :]
        return carry

    for part in range(PARTS):
        lax.fori_loop(part * steps // PARTS, (part + 1) * steps // PARTS, functools.partial(body, part), 0)
    if last:
        for i in range(max(0, steps - 2), steps):
            store(i).wait()


def numer_pass(where, base, pown, psib, blocks, pairs, phis, pix, model=None, total=None, last=False):
    first = model is not None
    pixels, count, columns = pown.shape[0], pairs[0].shape[0], pairs[0].shape[1]
    tm = min(512, pixels // PARTS)
    constrain = pltpu.with_memory_space_constraint
    args = [where, constrain(pown, pltpu.HBM), constrain(psib, pltpu.HBM), *pairs, *phis]
    in_specs = [SMEM, HBM, HBM] + [VMEM] * (len(pairs) + 2)
    scratch = [pltpu.VMEM((len(pairs) * count, columns), jnp.bfloat16)]
    shape, aliases = [pltpu.VMEM((pixels // PARTS, columns), jnp.float32)] * PARTS, {}
    shape.append(jax.ShapeDtypeStruct((1, columns), jnp.float32))
    if first:
        args.append(constrain(model, pltpu.HBM))
        in_specs.append(HBM)
        scratch += [pltpu.VMEM((3, tm, columns), jnp.bfloat16), pltpu.SemaphoreType.DMA((3,))]
    else:
        args += [total[-1], *(constrain(part, pltpu.VMEM) for part in total[:-1])]
        in_specs += [VMEM] * (PARTS + 1)
    if last:
        shape = jax.ShapeDtypeStruct((pixels, columns), jnp.bfloat16)
        scratch += [pltpu.VMEM((2, tm, columns), jnp.bfloat16), pltpu.SemaphoreType.DMA((2,))]
    elif not first:
        aliases = {len(args) - PARTS + part: part for part in range(PARTS)}
    scratch += [
        pltpu.VMEM((3, tm, len(pairs) * count), jnp.bfloat16),
        pltpu.SemaphoreType.DMA((3, len(pairs))),
    ]
    return pl.pallas_call(
        functools.partial(
            pass_kernel, blocks=(blocks, pix), first=first, last=last, base=base, side=1, tm=tm
        ),
        out_shape=shape,
        in_specs=in_specs,
        out_specs=HBM if last else [VMEM] * (PARTS + 1),
        scratch_shapes=scratch,
        input_output_aliases=aliases,
        compiler_params=params(14 * MIB),
        cost_estimate=cost(2 * pixels * columns * count * len(pairs), 4 * pixels * columns),
        name="numer",
    )(*args)


def numer_kernel(where, pown, psib, wown, wsib, fown, fsib, model, *refs, column, tm, sub):
    out, mbuf, obuf, msem, osem = refs[-5:]
    pixels, tn = pown.shape[0], wown.shape[1]
    steps = pixels // tm

    def fetch(i):
        slot = lax.rem(i, 3)
        at = pl.multiple_of(where[1] * pixels + i * tm, tm)
        return pltpu.make_async_copy(model.at[pl.ds(at, tm), pl.ds(column, tn)], mbuf.at[slot], msem.at[slot])

    def store(i):
        slot = lax.rem(i, 2)
        at = pl.multiple_of(i * tm, tm)
        return pltpu.make_async_copy(obuf.at[slot], out.at[pl.ds(at, tm), pl.ds(column, tn)], osem.at[slot])

    for i in range(min(2, steps)):
        fetch(i).start()
    den = jnp.sum(wown[...].astype(jnp.float32) * fown[...], axis=0, keepdims=True)
    den = den + jnp.sum(wsib[...].astype(jnp.float32) * fsib[...], axis=0, keepdims=True)
    scale = 1.0 / (prior_weight + den)

    def body(i, carry):
        fetch(i).wait()

        @pl.when(i + 2 < steps)
        def _():
            fetch(i + 2).start()

        @pl.when(i >= 2)
        def _():
            store(i - 2).wait()

        for r in range(0, tm, sub):
            rows = pl.ds(pl.multiple_of(i * tm + r, sub), sub)
            acc = jnp.dot(pown[rows, :], wown[...], preferred_element_type=jnp.float32)
            acc = acc + jnp.dot(psib[rows, :], wsib[...], preferred_element_type=jnp.float32)
            acc = acc + prior_weight * mbuf[lax.rem(i, 3), r : r + sub, :].astype(jnp.float32)
            obuf[lax.rem(i, 2), r : r + sub, :] = (acc * scale).astype(jnp.bfloat16)
        store(i).start()
        return carry

    lax.fori_loop(0, steps, body, 0)
    for i in range(max(0, steps - 2), steps):
        store(i).wait()


def numer_chunk(where, pown, psib, wown, wsib, fown, fsib, model, column, previous):
    depth, tn = wown.shape
    pixels, columns = pown.shape[0], model.shape[1]
    tm = min(1024, pixels)
    pown = pltpu.with_memory_space_constraint(pown, pltpu.VMEM)
    psib = pltpu.with_memory_space_constraint(psib, pltpu.VMEM)
    model = pltpu.with_memory_space_constraint(model, pltpu.HBM)
    args = [where, pown, psib, wown, wsib, fown, fsib, model]
    in_specs = [SMEM] + [VMEM] * 6 + [HBM]
    aliases = {}
    if previous is not None:
        in_specs.append(HBM)
        args.append(pltpu.with_memory_space_constraint(previous, pltpu.HBM))
        aliases = {len(args) - 1: 0}
    return pl.pallas_call(
        functools.partial(numer_kernel, column=column, tm=tm, sub=min(256, tm)),
        out_shape=jax.ShapeDtypeStruct((pixels, columns), jnp.bfloat16),
        in_specs=in_specs,
        out_specs=HBM,
        scratch_shapes=[
            pltpu.VMEM((3, tm, tn), jnp.bfloat16),
            pltpu.VMEM((2, tm, tn), jnp.bfloat16),
            pltpu.SemaphoreType.DMA((3,)),
            pltpu.SemaphoreType.DMA((2,)),
        ],
        input_output_aliases=aliases,
        compiler_params=params(24 * MIB),
        cost_estimate=cost(4 * depth * pixels * tn, 4 * pixels * (depth + tn)),
        name="numer",
    )(*args)


def exchange(value, axis, size, distance):
    return lax.ppermute(value, axis, [(i, i ^ distance) for i in range(size)])


def iteration(patterns, model, scale_table, scale_index, weight_table, weight_class, *, sizes):
    pix, ori = sizes["pix"], sizes["ori"]
    hops = pix.bit_length() - 1
    rows, columns = patterns.shape[0], model.shape[1]
    count = rows // pix
    tn = min(256, columns)
    chunks = columns // tn
    widths = [2 * tn] + [tn] * (chunks - 2) if chunks >= 4 else [tn] * chunks
    starts = [sum(widths[:c]) for c in range(len(widths))]
    chunks = len(widths)
    beta = (patterns.shape[1] * pix) ** -0.5
    place = lax.axis_index("pix")
    bits = [(place >> i) & 1 for i in range(hops)]

    phi = table_lookup(scale_table, scale_index)[:, None]
    classes = weight_class[None, :]
    side = lax.axis_index("pat")

    share = bit_reverse(place, hops) * count
    entries = [bits[0], side]
    places, offsets, size = {}, [0, 0], rows // 2
    for hop in range(1, hops):
        size //= 2
        places[hop] = len(entries)
        entries += [o + (1 - bits[hop]) * size for o in offsets]
        offsets = [o + bits[hop] * size for o in offsets] + [0]
    places["terms"] = len(entries)
    entries += offsets
    places["share"] = len(entries)
    entries.append(share)
    places["order"] = len(entries)
    entries += [share ^ (bit_reverse(d, hops) * count) for d in range(pix)]
    where = jnp.stack([jnp.asarray(e, jnp.int32) for e in entries])

    later = min(2, chunks - 1)
    turned, terms = {}, {}
    source, after = patterns, phi

    def relay(c, after):
        size = rows // 2
        for hop in range(1, hops):
            size //= 2
            after = forward(where, places[hop], terms[c], size, after)
            terms[c].append(exchange(after, "pix", pix, 1 << hop))
        return after

    for c in range(chunks):
        turns = ((False,) if c == 1 else ()) + ((True,) if c == later else ())
        send, keep, *rest = cross_chunk(
            where, phi, source, model, after, starts[c], widths[c], beta, c == 0, turns
        )
        if c == 0:
            source = rest[-1]
        for own, value in zip(turns, rest):
            turned[own] = value
        terms[c] = [keep, exchange(send, "pix", pix, 1)]
        if c == 1:
            psib = exchange(turned[False], "pat", 2, 1)
        if c >= 1 and c < chunks:
            after = relay(c - 1, keep)
    after = relay(chunks - 1, keep)
    split = pix == 4 and count % 128 == 0
    if split:
        token = phi
    else:
        token = psib = load(psib, after)
    held = [term for c in range(chunks) for term in terms[c]]
    phi_sib = exchange(phi, "pat", 2, 1)

    exps, own = softmax_stage(where, places["terms"], weight_table, classes, token, held, count, chunks)
    mine = own
    other = None
    for hop in range(ori.bit_length() - 1):
        if other is not None:
            mine = combine(mine, other)
        other = exchange(mine, "ori", ori, 1 << hop)
    shares = [columns] if split or columns < 512 else [columns // 2] * 2
    weights = weight_stage(where, places["share"], phi, exps, own, mine, other, shares)

    if split:
        base = places["order"]
        own = [weights[0], exchange(weights[0], "pix", pix, 1), exchange(weights[0], "pix", pix, 2)]
        own.append(exchange(own[2], "pix", pix, 1))
        pairs = [(w, exchange(w, "pat", 2, 1)) for w in own]
        phis = (phi, phi_sib)
        total = numer_pass(where, base, turned[True], psib, (0,), pairs[0], phis, pix, model=model)
        total = numer_pass(where, base, turned[True], psib, (1,), pairs[1], phis, pix, total=total)
        return numer_pass(where, base, turned[True], psib, (2, 3), pairs[2] + pairs[3], phis, pix, total=total, last=True)

    gathered = [[w] + [exchange(w, "pix", pix, d) for d in range(1, pix)] for w in weights]
    at, result, after = 0, None, model
    for width, parts in zip(shares, gathered):
        wown = pack(where, places["order"], parts, after)
        wsib = exchange(wown, "pat", 2, 1)
        result = numer_chunk(where, turned[True], psib, wown, wsib, phi, phi_sib, model, at, result)
        after = result
        at += width
    return result


def solution(mesh):
    placed = (
        P(("grp", "pat"), "pix"),
        P(("grp", "pix"), "ori"),
        P("grp"),
        P(("grp", "pat")),
        P("grp"),
        P(("grp", "ori")),
    )
    return jax.shard_map(
        functools.partial(iteration, sizes=dict(mesh.shape)),
        mesh=mesh,
        in_specs=placed,
        out_specs=P(("grp", "pix", "pat"), "ori"),
        check_vma=False,
    )
```

```python
import functools

import jax
import jax.numpy as jnp
from jax import lax
from jax.experimental import pallas as pl
from jax.experimental.pallas import tpu as pltpu
from jax.sharding import PartitionSpec as P

prior_weight = 0.5
MIB = 1 << 20
SLOTS = 4
PARTS = 4
SUB = 256
VMEM = pl.BlockSpec(memory_space=pltpu.VMEM)
SMEM = pl.BlockSpec(memory_space=pltpu.SMEM)
HBM = pl.BlockSpec(memory_space=pltpu.HBM)
ANY = pl.BlockSpec(memory_space=pl.ANY)


def table_lookup(table, index):
    levels = jnp.arange(table.shape[0], dtype=jnp.int32)
    return jnp.sum(jnp.where(index[:, None] == levels[None, :], table[None, :], 0.0), axis=1)


def params(limit):
    return pltpu.CompilerParams(vmem_limit_bytes=limit)


def cost(flops, moved):
    return pl.CostEstimate(flops=flops, bytes_accessed=moved, transcendentals=0)


def bit_reverse(value, bits):
    return sum(((value >> i) & 1) << (bits - 1 - i) for i in range(bits))


def cross_kernel(where, phi, patterns, model, after, send, keep, *refs, column, tk, steps, beta, first, turns):
    turned, refs = refs[: len(turns)], refs[len(turns) :]
    if first:
        held, mbuf, acc, squares, msem, psem = refs
    else:
        held, (mbuf, acc, squares, msem) = patterns, refs
    tn = acc.shape[1]

    def copies(i):
        slot = lax.rem(i, SLOTS)
        at = pl.multiple_of(i * tk, tk)
        both = [pltpu.make_async_copy(model.at[pl.ds(at, tk), pl.ds(column, tn)], mbuf.at[slot], msem.at[slot])]
        if first:
            both.append(pltpu.make_async_copy(patterns.at[:, pl.ds(at, tk)], held.at[:, pl.ds(at, tk)], psem.at[slot]))
        return both

    for i in range(min(SLOTS - 1, steps)):
        for copy in copies(i):
            copy.start()
    acc[...] = jnp.zeros_like(acc)
    squares[...] = jnp.zeros_like(squares)

    def body(i, carry):
        for copy in copies(i):
            copy.wait()

        @pl.when(i + SLOTS - 1 < steps)
        def _():
            for copy in copies(i + SLOTS - 1):
                copy.start()

        tile = mbuf[lax.rem(i, SLOTS)]
        part = held[:, pl.ds(pl.multiple_of(i * tk, tk), tk)]
        acc[...] += jnp.dot(part, tile, preferred_element_type=jnp.float32)
        wide = tile.astype(jnp.float32)
        squares[...] += jnp.sum((wide * wide).reshape(tk // 8, 8, tn), axis=0)
        for own, out in zip(turns, turned):
            pixels = out.shape[0]
            width = pixels // steps
            side = where[1] if own else 1 - where[1]
            piece = held[:, pl.ds(pl.multiple_of(side * pixels + i * width, width), width)]
            out[pl.ds(pl.multiple_of(i * width, width), width), :] = piece.T
        return carry

    lax.fori_loop(0, steps, body, 0)
    sq = jnp.sum(squares[...], axis=0, keepdims=True)
    scale = phi[...]
    acc[...] = beta * (scale * acc[...] - 0.5 * (scale * scale) * sq)
    half = send.shape[0]
    send[...] = acc[pl.ds(pl.multiple_of((1 - where[0]) * half, half), half), :]
    keep[...] = acc[pl.ds(pl.multiple_of(where[0] * half, half), half), :]


def cross_chunk(where, phi, patterns, model, after, column, tn, beta, first, turns):
    rows, depth = patterns.shape
    tk = min(2048, depth)
    half = rows // 2
    shapes = [jax.ShapeDtypeStruct((half, tn), jnp.float32)] * 2
    shapes += [pltpu.VMEM((depth // 2, rows), patterns.dtype)] * len(turns)
    scratch = [
        pltpu.VMEM((SLOTS, tk, tn), jnp.bfloat16),
        pltpu.VMEM((rows, tn), jnp.float32),
        pltpu.VMEM((8, tn), jnp.float32),
        pltpu.SemaphoreType.DMA((SLOTS,)),
    ]
    if first:
        shapes.append(pltpu.VMEM(patterns.shape, patterns.dtype))
        scratch.append(pltpu.SemaphoreType.DMA((SLOTS,)))
    patterns = pltpu.with_memory_space_constraint(patterns, pltpu.HBM if first else pltpu.VMEM)
    model = pltpu.with_memory_space_constraint(model, pltpu.HBM)
    return pl.pallas_call(
        functools.partial(
            cross_kernel, column=column, tk=tk, steps=depth // tk, beta=beta, first=first, turns=turns
        ),
        out_shape=shapes,
        in_specs=[SMEM, VMEM, HBM if first else VMEM, HBM, ANY],
        out_specs=[VMEM] * len(shapes),
        scratch_shapes=scratch,
        compiler_params=params(20 * MIB),
        cost_estimate=cost(2 * rows * depth * tn, 2 * depth * (rows + tn)),
        name="cross",
    )(where, phi, patterns, model, after)


def forward_kernel(where, after, *refs, base):
    parts, out = refs[:-1], refs[-1]
    size = out.shape[0]
    total = None
    for t, part in enumerate(parts):
        piece = part[pl.ds(pl.multiple_of(where[base + t], size), size), :]
        total = piece if total is None else total + piece
    out[...] = total


def forward(where, base, parts, size, after):
    return pl.pallas_call(
        functools.partial(forward_kernel, base=base),
        out_shape=jax.ShapeDtypeStruct((size, parts[0].shape[1]), jnp.float32),
        in_specs=[SMEM, ANY] + [VMEM] * len(parts),
        out_specs=VMEM,
        compiler_params=params(4 * MIB),
        name="forward",
    )(where, after, *parts)


def softmax_kernel(where, table, classes, after, *refs, chunks, terms, base):
    parts, (exps, stats) = refs[:-2], refs[-2:]
    count = exps.shape[0]
    logw = jnp.zeros(classes.shape, jnp.float32)
    for q in range(table.shape[0]):
        logw = logw + jnp.where(classes[...] == q, table[q], 0.0)
    at = 0
    for c in range(chunks):
        tn = parts[c * terms].shape[1]
        total = None
        for t in range(terms):
            rows = pl.ds(pl.multiple_of(where[base + t], count), count)
            part = parts[c * terms + t][rows, :]
            total = part if total is None else total + part
        exps[:, at : at + tn] = total + logw[:, at : at + tn]
        at += tn
    top = jnp.max(exps[...], axis=1, keepdims=True)
    exps[...] = jnp.exp(exps[...] - top)
    total = jnp.sum(exps[...], axis=1, keepdims=True)
    lanes = (count, 128)
    stats[:8, :] = jnp.transpose(jnp.broadcast_to(top, lanes))[:8, :]
    stats[8:, :] = jnp.transpose(jnp.broadcast_to(total, lanes))[:8, :]


def softmax_stage(where, base, table, classes, after, parts, count, chunks):
    terms = len(parts) // chunks
    columns = classes.shape[1]
    return pl.pallas_call(
        functools.partial(softmax_kernel, chunks=chunks, terms=terms, base=base),
        out_shape=(
            jax.ShapeDtypeStruct((count, columns), jnp.float32),
            jax.ShapeDtypeStruct((16, count), jnp.float32),
        ),
        in_specs=[SMEM, SMEM, VMEM, ANY] + [VMEM] * len(parts),
        out_specs=(VMEM, VMEM),
        compiler_params=params(6 * MIB),
        name="softmax",
    )(where, table, classes, after, *parts)


def combine(mine, other):
    top = jnp.maximum(mine[:8], other[:8])
    total = mine[8:] * jnp.exp(mine[:8] - top) + other[8:] * jnp.exp(other[:8] - top)
    return jnp.concatenate([top, total], axis=0)


def weight_kernel(where, phi, exps, own, mine, other, *outs, base):
    count = exps.shape[0]

    def column(row):
        return jnp.transpose(jnp.broadcast_to(row[:1, :], (128, count)))[:, :1]

    top = jnp.maximum(mine[:8, :], other[:8, :])
    total = mine[8:, :] * jnp.exp(mine[:8, :] - top) + other[8:, :] * jnp.exp(other[:8, :] - top)
    factor = column(jnp.exp(own[:8, :] - top) / total)
    factor = factor * phi[pl.ds(pl.multiple_of(where[base], count), count), :]
    at = 0
    for out in outs:
        tn = out.shape[1]
        out[...] = (exps[:, at : at + tn] * factor).astype(jnp.bfloat16)
        at += tn


def weight_stage(where, base, phi, exps, own, mine, other, widths):
    count = exps.shape[0]
    return pl.pallas_call(
        functools.partial(weight_kernel, base=base),
        out_shape=[jax.ShapeDtypeStruct((count, tn), jnp.bfloat16) for tn in widths],
        in_specs=[SMEM] + [VMEM] * 5,
        out_specs=[VMEM] * len(widths),
        compiler_params=params(4 * MIB),
        name="weights",
    )(where, phi, exps, own, mine, other)


def pack_kernel(where, *refs, base):
    parts, out = refs[:-2], refs[-1]
    count = parts[0].shape[0]
    for d, part in enumerate(parts):
        out[pl.ds(pl.multiple_of(where[base + d], count), count), :] = part[...]


def pack(where, base, parts, after):
    count, tn = parts[0].shape
    after = pltpu.with_memory_space_constraint(after, pltpu.HBM)
    return pl.pallas_call(
        functools.partial(pack_kernel, base=base),
        out_shape=jax.ShapeDtypeStruct((count * len(parts), tn), jnp.bfloat16),
        in_specs=[SMEM] + [VMEM] * len(parts) + [HBM],
        out_specs=VMEM,
        compiler_params=params(8 * MIB),
        name="pack",
    )(where, *parts, after)


def load_kernel(source, after, out, sems):
    n = sems.shape[0]
    rows = out.shape[0] // n
    pieces = [pl.ds(i * rows, rows) for i in range(n)]
    copies = [pltpu.make_async_copy(source.at[p], out.at[p], sems.at[i]) for i, p in enumerate(pieces)]
    for copy in copies:
        copy.start()
    for copy in copies:
        copy.wait()


def load(source, after):
    return pl.pallas_call(
        load_kernel,
        out_shape=pltpu.VMEM(source.shape, source.dtype),
        in_specs=[HBM, ANY],
        out_specs=VMEM,
        scratch_shapes=[pltpu.SemaphoreType.DMA((4,))],
        compiler_params=params(8 * MIB),
        name="load",
    )(pltpu.with_memory_space_constraint(source, pltpu.HBM), after)


def begin_kernel(where, model, after, *refs, side, tm):
    *sums, token, buf, sem = refs
    token[...] = jnp.zeros_like(token)
    size = sums[0].shape[0]
    steps = size * PARTS // tm

    def fetch(i):
        slot = lax.rem(i, 4)
        at = pl.multiple_of(where[side] * size * PARTS + i * tm, tm)
        return pltpu.make_async_copy(model.at[pl.ds(at, tm)], buf.at[slot], sem.at[slot])

    for i in range(min(3, steps)):
        fetch(i).start()

    def body(part, i, carry):
        fetch(i).wait()

        @pl.when(i + 3 < steps)
        def _():
            fetch(i + 3).start()

        rows = pl.ds(pl.multiple_of(i * tm - part * size, tm), tm)
        sums[part][rows, :] = prior_weight * buf[lax.rem(i, 4)].astype(jnp.float32)
        return carry

    for part in range(PARTS):
        lax.fori_loop(part * steps // PARTS, (part + 1) * steps // PARTS, functools.partial(body, part), 0)


def begin(where, model, after):
    pixels, columns = model.shape[0] // 2, model.shape[1]
    tm = min(512, pixels // PARTS)
    *total, token = pl.pallas_call(
        functools.partial(begin_kernel, side=1, tm=tm),
        out_shape=[pltpu.VMEM((pixels // PARTS, columns), jnp.float32)] * PARTS
        + [jax.ShapeDtypeStruct((8, 128), jnp.float32)],
        in_specs=[SMEM, HBM, ANY],
        out_specs=[VMEM] * (PARTS + 1),
        scratch_shapes=[pltpu.VMEM((4, tm, columns), jnp.bfloat16), pltpu.SemaphoreType.DMA((4,))],
        compiler_params=params(10 * MIB),
        name="begin",
    )(where, pltpu.with_memory_space_constraint(model, pltpu.HBM), after)
    return total, token


def pass_kernel(where, pown, psib, *refs, blocks, pix, first, last, base, tm, sub):
    mine = 2 * len(blocks)
    count = pown.shape[1] // pix
    pixels = pown.shape[0]
    steps = pixels // tm
    pairs, factors, refs = refs[:mine], refs[mine : mine + 2], refs[mine + 2 :]
    seen, refs = (prior_weight, refs) if first else (refs[0][...], refs[1:])
    totals, refs = refs[:PARTS], refs[PARTS:]
    *refs, wide, tiles, tsem = refs
    for k in range(mine):
        wide[k * count : (k + 1) * count, :] = pairs[k][...]

    def pieces(i):
        slot = lax.rem(i, 3)
        rows = pl.ds(pl.multiple_of(i * tm, tm), tm)
        for k in range(mine):
            columns = pl.ds(pl.multiple_of(where[base + blocks[k // 2]], count), count)
            part = (pown, psib)[k % 2].at[rows, columns]
            yield pltpu.make_async_copy(part, tiles.at[slot, :, pl.ds(k * count, count)], tsem.at[slot, k])

    for i in range(min(2, steps)):
        for copy in pieces(i):
            copy.start()
    for k, part in enumerate(pairs):
        rows = pl.ds(pl.multiple_of(where[base + blocks[k // 2]], count), count)
        seen = seen + jnp.sum(part[...].astype(jnp.float32) * factors[k % 2][rows, :], axis=0, keepdims=True)
    if last:
        out, buf, sem = refs
        scale = 1.0 / seen
    else:
        *sums, den = refs
        den[...] = seen

    def store(i):
        slot = lax.rem(i, 2)
        return pltpu.make_async_copy(buf.at[slot], out.at[pl.ds(pl.multiple_of(i * tm, tm), tm)], sem.at[slot])

    def body(part, i, carry):
        for copy in pieces(i):
            copy.wait()

        @pl.when(i + 2 < steps)
        def _():
            for copy in pieces(i + 2):
                copy.start()

        if last:

            @pl.when(i >= 2)
            def _():
                store(i - 2).wait()

        for r in range(0, tm, sub):
            rows = pl.ds(pl.multiple_of(i * tm + r - part * (pixels // PARTS), sub), sub)
            dot = jnp.dot(tiles[lax.rem(i, 3), r : r + sub, :], wide[...], preferred_element_type=jnp.float32)
            if last:
                buf[lax.rem(i, 2), r : r + sub, :] = ((dot + totals[part][rows, :]) * scale).astype(jnp.bfloat16)
            else:
                sums[part][rows, :] += dot
        if last:
            store(i).start()
        return carry

    for part in range(PARTS):
        lax.fori_loop(part * steps // PARTS, (part + 1) * steps // PARTS, functools.partial(body, part), 0)
    if last:
        for i in range(max(0, steps - 2), steps):
            store(i).wait()


def numer_pass(where, base, pown, psib, blocks, pairs, phis, pix, total, den=None, last=False):
    first = den is None
    pixels, count, columns = pown.shape[0], pairs[0].shape[0], pairs[0].shape[1]
    tm = min(512, pixels // PARTS)
    constrain = pltpu.with_memory_space_constraint
    args = [where, constrain(pown, pltpu.HBM), constrain(psib, pltpu.HBM), *pairs, *phis]
    args += [] if first else [den]
    args += [constrain(part, pltpu.VMEM) for part in total]
    in_specs = [SMEM, HBM, HBM] + [VMEM] * (len(args) - 3)
    scratch = [
        pltpu.VMEM((len(pairs) * count, columns), jnp.bfloat16),
        pltpu.VMEM((3, tm, len(pairs) * count), jnp.bfloat16),
        pltpu.SemaphoreType.DMA((3, len(pairs))),
    ]
    if last:
        shape, out_specs, aliases = jax.ShapeDtypeStruct((pixels, columns), jnp.bfloat16), HBM, {}
        scratch = [pltpu.VMEM((2, tm, columns), jnp.bfloat16), pltpu.SemaphoreType.DMA((2,))] + scratch
    else:
        shape = [pltpu.VMEM(total[0].shape, jnp.float32)] * PARTS + [jax.ShapeDtypeStruct((1, columns), jnp.float32)]
        out_specs = [VMEM] * (PARTS + 1)
        aliases = {len(args) - PARTS + part: part for part in range(PARTS)}
    result = pl.pallas_call(
        functools.partial(
            pass_kernel, blocks=blocks, pix=pix, first=first, last=last, base=base, tm=tm, sub=min(SUB if last else 512, tm)
        ),
        out_shape=shape,
        in_specs=in_specs,
        out_specs=out_specs,
        scratch_shapes=scratch,
        input_output_aliases=aliases,
        compiler_params=params(12 * MIB),
        cost_estimate=cost(2 * pixels * columns * count * len(pairs), 4 * pixels * columns),
        name="numer",
    )(*args)
    return result if last else (result[:-1], result[-1])


def numer_kernel(where, pown, psib, wown, wsib, fown, fsib, model, *refs, column, tm, sub):
    out, mbuf, obuf, msem, osem = refs[-5:]
    pixels, tn = pown.shape[0], wown.shape[1]
    steps = pixels // tm

    def fetch(i):
        slot = lax.rem(i, 3)
        at = pl.multiple_of(where[1] * pixels + i * tm, tm)
        return pltpu.make_async_copy(model.at[pl.ds(at, tm), pl.ds(column, tn)], mbuf.at[slot], msem.at[slot])

    def store(i):
        slot = lax.rem(i, 2)
        at = pl.multiple_of(i * tm, tm)
        return pltpu.make_async_copy(obuf.at[slot], out.at[pl.ds(at, tm), pl.ds(column, tn)], osem.at[slot])

    for i in range(min(2, steps)):
        fetch(i).start()
    den = jnp.sum(wown[...].astype(jnp.float32) * fown[...], axis=0, keepdims=True)
    den = den + jnp.sum(wsib[...].astype(jnp.float32) * fsib[...], axis=0, keepdims=True)
    scale = 1.0 / (prior_weight + den)

    def body(i, carry):
        fetch(i).wait()

        @pl.when(i + 2 < steps)
        def _():
            fetch(i + 2).start()

        @pl.when(i >= 2)
        def _():
            store(i - 2).wait()

        for r in range(0, tm, sub):
            rows = pl.ds(pl.multiple_of(i * tm + r, sub), sub)
            acc = jnp.dot(pown[rows, :], wown[...], preferred_element_type=jnp.float32)
            acc = acc + jnp.dot(psib[rows, :], wsib[...], preferred_element_type=jnp.float32)
            acc = acc + prior_weight * mbuf[lax.rem(i, 3), r : r + sub, :].astype(jnp.float32)
            obuf[lax.rem(i, 2), r : r + sub, :] = (acc * scale).astype(jnp.bfloat16)
        store(i).start()
        return carry

    lax.fori_loop(0, steps, body, 0)
    for i in range(max(0, steps - 2), steps):
        store(i).wait()


def numer_chunk(where, pown, psib, wown, wsib, fown, fsib, model, column, previous):
    depth, tn = wown.shape
    pixels, columns = pown.shape[0], model.shape[1]
    tm = min(1024, pixels)
    pown = pltpu.with_memory_space_constraint(pown, pltpu.VMEM)
    psib = pltpu.with_memory_space_constraint(psib, pltpu.VMEM)
    model = pltpu.with_memory_space_constraint(model, pltpu.HBM)
    args = [where, pown, psib, wown, wsib, fown, fsib, model]
    in_specs = [SMEM] + [VMEM] * 6 + [HBM]
    aliases = {}
    if previous is not None:
        in_specs.append(HBM)
        args.append(pltpu.with_memory_space_constraint(previous, pltpu.HBM))
        aliases = {len(args) - 1: 0}
    return pl.pallas_call(
        functools.partial(numer_kernel, column=column, tm=tm, sub=min(256, tm)),
        out_shape=jax.ShapeDtypeStruct((pixels, columns), jnp.bfloat16),
        in_specs=in_specs,
        out_specs=HBM,
        scratch_shapes=[
            pltpu.VMEM((3, tm, tn), jnp.bfloat16),
            pltpu.VMEM((2, tm, tn), jnp.bfloat16),
            pltpu.SemaphoreType.DMA((3,)),
            pltpu.SemaphoreType.DMA((2,)),
        ],
        input_output_aliases=aliases,
        compiler_params=params(24 * MIB),
        cost_estimate=cost(4 * depth * pixels * tn, 4 * pixels * (depth + tn)),
        name="numer",
    )(*args)


def exchange(value, axis, size, distance):
    return lax.ppermute(value, axis, [(i, i ^ distance) for i in range(size)])


def iteration(patterns, model, scale_table, scale_index, weight_table, weight_class, *, sizes):
    pix, ori = sizes["pix"], sizes["ori"]
    hops = pix.bit_length() - 1
    rows, columns = patterns.shape[0], model.shape[1]
    count = rows // pix
    tn = min(256, columns)
    chunks = columns // tn
    widths = [2 * tn] + [tn] * (chunks - 2) if chunks >= 4 else [tn] * chunks
    starts = [sum(widths[:c]) for c in range(len(widths))]
    chunks = len(widths)
    beta = (patterns.shape[1] * pix) ** -0.5
    place = lax.axis_index("pix")
    bits = [(place >> i) & 1 for i in range(hops)]

    phi = table_lookup(scale_table, scale_index)[:, None]
    classes = weight_class[None, :]
    side = lax.axis_index("pat")

    share = bit_reverse(place, hops) * count
    entries = [bits[0], side]
    places, offsets, size = {}, [0, 0], rows // 2
    for hop in range(1, hops):
        size //= 2
        places[hop] = len(entries)
        entries += [o + (1 - bits[hop]) * size for o in offsets]
        offsets = [o + bits[hop] * size for o in offsets] + [0]
    places["terms"] = len(entries)
    entries += offsets
    places["share"] = len(entries)
    entries.append(share)
    places["order"] = len(entries)
    entries += [share ^ (bit_reverse(d, hops) * count) for d in range(pix)]
    where = jnp.stack([jnp.asarray(e, jnp.int32) for e in entries])

    later = min(2, chunks - 1)
    turned, terms = {}, {}
    source, after = patterns, phi

    def relay(c, after):
        size = rows // 2
        for hop in range(1, hops):
            size //= 2
            after = forward(where, places[hop], terms[c], size, after)
            terms[c].append(exchange(after, "pix", pix, 1 << hop))
        return after

    for c in range(chunks):
        turns = ((True,) if c == 1 else ()) + ((False,) if c == later else ())
        send, keep, *rest = cross_chunk(
            where, phi, source, model, after, starts[c], widths[c], beta, c == 0, turns
        )
        if c == 0:
            source = rest[-1]
        for own, value in zip(turns, rest):
            turned[own] = value
        terms[c] = [keep, exchange(send, "pix", pix, 1)]
        if c == later:
            psib = exchange(turned[False], "pat", 2, 1)
        if c >= 1 and c < chunks:
            after = relay(c - 1, keep)
    after = relay(chunks - 1, keep)
    split = pix == 4 and count % 128 == 0
    if split:
        total, token = begin(where, model, after)
    else:
        token = psib = load(psib, after)
    held = [term for c in range(chunks) for term in terms[c]]
    phi_sib = exchange(phi, "pat", 2, 1)

    exps, own = softmax_stage(where, places["terms"], weight_table, classes, token, held, count, chunks)
    mine = own
    other = None
    for hop in range(ori.bit_length() - 1):
        if other is not None:
            mine = combine(mine, other)
        other = exchange(mine, "ori", ori, 1 << hop)
    shares = [columns] if split or columns < 512 else [columns // 2] * 2
    weights = weight_stage(where, places["share"], phi, exps, own, mine, other, shares)

    if split:
        base = places["order"]
        own = [weights[0], exchange(weights[0], "pix", pix, 1), exchange(weights[0], "pix", pix, 2)]
        own.append(exchange(own[2], "pix", pix, 1))
        pairs = [(w, exchange(w, "pat", 2, 1)) for w in own]
        fixed = (where, base, turned[True], psib)
        phis = (phi, phi_sib)
        total, den = numer_pass(*fixed, (0,), pairs[0], phis, pix, total)
        total, den = numer_pass(*fixed, (1,), pairs[1], phis, pix, total, den)
        return numer_pass(*fixed, (2, 3), pairs[2] + pairs[3], phis, pix, total, den, last=True)

    gathered = [[w] + [exchange(w, "pix", pix, d) for d in range(1, pix)] for w in weights]
    at, result, after = 0, None, model
    for width, parts in zip(shares, gathered):
        wown = pack(where, places["order"], parts, after)
        wsib = exchange(wown, "pat", 2, 1)
        result = numer_chunk(where, turned[True], psib, wown, wsib, phi, phi_sib, model, at, result)
        after = result
        at += width
    return result


def solution(mesh):
    placed = (
        P(("grp", "pat"), "pix"),
        P(("grp", "pix"), "ori"),
        P("grp"),
        P(("grp", "pat")),
        P("grp"),
        P(("grp", "ori")),
    )
    return jax.shard_map(
        functools.partial(iteration, sizes=dict(mesh.shape)),
        mesh=mesh,
        in_specs=placed,
        out_specs=P(("grp", "pix", "pat"), "ori"),
        check_vma=False,
    )
```

```python
import functools

import jax
import jax.numpy as jnp
from jax import lax
from jax.experimental import pallas as pl
from jax.experimental.pallas import tpu as pltpu
from jax.sharding import PartitionSpec as P

prior_weight = 0.5
MIB = 1 << 20
SLOTS = 4
PARTS = 4
SUB = 256
VMEM = pl.BlockSpec(memory_space=pltpu.VMEM)
SMEM = pl.BlockSpec(memory_space=pltpu.SMEM)
HBM = pl.BlockSpec(memory_space=pltpu.HBM)
ANY = pl.BlockSpec(memory_space=pl.ANY)


def table_lookup(table, index):
    levels = jnp.arange(table.shape[0], dtype=jnp.int32)
    return jnp.sum(jnp.where(index[:, None] == levels[None, :], table[None, :], 0.0), axis=1)


def params(limit):
    return pltpu.CompilerParams(vmem_limit_bytes=limit)


def cost(flops, moved):
    return pl.CostEstimate(flops=flops, bytes_accessed=moved, transcendentals=0)


def bit_reverse(value, bits):
    return sum(((value >> i) & 1) << (bits - 1 - i) for i in range(bits))


def cross_kernel(where, phi, patterns, model, after, send, keep, *refs, column, tk, steps, beta, first, turns):
    turned, refs = refs[: len(turns)], refs[len(turns) :]
    if turns:
        *refs, tbuf, tsem = refs
    if first:
        held, mbuf, acc, squares, msem, psem = refs
    else:
        held, (mbuf, acc, squares, msem) = patterns, refs
    tn = acc.shape[1]

    def copies(i):
        slot = lax.rem(i, SLOTS)
        at = pl.multiple_of(i * tk, tk)
        both = [pltpu.make_async_copy(model.at[pl.ds(at, tk), pl.ds(column, tn)], mbuf.at[slot], msem.at[slot])]
        if first:
            both.append(pltpu.make_async_copy(patterns.at[:, pl.ds(at, tk)], held.at[:, pl.ds(at, tk)], psem.at[slot]))
        return both

    def stores(i):
        slot = lax.rem(i, 2)
        for t, out in enumerate(turned):
            width = out.shape[0] // steps
            rows = pl.ds(pl.multiple_of(i * width, width), width)
            yield pltpu.make_async_copy(tbuf.at[t, slot], out.at[rows], tsem.at[t, slot])

    for i in range(min(SLOTS - 1, steps)):
        for copy in copies(i):
            copy.start()
    acc[...] = jnp.zeros_like(acc)
    squares[...] = jnp.zeros_like(squares)

    def body(i, carry):
        for copy in copies(i):
            copy.wait()

        @pl.when(i + SLOTS - 1 < steps)
        def _():
            for copy in copies(i + SLOTS - 1):
                copy.start()

        if turns:

            @pl.when(i >= 2)
            def _():
                for copy in stores(i - 2):
                    copy.wait()

        tile = mbuf[lax.rem(i, SLOTS)]
        part = held[:, pl.ds(pl.multiple_of(i * tk, tk), tk)]
        acc[...] += jnp.dot(part, tile, preferred_element_type=jnp.float32)
        wide = tile.astype(jnp.float32)
        squares[...] += jnp.sum((wide * wide).reshape(tk // 8, 8, tn), axis=0)
        for t, (own, out) in enumerate(zip(turns, turned)):
            pixels = out.shape[0]
            width = pixels // steps
            side = where[1] if own else 1 - where[1]
            piece = held[:, pl.ds(pl.multiple_of(side * pixels + i * width, width), width)]
            tbuf[t, lax.rem(i, 2)] = piece.T
        for copy in stores(i):
            copy.start()
        return carry

    lax.fori_loop(0, steps, body, 0)
    sq = jnp.sum(squares[...], axis=0, keepdims=True)
    scale = phi[...]
    acc[...] = beta * (scale * acc[...] - 0.5 * (scale * scale) * sq)
    half = send.shape[0]
    send[...] = acc[pl.ds(pl.multiple_of((1 - where[0]) * half, half), half), :]
    keep[...] = acc[pl.ds(pl.multiple_of(where[0] * half, half), half), :]
    for i in range(max(0, steps - 2), steps):
        for copy in stores(i):
            copy.wait()


def cross_chunk(where, phi, patterns, model, after, column, tn, beta, first, turns):
    rows, depth = patterns.shape
    tk = min(2048, depth)
    half = rows // 2
    shapes = [jax.ShapeDtypeStruct((half, tn), jnp.float32)] * 2
    shapes += [pltpu.HBM((depth // 2, rows), patterns.dtype)] * len(turns)
    places = [VMEM, VMEM] + [HBM] * len(turns)
    scratch = [
        pltpu.VMEM((SLOTS, tk, tn), jnp.bfloat16),
        pltpu.VMEM((rows, tn), jnp.float32),
        pltpu.VMEM((8, tn), jnp.float32),
        pltpu.SemaphoreType.DMA((SLOTS,)),
    ]
    if first:
        shapes.append(pltpu.VMEM(patterns.shape, patterns.dtype))
        scratch.append(pltpu.SemaphoreType.DMA((SLOTS,)))
        places.append(VMEM)
    if turns:
        scratch.append(pltpu.VMEM((len(turns), 2, tk // 2, rows), patterns.dtype))
        scratch.append(pltpu.SemaphoreType.DMA((len(turns), 2)))
    patterns = pltpu.with_memory_space_constraint(patterns, pltpu.HBM if first else pltpu.VMEM)
    model = pltpu.with_memory_space_constraint(model, pltpu.HBM)
    return pl.pallas_call(
        functools.partial(
            cross_kernel, column=column, tk=tk, steps=depth // tk, beta=beta, first=first, turns=turns
        ),
        out_shape=shapes,
        in_specs=[SMEM, VMEM, HBM if first else VMEM, HBM, ANY],
        out_specs=places,
        scratch_shapes=scratch,
        compiler_params=params(20 * MIB),
        cost_estimate=cost(2 * rows * depth * tn, 2 * depth * (rows + tn)),
        name="cross",
    )(where, phi, patterns, model, after)


def forward_kernel(where, after, *refs, base):
    parts, out = refs[:-1], refs[-1]
    size = out.shape[0]
    total = None
    for t, part in enumerate(parts):
        piece = part[pl.ds(pl.multiple_of(where[base + t], size), size), :]
        total = piece if total is None else total + piece
    out[...] = total


def forward(where, base, parts, size, after):
    return pl.pallas_call(
        functools.partial(forward_kernel, base=base),
        out_shape=jax.ShapeDtypeStruct((size, parts[0].shape[1]), jnp.float32),
        in_specs=[SMEM, ANY] + [VMEM] * len(parts),
        out_specs=VMEM,
        compiler_params=params(4 * MIB),
        name="forward",
    )(where, after, *parts)


def softmax_kernel(where, table, classes, after, *refs, chunks, terms, base):
    parts, (exps, stats) = refs[:-2], refs[-2:]
    count = exps.shape[0]
    logw = jnp.zeros(classes.shape, jnp.float32)
    for q in range(table.shape[0]):
        logw = logw + jnp.where(classes[...] == q, table[q], 0.0)
    at = 0
    for c in range(chunks):
        tn = parts[c * terms].shape[1]
        total = None
        for t in range(terms):
            rows = pl.ds(pl.multiple_of(where[base + t], count), count)
            part = parts[c * terms + t][rows, :]
            total = part if total is None else total + part
        exps[:, at : at + tn] = total + logw[:, at : at + tn]
        at += tn
    top = jnp.max(exps[...], axis=1, keepdims=True)
    exps[...] = jnp.exp(exps[...] - top)
    total = jnp.sum(exps[...], axis=1, keepdims=True)
    lanes = (count, 128)
    stats[:8, :] = jnp.transpose(jnp.broadcast_to(top, lanes))[:8, :]
    stats[8:, :] = jnp.transpose(jnp.broadcast_to(total, lanes))[:8, :]


def softmax_stage(where, base, table, classes, after, parts, count, chunks):
    terms = len(parts) // chunks
    columns = classes.shape[1]
    return pl.pallas_call(
        functools.partial(softmax_kernel, chunks=chunks, terms=terms, base=base),
        out_shape=(
            jax.ShapeDtypeStruct((count, columns), jnp.float32),
            jax.ShapeDtypeStruct((16, count), jnp.float32),
        ),
        in_specs=[SMEM, SMEM, VMEM, ANY] + [VMEM] * len(parts),
        out_specs=(VMEM, VMEM),
        compiler_params=params(6 * MIB),
        name="softmax",
    )(where, table, classes, after, *parts)


def combine(mine, other):
    top = jnp.maximum(mine[:8], other[:8])
    total = mine[8:] * jnp.exp(mine[:8] - top) + other[8:] * jnp.exp(other[:8] - top)
    return jnp.concatenate([top, total], axis=0)


def weight_kernel(where, phi, exps, own, mine, other, *outs, base):
    count = exps.shape[0]

    def column(row):
        return jnp.transpose(jnp.broadcast_to(row[:1, :], (128, count)))[:, :1]

    top = jnp.maximum(mine[:8, :], other[:8, :])
    total = mine[8:, :] * jnp.exp(mine[:8, :] - top) + other[8:, :] * jnp.exp(other[:8, :] - top)
    factor = column(jnp.exp(own[:8, :] - top) / total)
    factor = factor * phi[pl.ds(pl.multiple_of(where[base], count), count), :]
    at = 0
    for out in outs:
        tn = out.shape[1]
        out[...] = (exps[:, at : at + tn] * factor).astype(jnp.bfloat16)
        at += tn


def weight_stage(where, base, phi, exps, own, mine, other, widths):
    count = exps.shape[0]
    return pl.pallas_call(
        functools.partial(weight_kernel, base=base),
        out_shape=[jax.ShapeDtypeStruct((count, tn), jnp.bfloat16) for tn in widths],
        in_specs=[SMEM] + [VMEM] * 5,
        out_specs=[VMEM] * len(widths),
        compiler_params=params(4 * MIB),
        name="weights",
    )(where, phi, exps, own, mine, other)


def pack_kernel(where, *refs, base):
    parts, out = refs[:-2], refs[-1]
    count = parts[0].shape[0]
    for d, part in enumerate(parts):
        out[pl.ds(pl.multiple_of(where[base + d], count), count), :] = part[...]


def pack(where, base, parts, after):
    count, tn = parts[0].shape
    after = pltpu.with_memory_space_constraint(after, pltpu.HBM)
    return pl.pallas_call(
        functools.partial(pack_kernel, base=base),
        out_shape=jax.ShapeDtypeStruct((count * len(parts), tn), jnp.bfloat16),
        in_specs=[SMEM] + [VMEM] * len(parts) + [HBM],
        out_specs=VMEM,
        compiler_params=params(8 * MIB),
        name="pack",
    )(where, *parts, after)


def load_kernel(source, after, out, sems):
    n = sems.shape[0]
    rows = out.shape[0] // n
    pieces = [pl.ds(i * rows, rows) for i in range(n)]
    copies = [pltpu.make_async_copy(source.at[p], out.at[p], sems.at[i]) for i, p in enumerate(pieces)]
    for copy in copies:
        copy.start()
    for copy in copies:
        copy.wait()


def load(source, after):
    return pl.pallas_call(
        load_kernel,
        out_shape=pltpu.VMEM(source.shape, source.dtype),
        in_specs=[HBM, ANY],
        out_specs=VMEM,
        scratch_shapes=[pltpu.SemaphoreType.DMA((4,))],
        compiler_params=params(8 * MIB),
        name="load",
    )(pltpu.with_memory_space_constraint(source, pltpu.HBM), after)


def begin_kernel(where, model, after, *refs, side, tm, start):
    *sums, token, buf, sem = refs
    token[...] = jnp.zeros_like(token)
    size = sums[0].shape[0]
    steps = size * len(sums) // tm

    def fetch(i):
        slot = lax.rem(i, 4)
        at = pl.multiple_of((where[side] * PARTS + start) * size + i * tm, tm)
        return pltpu.make_async_copy(model.at[pl.ds(at, tm)], buf.at[slot], sem.at[slot])

    for i in range(min(3, steps)):
        fetch(i).start()

    def body(part, i, carry):
        fetch(i).wait()

        @pl.when(i + 3 < steps)
        def _():
            fetch(i + 3).start()

        rows = pl.ds(pl.multiple_of(i * tm - part * size, tm), tm)
        sums[part][rows, :] = prior_weight * buf[lax.rem(i, 4)].astype(jnp.float32)
        return carry

    n = len(sums)
    for part in range(n):
        lax.fori_loop(part * steps // n, (part + 1) * steps // n, functools.partial(body, part), 0)


def begin(where, model, after, start, stop):
    pixels, columns = model.shape[0] // 2, model.shape[1]
    tm = min(512, pixels // PARTS)
    *total, token = pl.pallas_call(
        functools.partial(begin_kernel, side=1, tm=tm, start=start),
        out_shape=[pltpu.VMEM((pixels // PARTS, columns), jnp.float32)] * (stop - start)
        + [jax.ShapeDtypeStruct((8, 128), jnp.float32)],
        in_specs=[SMEM, HBM, ANY],
        out_specs=[VMEM] * (stop - start + 1),
        scratch_shapes=[pltpu.VMEM((4, tm, columns), jnp.bfloat16), pltpu.SemaphoreType.DMA((4,))],
        compiler_params=params(10 * MIB),
        name="begin",
    )(where, pltpu.with_memory_space_constraint(model, pltpu.HBM), after)
    return total, token


def pass_kernel(where, pown, psib, *refs, blocks, pix, first, last, base, tm, sub):
    mine = 2 * len(blocks)
    count = pown.shape[1] // pix
    pixels = pown.shape[0]
    steps = pixels // tm
    pairs, factors, refs = refs[:mine], refs[mine : mine + 2], refs[mine + 2 :]
    seen, refs = (prior_weight, refs) if first else (refs[0][...], refs[1:])
    totals, refs = refs[:PARTS], refs[PARTS:]
    *refs, wide, tiles, tsem = refs
    for k in range(mine):
        wide[k * count : (k + 1) * count, :] = pairs[k][...]

    def pieces(i):
        slot = lax.rem(i, 3)
        rows = pl.ds(pl.multiple_of(i * tm, tm), tm)
        for k in range(mine):
            columns = pl.ds(pl.multiple_of(where[base + blocks[k // 2]], count), count)
            part = (pown, psib)[k % 2].at[rows, columns]
            yield pltpu.make_async_copy(part, tiles.at[slot, :, pl.ds(k * count, count)], tsem.at[slot, k])

    for i in range(min(2, steps)):
        for copy in pieces(i):
            copy.start()
    for k, part in enumerate(pairs):
        rows = pl.ds(pl.multiple_of(where[base + blocks[k // 2]], count), count)
        seen = seen + jnp.sum(part[...].astype(jnp.float32) * factors[k % 2][rows, :], axis=0, keepdims=True)
    if last:
        out, buf, sem = refs
        scale = 1.0 / seen
    else:
        *sums, den = refs
        den[...] = seen

    def store(i):
        slot = lax.rem(i, 2)
        return pltpu.make_async_copy(buf.at[slot], out.at[pl.ds(pl.multiple_of(i * tm, tm), tm)], sem.at[slot])

    def body(part, i, carry):
        for copy in pieces(i):
            copy.wait()

        @pl.when(i + 2 < steps)
        def _():
            for copy in pieces(i + 2):
                copy.start()

        if last:

            @pl.when(i >= 2)
            def _():
                store(i - 2).wait()

        for r in range(0, tm, sub):
            rows = pl.ds(pl.multiple_of(i * tm + r - part * (pixels // PARTS), sub), sub)
            dot = jnp.dot(tiles[lax.rem(i, 3), r : r + sub, :], wide[...], preferred_element_type=jnp.float32)
            if last:
                buf[lax.rem(i, 2), r : r + sub, :] = ((dot + totals[part][rows, :]) * scale).astype(jnp.bfloat16)
            else:
                sums[part][rows, :] += dot
        if last:
            store(i).start()
        return carry

    for part in range(PARTS):
        lax.fori_loop(part * steps // PARTS, (part + 1) * steps // PARTS, functools.partial(body, part), 0)
    if last:
        for i in range(max(0, steps - 2), steps):
            store(i).wait()


def numer_pass(where, base, pown, psib, blocks, pairs, phis, pix, total, den=None, last=False):
    first = den is None
    pixels, count, columns = pown.shape[0], pairs[0].shape[0], pairs[0].shape[1]
    tm = min(512, pixels // PARTS)
    constrain = pltpu.with_memory_space_constraint
    args = [where, constrain(pown, pltpu.HBM), constrain(psib, pltpu.HBM), *pairs, *phis]
    args += [] if first else [den]
    args += [constrain(part, pltpu.VMEM) for part in total]
    in_specs = [SMEM, HBM, HBM] + [VMEM] * (len(args) - 3)
    scratch = [
        pltpu.VMEM((len(pairs) * count, columns), jnp.bfloat16),
        pltpu.VMEM((3, tm, len(pairs) * count), jnp.bfloat16),
        pltpu.SemaphoreType.DMA((3, len(pairs))),
    ]
    if last:
        shape, out_specs, aliases = jax.ShapeDtypeStruct((pixels, columns), jnp.bfloat16), HBM, {}
        scratch = [pltpu.VMEM((2, tm, columns), jnp.bfloat16), pltpu.SemaphoreType.DMA((2,))] + scratch
    else:
        shape = [pltpu.VMEM(total[0].shape, jnp.float32)] * PARTS + [jax.ShapeDtypeStruct((1, columns), jnp.float32)]
        out_specs = [VMEM] * (PARTS + 1)
        aliases = {len(args) - PARTS + part: part for part in range(PARTS)}
    result = pl.pallas_call(
        functools.partial(
            pass_kernel, blocks=blocks, pix=pix, first=first, last=last, base=base, tm=tm, sub=min(SUB if last else 512, tm)
        ),
        out_shape=shape,
        in_specs=in_specs,
        out_specs=out_specs,
        scratch_shapes=scratch,
        input_output_aliases=aliases,
        compiler_params=params(12 * MIB),
        cost_estimate=cost(2 * pixels * columns * count * len(pairs), 4 * pixels * columns),
        name="numer",
    )(*args)
    return result if last else (result[:-1], result[-1])


def numer_kernel(where, pown, psib, wown, wsib, fown, fsib, model, *refs, column, tm, sub):
    out, mbuf, obuf, msem, osem = refs[-5:]
    pixels, tn = pown.shape[0], wown.shape[1]
    steps = pixels // tm

    def fetch(i):
        slot = lax.rem(i, 3)
        at = pl.multiple_of(where[1] * pixels + i * tm, tm)
        return pltpu.make_async_copy(model.at[pl.ds(at, tm), pl.ds(column, tn)], mbuf.at[slot], msem.at[slot])

    def store(i):
        slot = lax.rem(i, 2)
        at = pl.multiple_of(i * tm, tm)
        return pltpu.make_async_copy(obuf.at[slot], out.at[pl.ds(at, tm), pl.ds(column, tn)], osem.at[slot])

    for i in range(min(2, steps)):
        fetch(i).start()
    den = jnp.sum(wown[...].astype(jnp.float32) * fown[...], axis=0, keepdims=True)
    den = den + jnp.sum(wsib[...].astype(jnp.float32) * fsib[...], axis=0, keepdims=True)
    scale = 1.0 / (prior_weight + den)

    def body(i, carry):
        fetch(i).wait()

        @pl.when(i + 2 < steps)
        def _():
            fetch(i + 2).start()

        @pl.when(i >= 2)
        def _():
            store(i - 2).wait()

        for r in range(0, tm, sub):
            rows = pl.ds(pl.multiple_of(i * tm + r, sub), sub)
            acc = jnp.dot(pown[rows, :], wown[...], preferred_element_type=jnp.float32)
            acc = acc + jnp.dot(psib[rows, :], wsib[...], preferred_element_type=jnp.float32)
            acc = acc + prior_weight * mbuf[lax.rem(i, 3), r : r + sub, :].astype(jnp.float32)
            obuf[lax.rem(i, 2), r : r + sub, :] = (acc * scale).astype(jnp.bfloat16)
        store(i).start()
        return carry

    lax.fori_loop(0, steps, body, 0)
    for i in range(max(0, steps - 2), steps):
        store(i).wait()


def numer_chunk(where, pown, psib, wown, wsib, fown, fsib, model, column, previous):
    depth, tn = wown.shape
    pixels, columns = pown.shape[0], model.shape[1]
    tm = min(1024, pixels)
    pown = pltpu.with_memory_space_constraint(pown, pltpu.VMEM)
    psib = pltpu.with_memory_space_constraint(psib, pltpu.VMEM)
    model = pltpu.with_memory_space_constraint(model, pltpu.HBM)
    args = [where, pown, psib, wown, wsib, fown, fsib, model]
    in_specs = [SMEM] + [VMEM] * 6 + [HBM]
    aliases = {}
    if previous is not None:
        in_specs.append(HBM)
        args.append(pltpu.with_memory_space_constraint(previous, pltpu.HBM))
        aliases = {len(args) - 1: 0}
    return pl.pallas_call(
        functools.partial(numer_kernel, column=column, tm=tm, sub=min(256, tm)),
        out_shape=jax.ShapeDtypeStruct((pixels, columns), jnp.bfloat16),
        in_specs=in_specs,
        out_specs=HBM,
        scratch_shapes=[
            pltpu.VMEM((3, tm, tn), jnp.bfloat16),
            pltpu.VMEM((2, tm, tn), jnp.bfloat16),
            pltpu.SemaphoreType.DMA((3,)),
            pltpu.SemaphoreType.DMA((2,)),
        ],
        input_output_aliases=aliases,
        compiler_params=params(24 * MIB),
        cost_estimate=cost(4 * depth * pixels * tn, 4 * pixels * (depth + tn)),
        name="numer",
    )(*args)


def exchange(value, axis, size, distance):
    return lax.ppermute(value, axis, [(i, i ^ distance) for i in range(size)])


def iteration(patterns, model, scale_table, scale_index, weight_table, weight_class, *, sizes):
    pix, ori = sizes["pix"], sizes["ori"]
    hops = pix.bit_length() - 1
    rows, columns = patterns.shape[0], model.shape[1]
    count = rows // pix
    tn = min(256, columns)
    chunks = columns // tn
    widths = [2 * tn] + [tn] * (chunks - 2) if chunks >= 4 else [tn] * chunks
    starts = [sum(widths[:c]) for c in range(len(widths))]
    chunks = len(widths)
    beta = (patterns.shape[1] * pix) ** -0.5
    place = lax.axis_index("pix")
    bits = [(place >> i) & 1 for i in range(hops)]

    phi = table_lookup(scale_table, scale_index)[:, None]
    classes = weight_class[None, :]
    side = lax.axis_index("pat")

    share = bit_reverse(place, hops) * count
    entries = [bits[0], side]
    places, offsets, size = {}, [0, 0], rows // 2
    for hop in range(1, hops):
        size //= 2
        places[hop] = len(entries)
        entries += [o + (1 - bits[hop]) * size for o in offsets]
        offsets = [o + bits[hop] * size for o in offsets] + [0]
    places["terms"] = len(entries)
    entries += offsets
    places["share"] = len(entries)
    entries.append(share)
    places["order"] = len(entries)
    entries += [share ^ (bit_reverse(d, hops) * count) for d in range(pix)]
    where = jnp.stack([jnp.asarray(e, jnp.int32) for e in entries])

    later = min(2, chunks - 1)
    turned, terms = {}, {}
    source, after = patterns, phi

    def relay(c, after):
        size = rows // 2
        for hop in range(1, hops):
            size //= 2
            after = forward(where, places[hop], terms[c], size, after)
            terms[c].append(exchange(after, "pix", pix, 1 << hop))
        return after

    for c in range(chunks):
        turns = ((True,) if c == 1 else ()) + ((False,) if c == later else ())
        send, keep, *rest = cross_chunk(
            where, phi, source, model, after, starts[c], widths[c], beta, c == 0, turns
        )
        if c == 0:
            source = rest[-1]
        for own, value in zip(turns, rest):
            turned[own] = value
        terms[c] = [keep, exchange(send, "pix", pix, 1)]
        if c == later:
            psib = exchange(turned[False], "pat", 2, 1)
        if c >= 1 and c < chunks:
            after = relay(c - 1, keep)
    split = pix == 4 and count % 128 == 0
    ready = keep
    if split:
        total, ready = begin(where, model, after, 0, PARTS // 2)
    after = relay(chunks - 1, ready)
    if split:
        more, token = begin(where, model, after, PARTS // 2, PARTS)
        total = total + more
    else:
        token = psib = load(psib, after)
    held = [term for c in range(chunks) for term in terms[c]]
    phi_sib = exchange(phi, "pat", 2, 1)

    exps, own = softmax_stage(where, places["terms"], weight_table, classes, token, held, count, chunks)
    mine = own
    other = None
    for hop in range(ori.bit_length() - 1):
        if other is not None:
            mine = combine(mine, other)
        other = exchange(mine, "ori", ori, 1 << hop)
    shares = [columns] if split or columns < 512 else [columns // 2] * 2
    weights = weight_stage(where, places["share"], phi, exps, own, mine, other, shares)

    if split:
        base = places["order"]
        own = [weights[0], exchange(weights[0], "pix", pix, 1), exchange(weights[0], "pix", pix, 2)]
        own.append(exchange(own[2], "pix", pix, 1))
        pairs = [(w, exchange(w, "pat", 2, 1)) for w in own]
        fixed = (where, base, turned[True], psib)
        phis = (phi, phi_sib)
        total, den = numer_pass(*fixed, (0,), pairs[0], phis, pix, total)
        total, den = numer_pass(*fixed, (1,), pairs[1], phis, pix, total, den)
        return numer_pass(*fixed, (2, 3), pairs[2] + pairs[3], phis, pix, total, den, last=True)

    gathered = [[w] + [exchange(w, "pix", pix, d) for d in range(1, pix)] for w in weights]
    at, result, after = 0, None, model
    for width, parts in zip(shares, gathered):
        wown = pack(where, places["order"], parts, after)
        wsib = exchange(wown, "pat", 2, 1)
        result = numer_chunk(where, turned[True], psib, wown, wsib, phi, phi_sib, model, at, result)
        after = result
        at += width
    return result


def solution(mesh):
    placed = (
        P(("grp", "pat"), "pix"),
        P(("grp", "pix"), "ori"),
        P("grp"),
        P(("grp", "pat")),
        P("grp"),
        P(("grp", "ori")),
    )
    return jax.shard_map(
        functools.partial(iteration, sizes=dict(mesh.shape)),
        mesh=mesh,
        in_specs=placed,
        out_specs=P(("grp", "pix", "pat"), "ori"),
        check_vma=False,
    )
```

```python
import functools

import jax
import jax.numpy as jnp
from jax import lax
from jax.experimental import pallas as pl
from jax.experimental.pallas import tpu as pltpu
from jax.sharding import PartitionSpec as P

prior_weight = 0.5
MIB = 1 << 20
SLOTS = 4
PARTS = 4
SUB = 256
AHEAD = 6
OUT = 4
TURN = 3
VMEM = pl.BlockSpec(memory_space=pltpu.VMEM)
SMEM = pl.BlockSpec(memory_space=pltpu.SMEM)
HBM = pl.BlockSpec(memory_space=pltpu.HBM)
ANY = pl.BlockSpec(memory_space=pl.ANY)


def table_lookup(table, index):
    levels = jnp.arange(table.shape[0], dtype=jnp.int32)
    return jnp.sum(jnp.where(index[:, None] == levels[None, :], table[None, :], 0.0), axis=1)


def params(limit):
    return pltpu.CompilerParams(vmem_limit_bytes=limit)


def cost(flops, moved):
    return pl.CostEstimate(flops=flops, bytes_accessed=moved, transcendentals=0)


def bit_reverse(value, bits):
    return sum(((value >> i) & 1) << (bits - 1 - i) for i in range(bits))


def cross_kernel(where, phi, patterns, model, after, send, keep, *refs, column, tk, steps, beta, first, turns):
    turned, refs = refs[: len(turns)], refs[len(turns) :]
    if turns:
        *refs, tbuf, tsem = refs
    if first:
        held, mbuf, acc, squares, msem, psem = refs
    else:
        held, (mbuf, acc, squares, msem) = patterns, refs
    tn = acc.shape[1]

    def copies(i):
        slot = lax.rem(i, SLOTS)
        at = pl.multiple_of(i * tk, tk)
        both = [pltpu.make_async_copy(model.at[pl.ds(at, tk), pl.ds(column, tn)], mbuf.at[slot], msem.at[slot])]
        if first:
            both.append(pltpu.make_async_copy(patterns.at[:, pl.ds(at, tk)], held.at[:, pl.ds(at, tk)], psem.at[slot]))
        return both

    def stores(i):
        slot = lax.rem(i, TURN)
        for t, out in enumerate(turned):
            width = out.shape[0] // steps
            rows = pl.ds(pl.multiple_of(i * width, width), width)
            yield pltpu.make_async_copy(tbuf.at[t, slot], out.at[rows], tsem.at[t, slot])

    for i in range(min(SLOTS - 1, steps)):
        for copy in copies(i):
            copy.start()
    acc[...] = jnp.zeros_like(acc)
    squares[...] = jnp.zeros_like(squares)

    def body(i, carry):
        for copy in copies(i):
            copy.wait()

        @pl.when(i + SLOTS - 1 < steps)
        def _():
            for copy in copies(i + SLOTS - 1):
                copy.start()

        if turns:

            @pl.when(i >= TURN)
            def _():
                for copy in stores(i - TURN):
                    copy.wait()

        tile = mbuf[lax.rem(i, SLOTS)]
        part = held[:, pl.ds(pl.multiple_of(i * tk, tk), tk)]
        acc[...] += jnp.dot(part, tile, preferred_element_type=jnp.float32)
        wide = tile.astype(jnp.float32)
        squares[...] += jnp.sum((wide * wide).reshape(tk // 8, 8, tn), axis=0)
        for t, (own, out) in enumerate(zip(turns, turned)):
            pixels = out.shape[0]
            width = pixels // steps
            side = where[1] if own else 1 - where[1]
            piece = held[:, pl.ds(pl.multiple_of(side * pixels + i * width, width), width)]
            tbuf[t, lax.rem(i, TURN)] = piece.T
        for copy in stores(i):
            copy.start()
        return carry

    lax.fori_loop(0, steps, body, 0)
    sq = jnp.sum(squares[...], axis=0, keepdims=True)
    scale = phi[...]
    acc[...] = beta * (scale * acc[...] - 0.5 * (scale * scale) * sq)
    half = send.shape[0]
    send[...] = acc[pl.ds(pl.multiple_of((1 - where[0]) * half, half), half), :]
    keep[...] = acc[pl.ds(pl.multiple_of(where[0] * half, half), half), :]
    for i in range(max(0, steps - TURN), steps):
        for copy in stores(i):
            copy.wait()


def cross_chunk(where, phi, patterns, model, after, column, tn, beta, first, turns):
    rows, depth = patterns.shape
    tk = min(2048, depth)
    half = rows // 2
    shapes = [jax.ShapeDtypeStruct((half, tn), jnp.float32)] * 2
    shapes += [pltpu.HBM((depth // 2, rows), patterns.dtype)] * len(turns)
    places = [VMEM, VMEM] + [HBM] * len(turns)
    scratch = [
        pltpu.VMEM((SLOTS, tk, tn), jnp.bfloat16),
        pltpu.VMEM((rows, tn), jnp.float32),
        pltpu.VMEM((8, tn), jnp.float32),
        pltpu.SemaphoreType.DMA((SLOTS,)),
    ]
    if first:
        shapes.append(pltpu.VMEM(patterns.shape, patterns.dtype))
        scratch.append(pltpu.SemaphoreType.DMA((SLOTS,)))
        places.append(VMEM)
    if turns:
        scratch.append(pltpu.VMEM((len(turns), TURN, tk // 2, rows), patterns.dtype))
        scratch.append(pltpu.SemaphoreType.DMA((len(turns), TURN)))
    patterns = pltpu.with_memory_space_constraint(patterns, pltpu.HBM if first else pltpu.VMEM)
    model = pltpu.with_memory_space_constraint(model, pltpu.HBM)
    return pl.pallas_call(
        functools.partial(
            cross_kernel, column=column, tk=tk, steps=depth // tk, beta=beta, first=first, turns=turns
        ),
        out_shape=shapes,
        in_specs=[SMEM, VMEM, HBM if first else VMEM, HBM, ANY],
        out_specs=places,
        scratch_shapes=scratch,
        compiler_params=params(20 * MIB),
        cost_estimate=cost(2 * rows * depth * tn, 2 * depth * (rows + tn)),
        name="cross",
    )(where, phi, patterns, model, after)


def forward_kernel(where, after, *refs, base):
    parts, out = refs[:-1], refs[-1]
    size = out.shape[0]
    total = None
    for t, part in enumerate(parts):
        piece = part[pl.ds(pl.multiple_of(where[base + t], size), size), :]
        total = piece if total is None else total + piece
    out[...] = total


def forward(where, base, parts, size, after):
    return pl.pallas_call(
        functools.partial(forward_kernel, base=base),
        out_shape=jax.ShapeDtypeStruct((size, parts[0].shape[1]), jnp.float32),
        in_specs=[SMEM, ANY] + [VMEM] * len(parts),
        out_specs=VMEM,
        compiler_params=params(4 * MIB),
        name="forward",
    )(where, after, *parts)


def softmax_kernel(where, table, classes, after, *refs, chunks, terms, base):
    parts, (exps, stats) = refs[:-2], refs[-2:]
    count = exps.shape[0]
    logw = jnp.zeros(classes.shape, jnp.float32)
    for q in range(table.shape[0]):
        logw = logw + jnp.where(classes[...] == q, table[q], 0.0)
    at = 0
    for c in range(chunks):
        tn = parts[c * terms].shape[1]
        total = None
        for t in range(terms):
            rows = pl.ds(pl.multiple_of(where[base + t], count), count)
            part = parts[c * terms + t][rows, :]
            total = part if total is None else total + part
        exps[:, at : at + tn] = total + logw[:, at : at + tn]
        at += tn
    top = jnp.max(exps[...], axis=1, keepdims=True)
    exps[...] = jnp.exp(exps[...] - top)
    total = jnp.sum(exps[...], axis=1, keepdims=True)
    lanes = (count, 128)
    stats[:8, :] = jnp.transpose(jnp.broadcast_to(top, lanes))[:8, :]
    stats[8:, :] = jnp.transpose(jnp.broadcast_to(total, lanes))[:8, :]


def softmax_stage(where, base, table, classes, after, parts, count, chunks):
    terms = len(parts) // chunks
    columns = classes.shape[1]
    return pl.pallas_call(
        functools.partial(softmax_kernel, chunks=chunks, terms=terms, base=base),
        out_shape=(
            jax.ShapeDtypeStruct((count, columns), jnp.float32),
            jax.ShapeDtypeStruct((16, count), jnp.float32),
        ),
        in_specs=[SMEM, SMEM, VMEM, ANY] + [VMEM] * len(parts),
        out_specs=(VMEM, VMEM),
        compiler_params=params(6 * MIB),
        name="softmax",
    )(where, table, classes, after, *parts)


def combine(mine, other):
    top = jnp.maximum(mine[:8], other[:8])
    total = mine[8:] * jnp.exp(mine[:8] - top) + other[8:] * jnp.exp(other[:8] - top)
    return jnp.concatenate([top, total], axis=0)


def weight_kernel(where, phi, exps, own, mine, other, *outs, base):
    count = exps.shape[0]

    def column(row):
        return jnp.transpose(jnp.broadcast_to(row[:1, :], (128, count)))[:, :1]

    top = jnp.maximum(mine[:8, :], other[:8, :])
    total = mine[8:, :] * jnp.exp(mine[:8, :] - top) + other[8:, :] * jnp.exp(other[:8, :] - top)
    factor = column(jnp.exp(own[:8, :] - top) / total)
    factor = factor * phi[pl.ds(pl.multiple_of(where[base], count), count), :]
    at = 0
    for out in outs:
        tn = out.shape[1]
        out[...] = (exps[:, at : at + tn] * factor).astype(jnp.bfloat16)
        at += tn


def weight_stage(where, base, phi, exps, own, mine, other, widths):
    count = exps.shape[0]
    return pl.pallas_call(
        functools.partial(weight_kernel, base=base),
        out_shape=[jax.ShapeDtypeStruct((count, tn), jnp.bfloat16) for tn in widths],
        in_specs=[SMEM] + [VMEM] * 5,
        out_specs=[VMEM] * len(widths),
        compiler_params=params(22 * MIB),
        name="weights",
    )(where, phi, exps, own, mine, other)


def pack_kernel(where, *refs, base):
    parts, out = refs[:-2], refs[-1]
    count = parts[0].shape[0]
    for d, part in enumerate(parts):
        out[pl.ds(pl.multiple_of(where[base + d], count), count), :] = part[...]


def pack(where, base, parts, after):
    count, tn = parts[0].shape
    after = pltpu.with_memory_space_constraint(after, pltpu.HBM)
    return pl.pallas_call(
        functools.partial(pack_kernel, base=base),
        out_shape=jax.ShapeDtypeStruct((count * len(parts), tn), jnp.bfloat16),
        in_specs=[SMEM] + [VMEM] * len(parts) + [HBM],
        out_specs=VMEM,
        compiler_params=params(8 * MIB),
        name="pack",
    )(where, *parts, after)


def load_kernel(source, after, out, sems):
    n = sems.shape[0]
    rows = out.shape[0] // n
    pieces = [pl.ds(i * rows, rows) for i in range(n)]
    copies = [pltpu.make_async_copy(source.at[p], out.at[p], sems.at[i]) for i, p in enumerate(pieces)]
    for copy in copies:
        copy.start()
    for copy in copies:
        copy.wait()


def load(source, after):
    return pl.pallas_call(
        load_kernel,
        out_shape=pltpu.VMEM(source.shape, source.dtype),
        in_specs=[HBM, ANY],
        out_specs=VMEM,
        scratch_shapes=[pltpu.SemaphoreType.DMA((4,))],
        compiler_params=params(8 * MIB),
        name="load",
    )(pltpu.with_memory_space_constraint(source, pltpu.HBM), after)


def begin_kernel(where, model, after, *refs, side, tm, start):
    *sums, token, buf, sem = refs
    token[...] = jnp.zeros_like(token)
    size = sums[0].shape[0]
    steps = size * len(sums) // tm

    def fetch(i):
        slot = lax.rem(i, 4)
        at = pl.multiple_of((where[side] * PARTS + start) * size + i * tm, tm)
        return pltpu.make_async_copy(model.at[pl.ds(at, tm)], buf.at[slot], sem.at[slot])

    for i in range(min(3, steps)):
        fetch(i).start()

    def body(part, i, carry):
        fetch(i).wait()

        @pl.when(i + 3 < steps)
        def _():
            fetch(i + 3).start()

        rows = pl.ds(pl.multiple_of(i * tm - part * size, tm), tm)
        sums[part][rows, :] = prior_weight * buf[lax.rem(i, 4)].astype(jnp.float32)
        return carry

    n = len(sums)
    for part in range(n):
        lax.fori_loop(part * steps // n, (part + 1) * steps // n, functools.partial(body, part), 0)


def begin(where, model, after, start, stop):
    pixels, columns = model.shape[0] // 2, model.shape[1]
    tm = min(512, pixels // PARTS)
    *total, token = pl.pallas_call(
        functools.partial(begin_kernel, side=1, tm=tm, start=start),
        out_shape=[pltpu.VMEM((pixels // PARTS, columns), jnp.float32)] * (stop - start)
        + [jax.ShapeDtypeStruct((8, 128), jnp.float32)],
        in_specs=[SMEM, HBM, ANY],
        out_specs=[VMEM] * (stop - start + 1),
        scratch_shapes=[pltpu.VMEM((4, tm, columns), jnp.bfloat16), pltpu.SemaphoreType.DMA((4,))],
        compiler_params=params(10 * MIB),
        name="begin",
    )(where, pltpu.with_memory_space_constraint(model, pltpu.HBM), after)
    return total, token


def pass_kernel(where, pown, psib, *refs, blocks, pix, first, last, base, tm, sub):
    mine = 2 * len(blocks)
    count = pown.shape[1] // pix
    pixels = pown.shape[0]
    steps = pixels // tm
    pairs, factors, refs = refs[:mine], refs[mine : mine + 2], refs[mine + 2 :]
    seen, refs = (prior_weight, refs) if first else (refs[0][...], refs[1:])
    totals, refs = refs[:PARTS], refs[PARTS:]
    *refs, wide, tiles, tsem = refs
    for k in range(mine):
        wide[k * count : (k + 1) * count, :] = pairs[k][...]

    def pieces(i):
        slot = lax.rem(i, AHEAD)
        rows = pl.ds(pl.multiple_of(i * tm, tm), tm)
        for k in range(mine):
            columns = pl.ds(pl.multiple_of(where[base + blocks[k // 2]], count), count)
            part = (pown, psib)[k % 2].at[rows, columns]
            yield pltpu.make_async_copy(part, tiles.at[slot, :, pl.ds(k * count, count)], tsem.at[slot, k])

    for i in range(min(AHEAD - 1, steps)):
        for copy in pieces(i):
            copy.start()
    for k, part in enumerate(pairs):
        rows = pl.ds(pl.multiple_of(where[base + blocks[k // 2]], count), count)
        seen = seen + jnp.sum(part[...].astype(jnp.float32) * factors[k % 2][rows, :], axis=0, keepdims=True)
    if last:
        out, buf, sem = refs
        scale = 1.0 / seen
    else:
        *sums, den = refs
        den[...] = seen

    def store(i):
        slot = lax.rem(i, OUT)
        return pltpu.make_async_copy(buf.at[slot], out.at[pl.ds(pl.multiple_of(i * tm, tm), tm)], sem.at[slot])

    def body(part, i, carry):
        for copy in pieces(i):
            copy.wait()

        @pl.when(i + AHEAD - 1 < steps)
        def _():
            for copy in pieces(i + AHEAD - 1):
                copy.start()

        if last:

            @pl.when(i >= OUT)
            def _():
                store(i - OUT).wait()

        for r in range(0, tm, sub):
            rows = pl.ds(pl.multiple_of(i * tm + r - part * (pixels // PARTS), sub), sub)
            dot = jnp.dot(tiles[lax.rem(i, AHEAD), r : r + sub, :], wide[...], preferred_element_type=jnp.float32)
            if last:
                buf[lax.rem(i, OUT), r : r + sub, :] = ((dot + totals[part][rows, :]) * scale).astype(jnp.bfloat16)
            else:
                sums[part][rows, :] += dot
        if last:
            store(i).start()
        return carry

    for part in range(PARTS):
        lax.fori_loop(part * steps // PARTS, (part + 1) * steps // PARTS, functools.partial(body, part), 0)
    if last:
        for i in range(max(0, steps - OUT), steps):
            store(i).wait()


def numer_pass(where, base, pown, psib, blocks, pairs, phis, pix, total, den=None, last=False):
    first = den is None
    pixels, count, columns = pown.shape[0], pairs[0].shape[0], pairs[0].shape[1]
    tm = min(512, pixels // PARTS)
    constrain = pltpu.with_memory_space_constraint
    args = [where, constrain(pown, pltpu.HBM), constrain(psib, pltpu.HBM), *pairs, *phis]
    args += [] if first else [den]
    args += [constrain(part, pltpu.VMEM) for part in total]
    in_specs = [SMEM, HBM, HBM] + [VMEM] * (len(args) - 3)
    scratch = [
        pltpu.VMEM((len(pairs) * count, columns), jnp.bfloat16),
        pltpu.VMEM((AHEAD, tm, len(pairs) * count), jnp.bfloat16),
        pltpu.SemaphoreType.DMA((AHEAD, len(pairs))),
    ]
    if last:
        shape, out_specs, aliases = jax.ShapeDtypeStruct((pixels, columns), jnp.bfloat16), HBM, {}
        scratch = [pltpu.VMEM((OUT, tm, columns), jnp.bfloat16), pltpu.SemaphoreType.DMA((OUT,))] + scratch
    else:
        shape = [pltpu.VMEM(total[0].shape, jnp.float32)] * PARTS + [jax.ShapeDtypeStruct((1, columns), jnp.float32)]
        out_specs = [VMEM] * (PARTS + 1)
        aliases = {len(args) - PARTS + part: part for part in range(PARTS)}
    result = pl.pallas_call(
        functools.partial(
            pass_kernel, blocks=blocks, pix=pix, first=first, last=last, base=base, tm=tm, sub=min(SUB if last else 512, tm)
        ),
        out_shape=shape,
        in_specs=in_specs,
        out_specs=out_specs,
        scratch_shapes=scratch,
        input_output_aliases=aliases,
        compiler_params=params(14 * MIB),
        cost_estimate=cost(2 * pixels * columns * count * len(pairs), 4 * pixels * columns),
        name="numer",
    )(*args)
    return result if last else (result[:-1], result[-1])


def numer_kernel(where, pown, psib, wown, wsib, fown, fsib, model, *refs, column, tm, sub):
    out, mbuf, obuf, msem, osem = refs[-5:]
    pixels, tn = pown.shape[0], wown.shape[1]
    steps = pixels // tm

    def fetch(i):
        slot = lax.rem(i, 3)
        at = pl.multiple_of(where[1] * pixels + i * tm, tm)
        return pltpu.make_async_copy(model.at[pl.ds(at, tm), pl.ds(column, tn)], mbuf.at[slot], msem.at[slot])

    def store(i):
        slot = lax.rem(i, 2)
        at = pl.multiple_of(i * tm, tm)
        return pltpu.make_async_copy(obuf.at[slot], out.at[pl.ds(at, tm), pl.ds(column, tn)], osem.at[slot])

    for i in range(min(2, steps)):
        fetch(i).start()
    den = jnp.sum(wown[...].astype(jnp.float32) * fown[...], axis=0, keepdims=True)
    den = den + jnp.sum(wsib[...].astype(jnp.float32) * fsib[...], axis=0, keepdims=True)
    scale = 1.0 / (prior_weight + den)

    def body(i, carry):
        fetch(i).wait()

        @pl.when(i + 2 < steps)
        def _():
            fetch(i + 2).start()

        @pl.when(i >= 2)
        def _():
            store(i - 2).wait()

        for r in range(0, tm, sub):
            rows = pl.ds(pl.multiple_of(i * tm + r, sub), sub)
            acc = jnp.dot(pown[rows, :], wown[...], preferred_element_type=jnp.float32)
            acc = acc + jnp.dot(psib[rows, :], wsib[...], preferred_element_type=jnp.float32)
            acc = acc + prior_weight * mbuf[lax.rem(i, 3), r : r + sub, :].astype(jnp.float32)
            obuf[lax.rem(i, 2), r : r + sub, :] = (acc * scale).astype(jnp.bfloat16)
        store(i).start()
        return carry

    lax.fori_loop(0, steps, body, 0)
    for i in range(max(0, steps - 2), steps):
        store(i).wait()


def numer_chunk(where, pown, psib, wown, wsib, fown, fsib, model, column, previous):
    depth, tn = wown.shape
    pixels, columns = pown.shape[0], model.shape[1]
    tm = min(1024, pixels)
    pown = pltpu.with_memory_space_constraint(pown, pltpu.VMEM)
    psib = pltpu.with_memory_space_constraint(psib, pltpu.VMEM)
    model = pltpu.with_memory_space_constraint(model, pltpu.HBM)
    args = [where, pown, psib, wown, wsib, fown, fsib, model]
    in_specs = [SMEM] + [VMEM] * 6 + [HBM]
    aliases = {}
    if previous is not None:
        in_specs.append(HBM)
        args.append(pltpu.with_memory_space_constraint(previous, pltpu.HBM))
        aliases = {len(args) - 1: 0}
    return pl.pallas_call(
        functools.partial(numer_kernel, column=column, tm=tm, sub=min(256, tm)),
        out_shape=jax.ShapeDtypeStruct((pixels, columns), jnp.bfloat16),
        in_specs=in_specs,
        out_specs=HBM,
        scratch_shapes=[
            pltpu.VMEM((3, tm, tn), jnp.bfloat16),
            pltpu.VMEM((2, tm, tn), jnp.bfloat16),
            pltpu.SemaphoreType.DMA((3,)),
            pltpu.SemaphoreType.DMA((2,)),
        ],
        input_output_aliases=aliases,
        compiler_params=params(24 * MIB),
        cost_estimate=cost(4 * depth * pixels * tn, 4 * pixels * (depth + tn)),
        name="numer",
    )(*args)


def exchange(value, axis, size, distance):
    return lax.ppermute(value, axis, [(i, i ^ distance) for i in range(size)])


def iteration(patterns, model, scale_table, scale_index, weight_table, weight_class, *, sizes):
    pix, ori = sizes["pix"], sizes["ori"]
    hops = pix.bit_length() - 1
    rows, columns = patterns.shape[0], model.shape[1]
    count = rows // pix
    tn = min(256, columns)
    chunks = columns // tn
    widths = [columns // 2, columns * 3 // 8, columns // 8] if chunks >= 4 else [tn] * chunks
    starts = [sum(widths[:c]) for c in range(len(widths))]
    chunks = len(widths)
    beta = (patterns.shape[1] * pix) ** -0.5
    place = lax.axis_index("pix")
    bits = [(place >> i) & 1 for i in range(hops)]

    phi = table_lookup(scale_table, scale_index)[:, None]
    classes = weight_class[None, :]
    side = lax.axis_index("pat")

    share = bit_reverse(place, hops) * count
    entries = [bits[0], side]
    places, offsets, size = {}, [0, 0], rows // 2
    for hop in range(1, hops):
        size //= 2
        places[hop] = len(entries)
        entries += [o + (1 - bits[hop]) * size for o in offsets]
        offsets = [o + bits[hop] * size for o in offsets] + [0]
    places["terms"] = len(entries)
    entries += offsets
    places["share"] = len(entries)
    entries.append(share)
    places["order"] = len(entries)
    entries += [share ^ (bit_reverse(d, hops) * count) for d in range(pix)]
    where = jnp.stack([jnp.asarray(e, jnp.int32) for e in entries])

    later = min(2, chunks - 1)
    turned, terms = {}, {}
    source, after = patterns, phi

    def relay(c, after):
        size = rows // 2
        for hop in range(1, hops):
            size //= 2
            after = forward(where, places[hop], terms[c], size, after)
            terms[c].append(exchange(after, "pix", pix, 1 << hop))
        return after

    for c in range(chunks):
        turns = ((True,) if c == 1 else ()) + ((False,) if c == later else ())
        send, keep, *rest = cross_chunk(
            where, phi, source, model, after, starts[c], widths[c], beta, c == 0, turns
        )
        if c == 0:
            source = rest[-1]
        for own, value in zip(turns, rest):
            turned[own] = value
        terms[c] = [keep, exchange(send, "pix", pix, 1)]
        if c == later:
            psib = exchange(turned[False], "pat", 2, 1)
        if c >= 1 and c < chunks:
            after = relay(c - 1, keep)
    split = pix == 4 and count % 128 == 0
    ready = keep
    if split:
        total, ready = begin(where, model, after, 0, PARTS // 2)
    after = relay(chunks - 1, ready)
    if split:
        more, token = begin(where, model, after, PARTS // 2, PARTS)
        total = total + more
    else:
        token = psib = load(psib, after)
    held = [term for c in range(chunks) for term in terms[c]]
    phi_sib = exchange(phi, "pat", 2, 1)

    exps, own = softmax_stage(where, places["terms"], weight_table, classes, token, held, count, chunks)
    mine = own
    other = None
    for hop in range(ori.bit_length() - 1):
        if other is not None:
            mine = combine(mine, other)
        other = exchange(mine, "ori", ori, 1 << hop)
    shares = [columns] if split or columns < 512 else [columns // 2] * 2
    weights = weight_stage(where, places["share"], phi, exps, own, mine, other, shares)

    if split:
        base = places["order"]
        own = [weights[0], exchange(weights[0], "pix", pix, 1), exchange(weights[0], "pix", pix, 2)]
        own.append(exchange(own[2], "pix", pix, 1))
        pairs = [(w, exchange(w, "pat", 2, 1)) for w in own]
        fixed = (where, base, turned[True], psib)
        phis = (phi, phi_sib)
        total, den = numer_pass(*fixed, (0,), pairs[0], phis, pix, total)
        total, den = numer_pass(*fixed, (1,), pairs[1], phis, pix, total, den)
        return numer_pass(*fixed, (2, 3), pairs[2] + pairs[3], phis, pix, total, den, last=True)

    gathered = [[w] + [exchange(w, "pix", pix, d) for d in range(1, pix)] for w in weights]
    at, result, after = 0, None, model
    for width, parts in zip(shares, gathered):
        wown = pack(where, places["order"], parts, after)
        wsib = exchange(wown, "pat", 2, 1)
        result = numer_chunk(where, turned[True], psib, wown, wsib, phi, phi_sib, model, at, result)
        after = result
        at += width
    return result


def solution(mesh):
    placed = (
        P(("grp", "pat"), "pix"),
        P(("grp", "pix"), "ori"),
        P("grp"),
        P(("grp", "pat")),
        P("grp"),
        P(("grp", "ori")),
    )
    return jax.shard_map(
        functools.partial(iteration, sizes=dict(mesh.shape)),
        mesh=mesh,
        in_specs=placed,
        out_specs=P(("grp", "pix", "pat"), "ori"),
        check_vma=False,
    )
```

```python
import functools

import jax
import jax.numpy as jnp
from jax import lax
from jax.experimental import pallas as pl
from jax.experimental.pallas import tpu as pltpu
from jax.sharding import PartitionSpec as P

prior_weight = 0.5
MIB = 1 << 20
SLOTS = 4
PARTS = 4
SUB = 256
AHEAD = 6
OUT = 4
TURN = 3
VMEM = pl.BlockSpec(memory_space=pltpu.VMEM)
SMEM = pl.BlockSpec(memory_space=pltpu.SMEM)
HBM = pl.BlockSpec(memory_space=pltpu.HBM)
ANY = pl.BlockSpec(memory_space=pl.ANY)


def table_lookup(table, index):
    levels = jnp.arange(table.shape[0], dtype=jnp.int32)
    return jnp.sum(jnp.where(index[:, None] == levels[None, :], table[None, :], 0.0), axis=1)


def params(limit):
    return pltpu.CompilerParams(vmem_limit_bytes=limit)


def cost(flops, moved):
    return pl.CostEstimate(flops=flops, bytes_accessed=moved, transcendentals=0)


def bit_reverse(value, bits):
    return sum(((value >> i) & 1) << (bits - 1 - i) for i in range(bits))


EXPONENTS = range(-12, 21)


def encoded(rows, tn):
    return jax.ShapeDtypeStruct((rows * 3 // 4 + 8, tn), jnp.int32)


def power_of_two(exponent, sign):
    total = jnp.zeros(exponent.shape, jnp.float32)
    for e in EXPONENTS:
        total = total + jnp.where(exponent == e, 2.0 ** (sign * (e - 22)), 0.0)
    return total


def encode(values, out):
    rows, tn = values.shape
    n = rows // 4
    top = jnp.max(jnp.max(jnp.abs(values), axis=0, keepdims=True), axis=1, keepdims=True)
    top = jnp.broadcast_to(top, (8, 128))
    exponent = jnp.full(top.shape, EXPONENTS[0], jnp.int32)
    for e in EXPONENTS[:-1]:
        exponent = exponent + jnp.where(top > 2.0**e, 1, 0)
    factor = power_of_two(exponent, -1)[:1, :1]
    code = (values * factor + 12582912.0).astype(jnp.int32) - 8388608
    last = code[3 * n :, :]
    for k in range(3):
        part = jnp.bitwise_and(lax.shift_right_logical(last, 8 * k), 255)
        out[k * n : (k + 1) * n, :] = jnp.bitwise_or(code[k * n : (k + 1) * n, :], lax.shift_left(part, 24))
    out[3 * n :, :] = jnp.broadcast_to(exponent[:, :1], (8, tn))


def decode(words, out):
    rows = out.shape[0]
    n = rows // 4
    factor = power_of_two(words[3 * n :, :128], 1)[:1, :1]
    last = None
    for k in range(3):
        word = words[k * n : (k + 1) * n, :]
        code = jnp.bitwise_and(word, 16777215)
        out[k * n : (k + 1) * n, :] = (code.astype(jnp.float32) - 4194304.0) * factor
        high = lax.shift_left(lax.shift_right_logical(word, 24), 8 * k)
        last = high if last is None else jnp.bitwise_or(last, high)
    out[3 * n :, :] = (last.astype(jnp.float32) - 4194304.0) * factor


def cross_kernel(where, phi, patterns, model, after, send, keep, *refs, column, tk, steps, beta, first, turns):
    turned, refs = refs[: len(turns)], refs[len(turns) :]
    if turns:
        *refs, tbuf, tsem = refs
    if first:
        held, mbuf, acc, squares, msem, psem = refs
    else:
        held, (mbuf, acc, squares, msem) = patterns, refs
    tn = acc.shape[1]

    def copies(i):
        slot = lax.rem(i, SLOTS)
        at = pl.multiple_of(i * tk, tk)
        both = [pltpu.make_async_copy(model.at[pl.ds(at, tk), pl.ds(column, tn)], mbuf.at[slot], msem.at[slot])]
        if first:
            both.append(pltpu.make_async_copy(patterns.at[:, pl.ds(at, tk)], held.at[:, pl.ds(at, tk)], psem.at[slot]))
        return both

    def stores(i):
        slot = lax.rem(i, TURN)
        for t, out in enumerate(turned):
            width = out.shape[0] // steps
            rows = pl.ds(pl.multiple_of(i * width, width), width)
            yield pltpu.make_async_copy(tbuf.at[t, slot], out.at[rows], tsem.at[t, slot])

    for i in range(min(SLOTS - 1, steps)):
        for copy in copies(i):
            copy.start()
    acc[...] = jnp.zeros_like(acc)
    squares[...] = jnp.zeros_like(squares)

    def body(i, carry):
        for copy in copies(i):
            copy.wait()

        @pl.when(i + SLOTS - 1 < steps)
        def _():
            for copy in copies(i + SLOTS - 1):
                copy.start()

        if turns:

            @pl.when(i >= TURN)
            def _():
                for copy in stores(i - TURN):
                    copy.wait()

        tile = mbuf[lax.rem(i, SLOTS)]
        part = held[:, pl.ds(pl.multiple_of(i * tk, tk), tk)]
        acc[...] += jnp.dot(part, tile, preferred_element_type=jnp.float32)
        wide = tile.astype(jnp.float32)
        squares[...] += jnp.sum((wide * wide).reshape(tk // 8, 8, tn), axis=0)
        for t, (own, out) in enumerate(zip(turns, turned)):
            pixels = out.shape[0]
            width = pixels // steps
            side = where[1] if own else 1 - where[1]
            piece = held[:, pl.ds(pl.multiple_of(side * pixels + i * width, width), width)]
            tbuf[t, lax.rem(i, TURN)] = piece.T
        for copy in stores(i):
            copy.start()
        return carry

    lax.fori_loop(0, steps, body, 0)
    sq = jnp.sum(squares[...], axis=0, keepdims=True)
    scale = phi[...]
    acc[...] = beta * (scale * acc[...] - 0.5 * (scale * scale) * sq)
    half = keep.shape[0]
    encode(acc[pl.ds(pl.multiple_of((1 - where[0]) * half, half), half), :], send)
    keep[...] = acc[pl.ds(pl.multiple_of(where[0] * half, half), half), :]
    for i in range(max(0, steps - TURN), steps):
        for copy in stores(i):
            copy.wait()


def cross_chunk(where, phi, patterns, model, after, column, tn, beta, first, turns):
    rows, depth = patterns.shape
    tk = min(2048, depth)
    half = rows // 2
    shapes = [encoded(half, tn), jax.ShapeDtypeStruct((half, tn), jnp.float32)]
    shapes += [pltpu.HBM((depth // 2, rows), patterns.dtype)] * len(turns)
    places = [VMEM, VMEM] + [HBM] * len(turns)
    scratch = [
        pltpu.VMEM((SLOTS, tk, tn), jnp.bfloat16),
        pltpu.VMEM((rows, tn), jnp.float32),
        pltpu.VMEM((8, tn), jnp.float32),
        pltpu.SemaphoreType.DMA((SLOTS,)),
    ]
    if first:
        shapes.append(pltpu.VMEM(patterns.shape, patterns.dtype))
        scratch.append(pltpu.SemaphoreType.DMA((SLOTS,)))
        places.append(VMEM)
    if turns:
        scratch.append(pltpu.VMEM((len(turns), TURN, tk // 2, rows), patterns.dtype))
        scratch.append(pltpu.SemaphoreType.DMA((len(turns), TURN)))
    patterns = pltpu.with_memory_space_constraint(patterns, pltpu.HBM if first else pltpu.VMEM)
    model = pltpu.with_memory_space_constraint(model, pltpu.HBM)
    return pl.pallas_call(
        functools.partial(
            cross_kernel, column=column, tk=tk, steps=depth // tk, beta=beta, first=first, turns=turns
        ),
        out_shape=shapes,
        in_specs=[SMEM, VMEM, HBM if first else VMEM, HBM, ANY],
        out_specs=places,
        scratch_shapes=scratch,
        compiler_params=params(20 * MIB),
        cost_estimate=cost(2 * rows * depth * tn, 2 * depth * (rows + tn)),
        name="cross",
    )(where, phi, patterns, model, after)


def forward_kernel(where, after, *refs, base, terms):
    parts, out, decoded = refs[:terms], refs[terms], refs[terms + 1 :]
    size = (out.shape[0] - 8) * 4 // 3
    total = None
    for t, part in enumerate(parts):
        if t > 0:
            decode(part, decoded[t - 1])
            part = decoded[t - 1]
        piece = part[pl.ds(pl.multiple_of(where[base + t], size), size), :]
        total = piece if total is None else total + piece
    encode(total, out)


def sizes_of(parts):
    return [((p.shape[0] - 8) * 4 // 3, p.shape[1]) for p in parts]


def forward(where, base, parts, size, after):
    return pl.pallas_call(
        functools.partial(forward_kernel, base=base, terms=len(parts)),
        out_shape=encoded(size, parts[0].shape[1]),
        in_specs=[SMEM, ANY] + [VMEM] * len(parts),
        out_specs=VMEM,
        scratch_shapes=[pltpu.VMEM(shape, jnp.float32) for shape in sizes_of(parts[1:])],
        compiler_params=params(6 * MIB),
        name="forward",
    )(where, after, *parts)


def softmax_kernel(where, table, classes, after, *refs, chunks, terms, base):
    parts, refs = refs[: chunks * terms], refs[chunks * terms :]
    exps, stats, decoded = refs[0], refs[1], refs[2:]
    count = exps.shape[0]
    logw = jnp.zeros(classes.shape, jnp.float32)
    for q in range(table.shape[0]):
        logw = logw + jnp.where(classes[...] == q, table[q], 0.0)
    at = 0
    for c in range(chunks):
        tn = parts[c * terms].shape[1]
        total = None
        for t in range(terms):
            rows = pl.ds(pl.multiple_of(where[base + t], count), count)
            part = parts[c * terms + t]
            if t > 0:
                room = decoded[c * (terms - 1) + t - 1]
                decode(part, room)
                part = room
            part = part[rows, :]
            total = part if total is None else total + part
        exps[:, at : at + tn] = total + logw[:, at : at + tn]
        at += tn
    top = jnp.max(exps[...], axis=1, keepdims=True)
    exps[...] = jnp.exp(exps[...] - top)
    total = jnp.sum(exps[...], axis=1, keepdims=True)
    lanes = (count, 128)
    stats[:8, :] = jnp.transpose(jnp.broadcast_to(top, lanes))[:8, :]
    stats[8:, :] = jnp.transpose(jnp.broadcast_to(total, lanes))[:8, :]


def softmax_stage(where, base, table, classes, after, parts, count, chunks):
    terms = len(parts) // chunks
    columns = classes.shape[1]
    return pl.pallas_call(
        functools.partial(softmax_kernel, chunks=chunks, terms=terms, base=base),
        out_shape=(
            jax.ShapeDtypeStruct((count, columns), jnp.float32),
            jax.ShapeDtypeStruct((16, count), jnp.float32),
        ),
        in_specs=[SMEM, SMEM, VMEM, ANY] + [VMEM] * len(parts),
        out_specs=(VMEM, VMEM),
        scratch_shapes=[
            pltpu.VMEM(shape, jnp.float32)
            for c in range(chunks)
            for shape in sizes_of(parts[c * terms + 1 : (c + 1) * terms])
        ],
        compiler_params=params(6 * MIB),
        name="softmax",
    )(where, table, classes, after, *parts)


def combine(mine, other):
    top = jnp.maximum(mine[:8], other[:8])
    total = mine[8:] * jnp.exp(mine[:8] - top) + other[8:] * jnp.exp(other[:8] - top)
    return jnp.concatenate([top, total], axis=0)


def weight_kernel(where, phi, exps, own, mine, other, *outs, base):
    count = exps.shape[0]

    def column(row):
        return jnp.transpose(jnp.broadcast_to(row[:1, :], (128, count)))[:, :1]

    top = jnp.maximum(mine[:8, :], other[:8, :])
    total = mine[8:, :] * jnp.exp(mine[:8, :] - top) + other[8:, :] * jnp.exp(other[:8, :] - top)
    factor = column(jnp.exp(own[:8, :] - top) / total)
    factor = factor * phi[pl.ds(pl.multiple_of(where[base], count), count), :]
    at = 0
    for out in outs:
        tn = out.shape[1]
        out[...] = (exps[:, at : at + tn] * factor).astype(jnp.bfloat16)
        at += tn


def weight_stage(where, base, phi, exps, own, mine, other, widths):
    count = exps.shape[0]
    return pl.pallas_call(
        functools.partial(weight_kernel, base=base),
        out_shape=[jax.ShapeDtypeStruct((count, tn), jnp.bfloat16) for tn in widths],
        in_specs=[SMEM] + [VMEM] * 5,
        out_specs=[VMEM] * len(widths),
        compiler_params=params(22 * MIB),
        name="weights",
    )(where, phi, exps, own, mine, other)


def pack_kernel(where, *refs, base):
    parts, out = refs[:-2], refs[-1]
    count = parts[0].shape[0]
    for d, part in enumerate(parts):
        out[pl.ds(pl.multiple_of(where[base + d], count), count), :] = part[...]


def pack(where, base, parts, after):
    count, tn = parts[0].shape
    after = pltpu.with_memory_space_constraint(after, pltpu.HBM)
    return pl.pallas_call(
        functools.partial(pack_kernel, base=base),
        out_shape=jax.ShapeDtypeStruct((count * len(parts), tn), jnp.bfloat16),
        in_specs=[SMEM] + [VMEM] * len(parts) + [HBM],
        out_specs=VMEM,
        compiler_params=params(8 * MIB),
        name="pack",
    )(where, *parts, after)


def load_kernel(source, after, out, sems):
    n = sems.shape[0]
    rows = out.shape[0] // n
    pieces = [pl.ds(i * rows, rows) for i in range(n)]
    copies = [pltpu.make_async_copy(source.at[p], out.at[p], sems.at[i]) for i, p in enumerate(pieces)]
    for copy in copies:
        copy.start()
    for copy in copies:
        copy.wait()


def load(source, after):
    return pl.pallas_call(
        load_kernel,
        out_shape=pltpu.VMEM(source.shape, source.dtype),
        in_specs=[HBM, ANY],
        out_specs=VMEM,
        scratch_shapes=[pltpu.SemaphoreType.DMA((4,))],
        compiler_params=params(8 * MIB),
        name="load",
    )(pltpu.with_memory_space_constraint(source, pltpu.HBM), after)


def begin_kernel(where, model, after, *refs, side, tm, start):
    *sums, token, buf, sem = refs
    token[...] = jnp.zeros_like(token)
    size = sums[0].shape[0]
    steps = size * len(sums) // tm

    def fetch(i):
        slot = lax.rem(i, 4)
        at = pl.multiple_of((where[side] * PARTS + start) * size + i * tm, tm)
        return pltpu.make_async_copy(model.at[pl.ds(at, tm)], buf.at[slot], sem.at[slot])

    for i in range(min(3, steps)):
        fetch(i).start()

    def body(part, i, carry):
        fetch(i).wait()

        @pl.when(i + 3 < steps)
        def _():
            fetch(i + 3).start()

        rows = pl.ds(pl.multiple_of(i * tm - part * size, tm), tm)
        sums[part][rows, :] = prior_weight * buf[lax.rem(i, 4)].astype(jnp.float32)
        return carry

    n = len(sums)
    for part in range(n):
        lax.fori_loop(part * steps // n, (part + 1) * steps // n, functools.partial(body, part), 0)


def begin(where, model, after, start, stop):
    pixels, columns = model.shape[0] // 2, model.shape[1]
    tm = min(512, pixels // PARTS)
    *total, token = pl.pallas_call(
        functools.partial(begin_kernel, side=1, tm=tm, start=start),
        out_shape=[pltpu.VMEM((pixels // PARTS, columns), jnp.float32)] * (stop - start)
        + [jax.ShapeDtypeStruct((8, 128), jnp.float32)],
        in_specs=[SMEM, HBM, ANY],
        out_specs=[VMEM] * (stop - start + 1),
        scratch_shapes=[pltpu.VMEM((4, tm, columns), jnp.bfloat16), pltpu.SemaphoreType.DMA((4,))],
        compiler_params=params(10 * MIB),
        name="begin",
    )(where, pltpu.with_memory_space_constraint(model, pltpu.HBM), after)
    return total, token


def pass_kernel(where, pown, psib, *refs, blocks, pix, first, last, base, tm, sub):
    mine = 2 * len(blocks)
    count = pown.shape[1] // pix
    pixels = pown.shape[0]
    steps = pixels // tm
    pairs, factors, refs = refs[:mine], refs[mine : mine + 2], refs[mine + 2 :]
    seen, refs = (prior_weight, refs) if first else (refs[0][...], refs[1:])
    totals, refs = refs[:PARTS], refs[PARTS:]
    *refs, wide, tiles, tsem = refs
    for k in range(mine):
        wide[k * count : (k + 1) * count, :] = pairs[k][...]

    def pieces(i):
        slot = lax.rem(i, AHEAD)
        rows = pl.ds(pl.multiple_of(i * tm, tm), tm)
        for k in range(mine):
            columns = pl.ds(pl.multiple_of(where[base + blocks[k // 2]], count), count)
            part = (pown, psib)[k % 2].at[rows, columns]
            yield pltpu.make_async_copy(part, tiles.at[slot, :, pl.ds(k * count, count)], tsem.at[slot, k])

    for i in range(min(AHEAD - 1, steps)):
        for copy in pieces(i):
            copy.start()
    for k, part in enumerate(pairs):
        rows = pl.ds(pl.multiple_of(where[base + blocks[k // 2]], count), count)
        seen = seen + jnp.sum(part[...].astype(jnp.float32) * factors[k % 2][rows, :], axis=0, keepdims=True)
    if last:
        out, buf, sem = refs
        scale = 1.0 / seen
    else:
        *sums, den = refs
        den[...] = seen

    def store(i):
        slot = lax.rem(i, OUT)
        return pltpu.make_async_copy(buf.at[slot], out.at[pl.ds(pl.multiple_of(i * tm, tm), tm)], sem.at[slot])

    def body(part, i, carry):
        for copy in pieces(i):
            copy.wait()

        @pl.when(i + AHEAD - 1 < steps)
        def _():
            for copy in pieces(i + AHEAD - 1):
                copy.start()

        if last:

            @pl.when(i >= OUT)
            def _():
                store(i - OUT).wait()

        for r in range(0, tm, sub):
            rows = pl.ds(pl.multiple_of(i * tm + r - part * (pixels // PARTS), sub), sub)
            dot = jnp.dot(tiles[lax.rem(i, AHEAD), r : r + sub, :], wide[...], preferred_element_type=jnp.float32)
            if last:
                buf[lax.rem(i, OUT), r : r + sub, :] = ((dot + totals[part][rows, :]) * scale).astype(jnp.bfloat16)
            else:
                sums[part][rows, :] += dot
        if last:
            store(i).start()
        return carry

    for part in range(PARTS):
        lax.fori_loop(part * steps // PARTS, (part + 1) * steps // PARTS, functools.partial(body, part), 0)
    if last:
        for i in range(max(0, steps - OUT), steps):
            store(i).wait()


def numer_pass(where, base, pown, psib, blocks, pairs, phis, pix, total, den=None, last=False):
    first = den is None
    pixels, count, columns = pown.shape[0], pairs[0].shape[0], pairs[0].shape[1]
    tm = min(512, pixels // PARTS)
    constrain = pltpu.with_memory_space_constraint
    args = [where, constrain(pown, pltpu.HBM), constrain(psib, pltpu.HBM), *pairs, *phis]
    args += [] if first else [den]
    args += [constrain(part, pltpu.VMEM) for part in total]
    in_specs = [SMEM, HBM, HBM] + [VMEM] * (len(args) - 3)
    scratch = [
        pltpu.VMEM((len(pairs) * count, columns), jnp.bfloat16),
        pltpu.VMEM((AHEAD, tm, len(pairs) * count), jnp.bfloat16),
        pltpu.SemaphoreType.DMA((AHEAD, len(pairs))),
    ]
    if last:
        shape, out_specs, aliases = jax.ShapeDtypeStruct((pixels, columns), jnp.bfloat16), HBM, {}
        scratch = [pltpu.VMEM((OUT, tm, columns), jnp.bfloat16), pltpu.SemaphoreType.DMA((OUT,))] + scratch
    else:
        shape = [pltpu.VMEM(total[0].shape, jnp.float32)] * PARTS + [jax.ShapeDtypeStruct((1, columns), jnp.float32)]
        out_specs = [VMEM] * (PARTS + 1)
        aliases = {len(args) - PARTS + part: part for part in range(PARTS)}
    result = pl.pallas_call(
        functools.partial(
            pass_kernel, blocks=blocks, pix=pix, first=first, last=last, base=base, tm=tm, sub=min(SUB if last else 512, tm)
        ),
        out_shape=shape,
        in_specs=in_specs,
        out_specs=out_specs,
        scratch_shapes=scratch,
        input_output_aliases=aliases,
        compiler_params=params(14 * MIB),
        cost_estimate=cost(2 * pixels * columns * count * len(pairs), 4 * pixels * columns),
        name="numer",
    )(*args)
    return result if last else (result[:-1], result[-1])


def numer_kernel(where, pown, psib, wown, wsib, fown, fsib, model, *refs, column, tm, sub):
    out, mbuf, obuf, msem, osem = refs[-5:]
    pixels, tn = pown.shape[0], wown.shape[1]
    steps = pixels // tm

    def fetch(i):
        slot = lax.rem(i, 3)
        at = pl.multiple_of(where[1] * pixels + i * tm, tm)
        return pltpu.make_async_copy(model.at[pl.ds(at, tm), pl.ds(column, tn)], mbuf.at[slot], msem.at[slot])

    def store(i):
        slot = lax.rem(i, 2)
        at = pl.multiple_of(i * tm, tm)
        return pltpu.make_async_copy(obuf.at[slot], out.at[pl.ds(at, tm), pl.ds(column, tn)], osem.at[slot])

    for i in range(min(2, steps)):
        fetch(i).start()
    den = jnp.sum(wown[...].astype(jnp.float32) * fown[...], axis=0, keepdims=True)
    den = den + jnp.sum(wsib[...].astype(jnp.float32) * fsib[...], axis=0, keepdims=True)
    scale = 1.0 / (prior_weight + den)

    def body(i, carry):
        fetch(i).wait()

        @pl.when(i + 2 < steps)
        def _():
            fetch(i + 2).start()

        @pl.when(i >= 2)
        def _():
            store(i - 2).wait()

        for r in range(0, tm, sub):
            rows = pl.ds(pl.multiple_of(i * tm + r, sub), sub)
            acc = jnp.dot(pown[rows, :], wown[...], preferred_element_type=jnp.float32)
            acc = acc + jnp.dot(psib[rows, :], wsib[...], preferred_element_type=jnp.float32)
            acc = acc + prior_weight * mbuf[lax.rem(i, 3), r : r + sub, :].astype(jnp.float32)
            obuf[lax.rem(i, 2), r : r + sub, :] = (acc * scale).astype(jnp.bfloat16)
        store(i).start()
        return carry

    lax.fori_loop(0, steps, body, 0)
    for i in range(max(0, steps - 2), steps):
        store(i).wait()


def numer_chunk(where, pown, psib, wown, wsib, fown, fsib, model, column, previous):
    depth, tn = wown.shape
    pixels, columns = pown.shape[0], model.shape[1]
    tm = min(1024, pixels)
    pown = pltpu.with_memory_space_constraint(pown, pltpu.VMEM)
    psib = pltpu.with_memory_space_constraint(psib, pltpu.VMEM)
    model = pltpu.with_memory_space_constraint(model, pltpu.HBM)
    args = [where, pown, psib, wown, wsib, fown, fsib, model]
    in_specs = [SMEM] + [VMEM] * 6 + [HBM]
    aliases = {}
    if previous is not None:
        in_specs.append(HBM)
        args.append(pltpu.with_memory_space_constraint(previous, pltpu.HBM))
        aliases = {len(args) - 1: 0}
    return pl.pallas_call(
        functools.partial(numer_kernel, column=column, tm=tm, sub=min(256, tm)),
        out_shape=jax.ShapeDtypeStruct((pixels, columns), jnp.bfloat16),
        in_specs=in_specs,
        out_specs=HBM,
        scratch_shapes=[
            pltpu.VMEM((3, tm, tn), jnp.bfloat16),
            pltpu.VMEM((2, tm, tn), jnp.bfloat16),
            pltpu.SemaphoreType.DMA((3,)),
            pltpu.SemaphoreType.DMA((2,)),
        ],
        input_output_aliases=aliases,
        compiler_params=params(24 * MIB),
        cost_estimate=cost(4 * depth * pixels * tn, 4 * pixels * (depth + tn)),
        name="numer",
    )(*args)


def exchange(value, axis, size, distance):
    return lax.ppermute(value, axis, [(i, i ^ distance) for i in range(size)])


def iteration(patterns, model, scale_table, scale_index, weight_table, weight_class, *, sizes):
    pix, ori = sizes["pix"], sizes["ori"]
    hops = pix.bit_length() - 1
    rows, columns = patterns.shape[0], model.shape[1]
    count = rows // pix
    tn = min(256, columns)
    chunks = columns // tn
    widths = [columns // 2, columns // 4, columns // 4] if chunks >= 4 else [tn] * chunks
    starts = [sum(widths[:c]) for c in range(len(widths))]
    chunks = len(widths)
    beta = (patterns.shape[1] * pix) ** -0.5
    place = lax.axis_index("pix")
    bits = [(place >> i) & 1 for i in range(hops)]

    phi = table_lookup(scale_table, scale_index)[:, None]
    classes = weight_class[None, :]
    side = lax.axis_index("pat")

    share = bit_reverse(place, hops) * count
    entries = [bits[0], side]
    places, offsets, size = {}, [0, 0], rows // 2
    for hop in range(1, hops):
        size //= 2
        places[hop] = len(entries)
        entries += [o + (1 - bits[hop]) * size for o in offsets]
        offsets = [o + bits[hop] * size for o in offsets] + [0]
    places["terms"] = len(entries)
    entries += offsets
    places["share"] = len(entries)
    entries.append(share)
    places["order"] = len(entries)
    entries += [share ^ (bit_reverse(d, hops) * count) for d in range(pix)]
    where = jnp.stack([jnp.asarray(e, jnp.int32) for e in entries])

    later = min(2, chunks - 1)
    turned, terms = {}, {}
    source, after = patterns, phi

    def relay(c, after):
        size = rows // 2
        for hop in range(1, hops):
            size //= 2
            after = forward(where, places[hop], terms[c], size, after)
            terms[c].append(exchange(after, "pix", pix, 1 << hop))
        return after

    for c in range(chunks):
        turns = ((True,) if c == 1 else ()) + ((False,) if c == later else ())
        send, keep, *rest = cross_chunk(
            where, phi, source, model, after, starts[c], widths[c], beta, c == 0, turns
        )
        if c == 0:
            source = rest[-1]
        for own, value in zip(turns, rest):
            turned[own] = value
        terms[c] = [keep, exchange(send, "pix", pix, 1)]
        if c == later:
            psib = exchange(turned[False], "pat", 2, 1)
        if c >= 1 and c < chunks:
            after = relay(c - 1, keep)
    split = pix == 4 and count % 128 == 0
    ready = keep
    if split:
        total, ready = begin(where, model, after, 0, PARTS // 2)
    after = relay(chunks - 1, ready)
    if split:
        more, token = begin(where, model, after, PARTS // 2, PARTS)
        total = total + more
    else:
        token = psib = load(psib, after)
    held = [term for c in range(chunks) for term in terms[c]]
    phi_sib = exchange(phi, "pat", 2, 1)

    exps, own = softmax_stage(where, places["terms"], weight_table, classes, token, held, count, chunks)
    mine = own
    other = None
    for hop in range(ori.bit_length() - 1):
        if other is not None:
            mine = combine(mine, other)
        other = exchange(mine, "ori", ori, 1 << hop)
    shares = [columns] if split or columns < 512 else [columns // 2] * 2
    weights = weight_stage(where, places["share"], phi, exps, own, mine, other, shares)

    if split:
        base = places["order"]
        own = [weights[0], exchange(weights[0], "pix", pix, 1), exchange(weights[0], "pix", pix, 2)]
        own.append(exchange(own[2], "pix", pix, 1))
        pairs = [(w, exchange(w, "pat", 2, 1)) for w in own]
        fixed = (where, base, turned[True], psib)
        phis = (phi, phi_sib)
        total, den = numer_pass(*fixed, (0,), pairs[0], phis, pix, total)
        total, den = numer_pass(*fixed, (1,), pairs[1], phis, pix, total, den)
        return numer_pass(*fixed, (2, 3), pairs[2] + pairs[3], phis, pix, total, den, last=True)

    gathered = [[w] + [exchange(w, "pix", pix, d) for d in range(1, pix)] for w in weights]
    at, result, after = 0, None, model
    for width, parts in zip(shares, gathered):
        wown = pack(where, places["order"], parts, after)
        wsib = exchange(wown, "pat", 2, 1)
        result = numer_chunk(where, turned[True], psib, wown, wsib, phi, phi_sib, model, at, result)
        after = result
        at += width
    return result


def solution(mesh):
    placed = (
        P(("grp", "pat"), "pix"),
        P(("grp", "pix"), "ori"),
        P("grp"),
        P(("grp", "pat")),
        P("grp"),
        P(("grp", "ori")),
    )
    return jax.shard_map(
        functools.partial(iteration, sizes=dict(mesh.shape)),
        mesh=mesh,
        in_specs=placed,
        out_specs=P(("grp", "pix", "pat"), "ori"),
        check_vma=False,
    )
```

```python
import functools

import jax
import jax.numpy as jnp
from jax import lax
from jax.experimental import pallas as pl
from jax.experimental.pallas import tpu as pltpu
from jax.sharding import PartitionSpec as P

prior_weight = 0.5
MIB = 1 << 20
SLOTS = 4
PARTS = 4
SUB = 256
OUT = 4
TURN = 3
VMEM = pl.BlockSpec(memory_space=pltpu.VMEM)
SMEM = pl.BlockSpec(memory_space=pltpu.SMEM)
HBM = pl.BlockSpec(memory_space=pltpu.HBM)
ANY = pl.BlockSpec(memory_space=pl.ANY)


def table_lookup(table, index):
    levels = jnp.arange(table.shape[0], dtype=jnp.int32)
    return jnp.sum(jnp.where(index[:, None] == levels[None, :], table[None, :], 0.0), axis=1)


def params(limit):
    return pltpu.CompilerParams(vmem_limit_bytes=limit)


def cost(flops, moved):
    return pl.CostEstimate(flops=flops, bytes_accessed=moved, transcendentals=0)


def bit_reverse(value, bits):
    return sum(((value >> i) & 1) << (bits - 1 - i) for i in range(bits))


EXPONENTS = range(-12, 21)


def encoded(rows, tn):
    return jax.ShapeDtypeStruct((rows * 3 // 4 + 8, tn), jnp.int32)


def power_of_two(exponent, sign):
    total = jnp.zeros(exponent.shape, jnp.float32)
    for e in EXPONENTS:
        total = total + jnp.where(exponent == e, 2.0 ** (sign * (e - 22)), 0.0)
    return total


def encode(values, out):
    rows, tn = values.shape
    n = rows // 4
    top = jnp.max(jnp.max(jnp.abs(values), axis=0, keepdims=True), axis=1, keepdims=True)
    top = jnp.broadcast_to(top, (8, 128))
    exponent = jnp.full(top.shape, EXPONENTS[0], jnp.int32)
    for e in EXPONENTS[:-1]:
        exponent = exponent + jnp.where(top > 2.0**e, 1, 0)
    factor = power_of_two(exponent, -1)[:1, :1]
    code = (values * factor + 12582912.0).astype(jnp.int32) - 8388608
    last = code[3 * n :, :]
    for k in range(3):
        part = jnp.bitwise_and(lax.shift_right_logical(last, 8 * k), 255)
        out[k * n : (k + 1) * n, :] = jnp.bitwise_or(code[k * n : (k + 1) * n, :], lax.shift_left(part, 24))
    out[3 * n :, :] = jnp.broadcast_to(exponent[:, :1], (8, tn))


def decode(words, out):
    rows = out.shape[0]
    n = rows // 4
    factor = power_of_two(words[3 * n :, :128], 1)[:1, :1]
    last = None
    for k in range(3):
        word = words[k * n : (k + 1) * n, :]
        code = jnp.bitwise_and(word, 16777215)
        out[k * n : (k + 1) * n, :] = (code.astype(jnp.float32) - 4194304.0) * factor
        high = lax.shift_left(lax.shift_right_logical(word, 24), 8 * k)
        last = high if last is None else jnp.bitwise_or(last, high)
    out[3 * n :, :] = (last.astype(jnp.float32) - 4194304.0) * factor


def cross_kernel(where, phi, patterns, model, after, send, keep, *refs, column, tk, steps, beta, first, turns):
    turned, refs = refs[: len(turns)], refs[len(turns) :]
    if turns:
        *refs, tbuf, tsem = refs
    if first:
        held, mbuf, acc, squares, msem, psem = refs
    else:
        held, (mbuf, acc, squares, msem) = patterns, refs
    tn = acc.shape[1]

    def copies(i):
        slot = lax.rem(i, SLOTS)
        at = pl.multiple_of(i * tk, tk)
        both = [pltpu.make_async_copy(model.at[pl.ds(at, tk), pl.ds(column, tn)], mbuf.at[slot], msem.at[slot])]
        if first:
            both.append(pltpu.make_async_copy(patterns.at[:, pl.ds(at, tk)], held.at[:, pl.ds(at, tk)], psem.at[slot]))
        return both

    def stores(i):
        slot = lax.rem(i, TURN)
        for t, out in enumerate(turned):
            width = out.shape[0] // steps
            rows = pl.ds(pl.multiple_of(i * width, width), width)
            yield pltpu.make_async_copy(tbuf.at[t, slot], out.at[rows], tsem.at[t, slot])

    for i in range(min(SLOTS - 1, steps)):
        for copy in copies(i):
            copy.start()
    acc[...] = jnp.zeros_like(acc)
    squares[...] = jnp.zeros_like(squares)

    def body(i, carry):
        for copy in copies(i):
            copy.wait()

        @pl.when(i + SLOTS - 1 < steps)
        def _():
            for copy in copies(i + SLOTS - 1):
                copy.start()

        if turns:

            @pl.when(i >= TURN)
            def _():
                for copy in stores(i - TURN):
                    copy.wait()

        tile = mbuf[lax.rem(i, SLOTS)]
        part = held[:, pl.ds(pl.multiple_of(i * tk, tk), tk)]
        acc[...] += jnp.dot(part, tile, preferred_element_type=jnp.float32)
        wide = tile.astype(jnp.float32)
        squares[...] += jnp.sum((wide * wide).reshape(tk // 8, 8, tn), axis=0)
        for t, (own, out) in enumerate(zip(turns, turned)):
            pixels = out.shape[0]
            width = pixels // steps
            side = where[1] if own else 1 - where[1]
            piece = held[:, pl.ds(pl.multiple_of(side * pixels + i * width, width), width)]
            tbuf[t, lax.rem(i, TURN)] = piece.T
        for copy in stores(i):
            copy.start()
        return carry

    lax.fori_loop(0, steps, body, 0)
    sq = jnp.sum(squares[...], axis=0, keepdims=True)
    scale = phi[...]
    acc[...] = beta * (scale * acc[...] - 0.5 * (scale * scale) * sq)
    half = keep.shape[0]
    encode(acc[pl.ds(pl.multiple_of((1 - where[0]) * half, half), half), :], send)
    keep[...] = acc[pl.ds(pl.multiple_of(where[0] * half, half), half), :]
    for i in range(max(0, steps - TURN), steps):
        for copy in stores(i):
            copy.wait()


def cross_chunk(where, phi, patterns, model, after, column, tn, beta, first, turns):
    rows, depth = patterns.shape
    tk = min(2048, depth)
    half = rows // 2
    shapes = [encoded(half, tn), jax.ShapeDtypeStruct((half, tn), jnp.float32)]
    shapes += [pltpu.HBM((depth // 2, rows), patterns.dtype)] * len(turns)
    places = [VMEM, VMEM] + [HBM] * len(turns)
    scratch = [
        pltpu.VMEM((SLOTS, tk, tn), jnp.bfloat16),
        pltpu.VMEM((rows, tn), jnp.float32),
        pltpu.VMEM((8, tn), jnp.float32),
        pltpu.SemaphoreType.DMA((SLOTS,)),
    ]
    if first:
        shapes.append(pltpu.VMEM(patterns.shape, patterns.dtype))
        scratch.append(pltpu.SemaphoreType.DMA((SLOTS,)))
        places.append(VMEM)
    if turns:
        scratch.append(pltpu.VMEM((len(turns), TURN, tk // 2, rows), patterns.dtype))
        scratch.append(pltpu.SemaphoreType.DMA((len(turns), TURN)))
    patterns = pltpu.with_memory_space_constraint(patterns, pltpu.HBM if first else pltpu.VMEM)
    model = pltpu.with_memory_space_constraint(model, pltpu.HBM)
    return pl.pallas_call(
        functools.partial(
            cross_kernel, column=column, tk=tk, steps=depth // tk, beta=beta, first=first, turns=turns
        ),
        out_shape=shapes,
        in_specs=[SMEM, VMEM, HBM if first else VMEM, HBM, ANY],
        out_specs=places,
        scratch_shapes=scratch,
        compiler_params=params(20 * MIB),
        cost_estimate=cost(2 * rows * depth * tn, 2 * depth * (rows + tn)),
        name="cross",
    )(where, phi, patterns, model, after)


def forward_kernel(where, after, *refs, base, terms):
    parts, out, decoded = refs[:terms], refs[terms], refs[terms + 1 :]
    size = (out.shape[0] - 8) * 4 // 3
    total = None
    for t, part in enumerate(parts):
        if t > 0:
            decode(part, decoded[t - 1])
            part = decoded[t - 1]
        piece = part[pl.ds(pl.multiple_of(where[base + t], size), size), :]
        total = piece if total is None else total + piece
    encode(total, out)


def sizes_of(parts):
    return [((p.shape[0] - 8) * 4 // 3, p.shape[1]) for p in parts]


def forward(where, base, parts, size, after):
    return pl.pallas_call(
        functools.partial(forward_kernel, base=base, terms=len(parts)),
        out_shape=encoded(size, parts[0].shape[1]),
        in_specs=[SMEM, ANY] + [VMEM] * len(parts),
        out_specs=VMEM,
        scratch_shapes=[pltpu.VMEM(shape, jnp.float32) for shape in sizes_of(parts[1:])],
        compiler_params=params(6 * MIB),
        name="forward",
    )(where, after, *parts)


def softmax_kernel(where, table, classes, after, *refs, chunks, terms, base):
    parts, refs = refs[: chunks * terms], refs[chunks * terms :]
    exps, stats, decoded = refs[0], refs[1], refs[2:]
    count = exps.shape[0]
    logw = jnp.zeros(classes.shape, jnp.float32)
    for q in range(table.shape[0]):
        logw = logw + jnp.where(classes[...] == q, table[q], 0.0)
    at = 0
    for c in range(chunks):
        tn = parts[c * terms].shape[1]
        total = None
        for t in range(terms):
            rows = pl.ds(pl.multiple_of(where[base + t], count), count)
            part = parts[c * terms + t]
            if t > 0:
                room = decoded[c * (terms - 1) + t - 1]
                decode(part, room)
                part = room
            part = part[rows, :]
            total = part if total is None else total + part
        exps[:, at : at + tn] = total + logw[:, at : at + tn]
        at += tn
    top = jnp.max(exps[...], axis=1, keepdims=True)
    exps[...] = jnp.exp(exps[...] - top)
    total = jnp.sum(exps[...], axis=1, keepdims=True)
    lanes = (count, 128)
    stats[:8, :] = jnp.transpose(jnp.broadcast_to(top, lanes))[:8, :]
    stats[8:, :] = jnp.transpose(jnp.broadcast_to(total, lanes))[:8, :]


def softmax_stage(where, base, table, classes, after, parts, count, chunks):
    terms = len(parts) // chunks
    columns = classes.shape[1]
    return pl.pallas_call(
        functools.partial(softmax_kernel, chunks=chunks, terms=terms, base=base),
        out_shape=(
            jax.ShapeDtypeStruct((count, columns), jnp.float32),
            jax.ShapeDtypeStruct((16, count), jnp.float32),
        ),
        in_specs=[SMEM, SMEM, VMEM, ANY] + [VMEM] * len(parts),
        out_specs=(VMEM, VMEM),
        scratch_shapes=[
            pltpu.VMEM(shape, jnp.float32)
            for c in range(chunks)
            for shape in sizes_of(parts[c * terms + 1 : (c + 1) * terms])
        ],
        compiler_params=params(6 * MIB),
        name="softmax",
    )(where, table, classes, after, *parts)


def combine(mine, other):
    top = jnp.maximum(mine[:8], other[:8])
    total = mine[8:] * jnp.exp(mine[:8] - top) + other[8:] * jnp.exp(other[:8] - top)
    return jnp.concatenate([top, total], axis=0)


def weight_kernel(where, phi, exps, own, mine, other, *outs, base):
    count = exps.shape[0]

    def column(row):
        return jnp.transpose(jnp.broadcast_to(row[:1, :], (128, count)))[:, :1]

    top = jnp.maximum(mine[:8, :], other[:8, :])
    total = mine[8:, :] * jnp.exp(mine[:8, :] - top) + other[8:, :] * jnp.exp(other[:8, :] - top)
    factor = column(jnp.exp(own[:8, :] - top) / total)
    factor = factor * phi[pl.ds(pl.multiple_of(where[base], count), count), :]
    at = 0
    for out in outs:
        tn = out.shape[1]
        out[...] = (exps[:, at : at + tn] * factor).astype(jnp.bfloat16)
        at += tn


def weight_stage(where, base, phi, exps, own, mine, other, widths):
    count = exps.shape[0]
    return pl.pallas_call(
        functools.partial(weight_kernel, base=base),
        out_shape=[jax.ShapeDtypeStruct((count, tn), jnp.bfloat16) for tn in widths],
        in_specs=[SMEM] + [VMEM] * 5,
        out_specs=[VMEM] * len(widths),
        compiler_params=params(22 * MIB),
        name="weights",
    )(where, phi, exps, own, mine, other)


def pack_kernel(where, *refs, base):
    parts, out = refs[:-2], refs[-1]
    count = parts[0].shape[0]
    for d, part in enumerate(parts):
        out[pl.ds(pl.multiple_of(where[base + d], count), count), :] = part[...]


def pack(where, base, parts, after):
    count, tn = parts[0].shape
    after = pltpu.with_memory_space_constraint(after, pltpu.HBM)
    return pl.pallas_call(
        functools.partial(pack_kernel, base=base),
        out_shape=jax.ShapeDtypeStruct((count * len(parts), tn), jnp.bfloat16),
        in_specs=[SMEM] + [VMEM] * len(parts) + [HBM],
        out_specs=VMEM,
        compiler_params=params(8 * MIB),
        name="pack",
    )(where, *parts, after)


def load_kernel(source, after, out, sems):
    n = sems.shape[0]
    rows = out.shape[0] // n
    pieces = [pl.ds(i * rows, rows) for i in range(n)]
    copies = [pltpu.make_async_copy(source.at[p], out.at[p], sems.at[i]) for i, p in enumerate(pieces)]
    for copy in copies:
        copy.start()
    for copy in copies:
        copy.wait()


def load(source, after):
    return pl.pallas_call(
        load_kernel,
        out_shape=pltpu.VMEM(source.shape, source.dtype),
        in_specs=[HBM, ANY],
        out_specs=VMEM,
        scratch_shapes=[pltpu.SemaphoreType.DMA((4,))],
        compiler_params=params(8 * MIB),
        name="load",
    )(pltpu.with_memory_space_constraint(source, pltpu.HBM), after)


def begin_kernel(where, model, after, *refs, side, tm, start):
    *sums, token, buf, sem = refs
    token[...] = jnp.zeros_like(token)
    size = sums[0].shape[0]
    steps = size * len(sums) // tm

    def fetch(i):
        slot = lax.rem(i, 4)
        at = pl.multiple_of((where[side] * PARTS + start) * size + i * tm, tm)
        return pltpu.make_async_copy(model.at[pl.ds(at, tm)], buf.at[slot], sem.at[slot])

    for i in range(min(3, steps)):
        fetch(i).start()

    def body(part, i, carry):
        fetch(i).wait()

        @pl.when(i + 3 < steps)
        def _():
            fetch(i + 3).start()

        rows = pl.ds(pl.multiple_of(i * tm - part * size, tm), tm)
        sums[part][rows, :] = prior_weight * buf[lax.rem(i, 4)].astype(jnp.float32)
        return carry

    n = len(sums)
    for part in range(n):
        lax.fori_loop(part * steps // n, (part + 1) * steps // n, functools.partial(body, part), 0)


def begin(where, model, after, start, stop):
    pixels, columns = model.shape[0] // 2, model.shape[1]
    tm = min(512, pixels // PARTS)
    *total, token = pl.pallas_call(
        functools.partial(begin_kernel, side=1, tm=tm, start=start),
        out_shape=[pltpu.VMEM((pixels // PARTS, columns), jnp.float32)] * (stop - start)
        + [jax.ShapeDtypeStruct((8, 128), jnp.float32)],
        in_specs=[SMEM, HBM, ANY],
        out_specs=[VMEM] * (stop - start + 1),
        scratch_shapes=[pltpu.VMEM((4, tm, columns), jnp.bfloat16), pltpu.SemaphoreType.DMA((4,))],
        compiler_params=params(10 * MIB),
        name="begin",
    )(where, pltpu.with_memory_space_constraint(model, pltpu.HBM), after)
    return total, token


def pass_kernel(where, pown, psib, *refs, blocks, pix, first, last, base, tm, sub, ahead):
    mine = 2 * len(blocks)
    count = pown.shape[1] // pix
    pixels = pown.shape[0]
    steps = pixels // tm
    pairs, factors, refs = refs[:mine], refs[mine : mine + 2], refs[mine + 2 :]
    seen, refs = (prior_weight, refs) if first else (refs[0][...], refs[1:])
    totals, refs = refs[:PARTS], refs[PARTS:]
    *refs, wide, tiles, tsem = refs
    for k in range(mine):
        wide[k * count : (k + 1) * count, :] = pairs[k][...]

    def pieces(i):
        slot = lax.rem(i, ahead)
        rows = pl.ds(pl.multiple_of(i * tm, tm), tm)
        for k in range(mine):
            columns = pl.ds(pl.multiple_of(where[base + blocks[k // 2]], count), count)
            part = (pown, psib)[k % 2].at[rows, columns]
            yield pltpu.make_async_copy(part, tiles.at[slot, :, pl.ds(k * count, count)], tsem.at[slot, k])

    for i in range(min(ahead - 1, steps)):
        for copy in pieces(i):
            copy.start()
    for k, part in enumerate(pairs):
        rows = pl.ds(pl.multiple_of(where[base + blocks[k // 2]], count), count)
        seen = seen + jnp.sum(part[...].astype(jnp.float32) * factors[k % 2][rows, :], axis=0, keepdims=True)
    if last:
        out, buf, sem = refs
        scale = 1.0 / seen
    else:
        *sums, den = refs
        den[...] = seen

    def store(i):
        slot = lax.rem(i, OUT)
        return pltpu.make_async_copy(buf.at[slot], out.at[pl.ds(pl.multiple_of(i * tm, tm), tm)], sem.at[slot])

    def body(part, i, carry):
        for copy in pieces(i):
            copy.wait()

        @pl.when(i + ahead - 1 < steps)
        def _():
            for copy in pieces(i + ahead - 1):
                copy.start()

        if last:

            @pl.when(i >= OUT)
            def _():
                store(i - OUT).wait()

        for r in range(0, tm, sub):
            rows = pl.ds(pl.multiple_of(i * tm + r - part * (pixels // PARTS), sub), sub)
            dot = jnp.dot(tiles[lax.rem(i, ahead), r : r + sub, :], wide[...], preferred_element_type=jnp.float32)
            if last:
                buf[lax.rem(i, OUT), r : r + sub, :] = ((dot + totals[part][rows, :]) * scale).astype(jnp.bfloat16)
            else:
                sums[part][rows, :] += dot
        if last:
            store(i).start()
        return carry

    for part in range(PARTS):
        lax.fori_loop(part * steps // PARTS, (part + 1) * steps // PARTS, functools.partial(body, part), 0)
    if last:
        for i in range(max(0, steps - OUT), steps):
            store(i).wait()


def numer_pass(where, base, pown, psib, blocks, pairs, phis, pix, total, den=None, last=False):
    first = den is None
    pixels, count, columns = pown.shape[0], pairs[0].shape[0], pairs[0].shape[1]
    tm = min(512 if last else 1024, pixels // PARTS)
    ahead = 6 if last else 4
    constrain = pltpu.with_memory_space_constraint
    args = [where, constrain(pown, pltpu.HBM), constrain(psib, pltpu.HBM), *pairs, *phis]
    args += [] if first else [den]
    args += [constrain(part, pltpu.VMEM) for part in total]
    in_specs = [SMEM, HBM, HBM] + [VMEM] * (len(args) - 3)
    scratch = [
        pltpu.VMEM((len(pairs) * count, columns), jnp.bfloat16),
        pltpu.VMEM((ahead, tm, len(pairs) * count), jnp.bfloat16),
        pltpu.SemaphoreType.DMA((ahead, len(pairs))),
    ]
    if last:
        shape, out_specs, aliases = jax.ShapeDtypeStruct((pixels, columns), jnp.bfloat16), HBM, {}
        scratch = [pltpu.VMEM((OUT, tm, columns), jnp.bfloat16), pltpu.SemaphoreType.DMA((OUT,))] + scratch
    else:
        shape = [pltpu.VMEM(total[0].shape, jnp.float32)] * PARTS + [jax.ShapeDtypeStruct((1, columns), jnp.float32)]
        out_specs = [VMEM] * (PARTS + 1)
        aliases = {len(args) - PARTS + part: part for part in range(PARTS)}
    result = pl.pallas_call(
        functools.partial(
            pass_kernel, blocks=blocks, pix=pix, first=first, last=last, base=base, tm=tm,
            sub=min(SUB if last else 512, tm), ahead=ahead,
        ),
        out_shape=shape,
        in_specs=in_specs,
        out_specs=out_specs,
        scratch_shapes=scratch,
        input_output_aliases=aliases,
        compiler_params=params(14 * MIB),
        cost_estimate=cost(2 * pixels * columns * count * len(pairs), 4 * pixels * columns),
        name="numer",
    )(*args)
    return result if last else (result[:-1], result[-1])


def numer_kernel(where, pown, psib, wown, wsib, fown, fsib, model, *refs, column, tm, sub):
    out, mbuf, obuf, msem, osem = refs[-5:]
    pixels, tn = pown.shape[0], wown.shape[1]
    steps = pixels // tm

    def fetch(i):
        slot = lax.rem(i, 3)
        at = pl.multiple_of(where[1] * pixels + i * tm, tm)
        return pltpu.make_async_copy(model.at[pl.ds(at, tm), pl.ds(column, tn)], mbuf.at[slot], msem.at[slot])

    def store(i):
        slot = lax.rem(i, 2)
        at = pl.multiple_of(i * tm, tm)
        return pltpu.make_async_copy(obuf.at[slot], out.at[pl.ds(at, tm), pl.ds(column, tn)], osem.at[slot])

    for i in range(min(2, steps)):
        fetch(i).start()
    den = jnp.sum(wown[...].astype(jnp.float32) * fown[...], axis=0, keepdims=True)
    den = den + jnp.sum(wsib[...].astype(jnp.float32) * fsib[...], axis=0, keepdims=True)
    scale = 1.0 / (prior_weight + den)

    def body(i, carry):
        fetch(i).wait()

        @pl.when(i + 2 < steps)
        def _():
            fetch(i + 2).start()

        @pl.when(i >= 2)
        def _():
            store(i - 2).wait()

        for r in range(0, tm, sub):
            rows = pl.ds(pl.multiple_of(i * tm + r, sub), sub)
            acc = jnp.dot(pown[rows, :], wown[...], preferred_element_type=jnp.float32)
            acc = acc + jnp.dot(psib[rows, :], wsib[...], preferred_element_type=jnp.float32)
            acc = acc + prior_weight * mbuf[lax.rem(i, 3), r : r + sub, :].astype(jnp.float32)
            obuf[lax.rem(i, 2), r : r + sub, :] = (acc * scale).astype(jnp.bfloat16)
        store(i).start()
        return carry

    lax.fori_loop(0, steps, body, 0)
    for i in range(max(0, steps - 2), steps):
        store(i).wait()


def numer_chunk(where, pown, psib, wown, wsib, fown, fsib, model, column, previous):
    depth, tn = wown.shape
    pixels, columns = pown.shape[0], model.shape[1]
    tm = min(1024, pixels)
    pown = pltpu.with_memory_space_constraint(pown, pltpu.VMEM)
    psib = pltpu.with_memory_space_constraint(psib, pltpu.VMEM)
    model = pltpu.with_memory_space_constraint(model, pltpu.HBM)
    args = [where, pown, psib, wown, wsib, fown, fsib, model]
    in_specs = [SMEM] + [VMEM] * 6 + [HBM]
    aliases = {}
    if previous is not None:
        in_specs.append(HBM)
        args.append(pltpu.with_memory_space_constraint(previous, pltpu.HBM))
        aliases = {len(args) - 1: 0}
    return pl.pallas_call(
        functools.partial(numer_kernel, column=column, tm=tm, sub=min(256, tm)),
        out_shape=jax.ShapeDtypeStruct((pixels, columns), jnp.bfloat16),
        in_specs=in_specs,
        out_specs=HBM,
        scratch_shapes=[
            pltpu.VMEM((3, tm, tn), jnp.bfloat16),
            pltpu.VMEM((2, tm, tn), jnp.bfloat16),
            pltpu.SemaphoreType.DMA((3,)),
            pltpu.SemaphoreType.DMA((2,)),
        ],
        input_output_aliases=aliases,
        compiler_params=params(24 * MIB),
        cost_estimate=cost(4 * depth * pixels * tn, 4 * pixels * (depth + tn)),
        name="numer",
    )(*args)


def exchange(value, axis, size, distance):
    return lax.ppermute(value, axis, [(i, i ^ distance) for i in range(size)])


def iteration(patterns, model, scale_table, scale_index, weight_table, weight_class, *, sizes):
    pix, ori = sizes["pix"], sizes["ori"]
    hops = pix.bit_length() - 1
    rows, columns = patterns.shape[0], model.shape[1]
    count = rows // pix
    tn = min(256, columns)
    chunks = columns // tn
    widths = [columns // 2, columns // 4, columns // 4] if chunks >= 4 else [tn] * chunks
    starts = [sum(widths[:c]) for c in range(len(widths))]
    chunks = len(widths)
    beta = (patterns.shape[1] * pix) ** -0.5
    place = lax.axis_index("pix")
    bits = [(place >> i) & 1 for i in range(hops)]

    phi = table_lookup(scale_table, scale_index)[:, None]
    classes = weight_class[None, :]
    side = lax.axis_index("pat")

    share = bit_reverse(place, hops) * count
    entries = [bits[0], side]
    places, offsets, size = {}, [0, 0], rows // 2
    for hop in range(1, hops):
        size //= 2
        places[hop] = len(entries)
        entries += [o + (1 - bits[hop]) * size for o in offsets]
        offsets = [o + bits[hop] * size for o in offsets] + [0]
    places["terms"] = len(entries)
    entries += offsets
    places["share"] = len(entries)
    entries.append(share)
    places["order"] = len(entries)
    entries += [share ^ (bit_reverse(d, hops) * count) for d in range(pix)]
    where = jnp.stack([jnp.asarray(e, jnp.int32) for e in entries])

    later = min(2, chunks - 1)
    turned, terms = {}, {}
    source, after = patterns, phi

    def relay(c, after):
        size = rows // 2
        for hop in range(1, hops):
            size //= 2
            after = forward(where, places[hop], terms[c], size, after)
            terms[c].append(exchange(after, "pix", pix, 1 << hop))
        return after

    for c in range(chunks):
        turns = ((True,) if c == 1 else ()) + ((False,) if c == later else ())
        send, keep, *rest = cross_chunk(
            where, phi, source, model, after, starts[c], widths[c], beta, c == 0, turns
        )
        if c == 0:
            source = rest[-1]
        for own, value in zip(turns, rest):
            turned[own] = value
        terms[c] = [keep, exchange(send, "pix", pix, 1)]
        if c == later:
            psib = exchange(turned[False], "pat", 2, 1)
        if c >= 1 and c < chunks:
            after = relay(c - 1, keep)
    split = pix == 4 and count % 128 == 0
    ready = keep
    if split:
        total, ready = begin(where, model, after, 0, PARTS // 2)
    after = relay(chunks - 1, ready)
    if split:
        more, token = begin(where, model, after, PARTS // 2, PARTS)
        total = total + more
    else:
        token = psib = load(psib, after)
    held = [term for c in range(chunks) for term in terms[c]]
    phi_sib = exchange(phi, "pat", 2, 1)

    exps, own = softmax_stage(where, places["terms"], weight_table, classes, token, held, count, chunks)
    mine = own
    other = None
    for hop in range(ori.bit_length() - 1):
        if other is not None:
            mine = combine(mine, other)
        other = exchange(mine, "ori", ori, 1 << hop)
    shares = [columns] if split or columns < 512 else [columns // 2] * 2
    weights = weight_stage(where, places["share"], phi, exps, own, mine, other, shares)

    if split:
        base = places["order"]
        own = [weights[0], exchange(weights[0], "pix", pix, 1), exchange(weights[0], "pix", pix, 2)]
        own.append(exchange(own[2], "pix", pix, 1))
        pairs = [(w, exchange(w, "pat", 2, 1)) for w in own]
        fixed = (where, base, turned[True], psib)
        phis = (phi, phi_sib)
        total, den = numer_pass(*fixed, (0,), pairs[0], phis, pix, total)
        total, den = numer_pass(*fixed, (1,), pairs[1], phis, pix, total, den)
        return numer_pass(*fixed, (2, 3), pairs[2] + pairs[3], phis, pix, total, den, last=True)

    gathered = [[w] + [exchange(w, "pix", pix, d) for d in range(1, pix)] for w in weights]
    at, result, after = 0, None, model
    for width, parts in zip(shares, gathered):
        wown = pack(where, places["order"], parts, after)
        wsib = exchange(wown, "pat", 2, 1)
        result = numer_chunk(where, turned[True], psib, wown, wsib, phi, phi_sib, model, at, result)
        after = result
        at += width
    return result


def solution(mesh):
    placed = (
        P(("grp", "pat"), "pix"),
        P(("grp", "pix"), "ori"),
        P("grp"),
        P(("grp", "pat")),
        P("grp"),
        P(("grp", "ori")),
    )
    return jax.shard_map(
        functools.partial(iteration, sizes=dict(mesh.shape)),
        mesh=mesh,
        in_specs=placed,
        out_specs=P(("grp", "pix", "pat"), "ori"),
        check_vma=False,
    )
```
